32 devices in a mesh: fsdp: 4 (over y, x), ctx: 8 (over z, core).
Axes of the slice: x: 2, y: 2, z: 4, core: 2. Of those that a mesh axis runs over, the one named last changes fastest.
Arguments:
- inputs: bfloat16 [2, 8, 512, 768], P(None, 'fsdp', 'ctx'), may hold values from -6 to 6
- segments: int32 [2, 8, 512], P(None, 'fsdp', 'ctx'), may hold values from -1 to 2, as said below
- ln1_scale: bfloat16 [768], P('fsdp'), may hold values from 0.099609375 to 1.8984375
- ln1_bias: bfloat16 [768], P('fsdp'), may hold values from -1.75 to 1.75
- w_qkv: bfloat16 [768, 2304], P('fsdp'), may hold values from -0.21875 to 0.21875
- b_query: bfloat16 [768], P('fsdp'), may hold values from -1.75 to 1.75
- b_value: bfloat16 [768], P('fsdp'), may hold values from -1.75 to 1.75
- w_proj: bfloat16 [768, 768], P('fsdp'), may hold values from -2.5 to 2.5
- b_proj: bfloat16 [768], P('fsdp'), may hold values from -1.75 to 1.75
- ln2_scale: bfloat16 [768], P('fsdp'), may hold values from 0.099609375 to 1.8984375
- ln2_bias: bfloat16 [768], P('fsdp'), may hold values from -1.75 to 1.75
- w_up: bfloat16 [768, 3072], P('fsdp'), may hold values from -0.21875 to 0.21875
- b_up: bfloat16 [3072], P('fsdp'), may hold values from -1.75 to 1.75
- w_down: bfloat16 [3072, 768], P('fsdp'), may hold values from -0.109375 to 0.109375
- b_down: bfloat16 [768], P('fsdp'), may hold values from -1.75 to 1.75
- cotangent: bfloat16 [2, 8, 512, 768], P(None, 'fsdp', 'ctx'), may hold values from -6 to 6
Outputs:
- out: bfloat16 [2, 8, 512, 768], P(None, 'fsdp', 'ctx')
- d_input: bfloat16 [2, 8, 512, 768], P(None, 'fsdp', 'ctx')
- grad_ln1_scale: float32 [768], P('fsdp')
- grad_ln1_bias: float32 [768], P('fsdp')
- grad_w_qkv: float32 [768, 2304], P('fsdp')
- grad_b_query: float32 [768], P('fsdp')
- grad_b_value: float32 [768], P('fsdp')
- grad_w_proj: float32 [768, 768], P('fsdp')
- grad_b_proj: float32 [768], P('fsdp')
- grad_ln2_scale: float32 [768], P('fsdp')
- grad_ln2_bias: float32 [768], P('fsdp')
- grad_w_up: float32 [768, 3072], P('fsdp')
- grad_b_up: float32 [3072], P('fsdp')
- grad_w_down: float32 [3072, 768], P('fsdp')
- grad_b_down: float32 [768], P('fsdp')
The draws below stay inside these ranges and needn't reach their ends.
Inputs may be any that keep to these rules, and one draw needn't show every extreme that they name: `segments`: along a sequence document numbers never fall until the padding (-1) that ends it. In every group of 2 consecutive sequences of a micro-batch, one sequence, drawn from the seed, is a single document numbered 0 with no padding; every other sequence ends in padding.
All inputs are finite; a program needn't handle non-finite values.
Results may differ from the reference program's by a relative error of at most 0.019.
Values may be sent and summed in bfloat16 or wider, within the bound.
A program may use at most 320 MiB of HBM per device.

```python
import math
import jax
import jax.numpy as jnp
from jax import lax

D = 768
HEADS = 12
HEAD_DIM = 64
FF = 3072
SEQ_DEV = 2
MICRO = 2
SEQS = 8
LENGTH = 512


def draw_segments(key, part):
    doc_breaks = max(2, LENGTH // 512)
    pad_most = LENGTH // 8
    key_bounds, key_pad, key_pick = jax.random.split(jax.random.fold_in(key, 17), 3)
    bounds = jax.random.randint(key_bounds, (MICRO, SEQS, doc_breaks), 1, LENGTH - pad_most)
    padding = jax.random.randint(key_pad, (MICRO, SEQS, 1), 1, pad_most + 1)
    places = jnp.arange(LENGTH, dtype=jnp.int32)
    numbers = jnp.sum((places[None, None, :, None] >= bounds[:, :, None, :]).astype(jnp.int32), -1)
    numbers = jnp.where(places[None, None, :] >= LENGTH - padding, -1, numbers)
    picked = jax.random.randint(key_pick, (MICRO, SEQS // SEQ_DEV), 0, SEQ_DEV)
    picked = jnp.repeat(picked, SEQ_DEV, axis=1)
    single_doc = (jnp.arange(SEQS, dtype=jnp.int32) % SEQ_DEV)[None, :] == picked
    return jnp.where(single_doc[:, :, None], 0, numbers).astype(jnp.int32)


def shard_levels(stream_key, dims, cuts, smallest, top_value):
    loudness = 1.0
    for dim, blocks in cuts:
        steps = jax.random.uniform(jax.random.fold_in(jax.random.fold_in(stream_key, 6), dim), (blocks,), jnp.float32, smallest / len(cuts), top_value / len(cuts))
        loudness = loudness * jnp.repeat(jnp.exp(steps), dims[dim] // blocks).reshape((-1,) + (1,) * (len(dims) - 1 - dim))
    return loudness


def noise(stream_key, shape, scale, bound, shards=(), kind=jnp.bfloat16):
    entries = scale * jax.random.normal(stream_key, shape, jnp.float32)
    if shards:
        entries = entries * shard_levels(stream_key, shape, shards, -0.22, 0.18)
    return jnp.clip(entries, -bound, bound).astype(kind)


def setup_inputs(seed: int = 0) -> dict:
    streams_of = jax.random.split(jax.random.key(seed), 17)
    inputs = noise(streams_of[0], (MICRO, SEQS, LENGTH, D), 1.0, 6.0, ((1, 4), (2, 8)))
    segments = draw_segments(jax.random.fold_in(streams_of[16], 71), 0)
    ln1_scale = jnp.clip(1.0 + 0.18 * jax.random.normal(streams_of[2], (D,), jnp.float32), 0.099609375, 1.8984375).astype(jnp.bfloat16)
    ln1_bias = noise(streams_of[3], (D,), 0.3, 1.75, ((0, 4),))
    w_qkv = noise(streams_of[4], (D, 3 * D), D ** -0.5, 0.21875, ((0, 4),))
    b_query = noise(streams_of[5], (D,), 0.3, 1.75, ((0, 4),))
    b_value = noise(streams_of[6], (D,), 0.3, 1.75, ((0, 4),))
    w_proj = noise(streams_of[7], (D, D), (max(1, D // 128)) ** -0.5, 2.5, ((0, 4),))
    b_proj = noise(streams_of[8], (D,), 0.3, 1.75, ((0, 4),))
    ln2_scale = jnp.clip(1.0 + 0.18 * jax.random.normal(streams_of[9], (D,), jnp.float32), 0.099609375, 1.8984375).astype(jnp.bfloat16)
    ln2_bias = noise(streams_of[10], (D,), 0.3, 1.75, ((0, 4),))
    w_up = noise(streams_of[11], (D, FF), D ** -0.5, 0.21875, ((0, 4),))
    b_up = noise(streams_of[12], (FF,), 0.3, 1.75, ((0, 4),))
    w_down = noise(streams_of[13], (FF, D), FF ** -0.5, 0.109375, ((0, 4),))
    b_down = noise(streams_of[14], (D,), 0.3, 1.75, ((0, 4),))
    cotangent = noise(streams_of[15], (MICRO, SEQS, LENGTH, D), 1.0, 6.0, ((1, 4), (2, 8)))
    return {"inputs": inputs, "segments": segments, "ln1_scale": ln1_scale, "ln1_bias": ln1_bias, "w_qkv": w_qkv, "b_query": b_query, "b_value": b_value, "w_proj": w_proj, "b_proj": b_proj, "ln2_scale": ln2_scale, "ln2_bias": ln2_bias, "w_up": w_up, "b_up": b_up, "w_down": w_down, "b_down": b_down, "cotangent": cotangent}


@jax.custom_vjp
def low(v):
    return lax.optimization_barrier(v.astype(jnp.bfloat16)).astype(jnp.float32)

@jax.custom_vjp
def low_back(v):
    return v

def low_keep(v):
    return (low(v), None)

def low_pass(kept, grad):
    return (grad,)

def back_keep(v):
    return (v, None)

def back_low(kept, grad):
    return (low(grad),)
low.defvjp(low_keep, low_pass)
low_back.defvjp(back_keep, back_low)
NORM_EPS = 1e-06
SCORE_SCALE = 0.125
MASKED = -1e+30

def rounded_both(values):
    return low(low_back(values))

def product(left, right):
    return jnp.dot(left, right, precision=lax.Precision.HIGHEST, preferred_element_type=jnp.float32)

def layer_norm(values, scale_vec, bias_vec):
    center = values - lax.optimization_barrier(jnp.mean(values, -1, keepdims=True))
    spread = lax.optimization_barrier(jnp.mean(center * center, -1, keepdims=True))
    return center * lax.rsqrt(spread + NORM_EPS) * scale_vec + bias_vec

def attend(queries, keys, values, segment_row):
    length = queries.shape[0]
    block_rows = math.gcd(length, 512)
    places = jnp.arange(length, dtype=jnp.int32)

    def one_block(element):
        query_blk, seg_blk, pos_blk = element
        scores = low_back(jnp.einsum('qhd,khd->qhk', query_blk, keys, precision=lax.Precision.HIGHEST) * SCORE_SCALE)
        allowed = (seg_blk[:, None] == segment_row[None, :]) & ((segment_row[None, :] >= 0) | (pos_blk[:, None] == places[None, :]))
        scores = jnp.where(allowed[:, None, :], scores, MASKED)
        row_top = lax.optimization_barrier(jnp.max(scores, -1, keepdims=True))
        expo = jnp.exp(scores - row_top)
        row_total = lax.optimization_barrier(jnp.sum(expo, -1))
        weighted = jnp.einsum('qhk,khd->qhd', low(expo), values, precision=lax.Precision.HIGHEST)
        return weighted / row_total[..., None]
    blocks = lax.map(jax.checkpoint(one_block), (queries.reshape(-1, block_rows, HEADS, HEAD_DIM), segment_row.reshape(-1, block_rows), places.reshape(-1, block_rows)))
    return blocks.reshape(length, HEADS * HEAD_DIM)

def block_layer(x_rows, segment_row, params):
    gain_one, shift_one, w_qkv, bias_query, bias_value, w_proj, bias_proj, gain_two, shift_two, w_up, bias_up, w_down, bias_down = params
    length = x_rows.shape[0]
    hidden_one = low(layer_norm(x_rows, gain_one, shift_one))
    projected = product(hidden_one, w_qkv)
    queries = rounded_both(projected[:, :D] + bias_query).reshape(length, HEADS, HEAD_DIM)
    keys = rounded_both(projected[:, D:2 * D]).reshape(length, HEADS, HEAD_DIM)
    values = rounded_both(projected[:, 2 * D:] + bias_value).reshape(length, HEADS, HEAD_DIM)
    mixed = rounded_both(attend(queries, keys, values, segment_row))
    resid = x_rows + low_back(product(mixed, w_proj) + bias_proj)
    hidden_two = low(layer_norm(resid, gain_two, shift_two))
    pre_act = low_back(product(hidden_two, w_up) + bias_up)
    activ = low(jax.nn.gelu(pre_act, approximate=True))
    return resid + product(activ, w_down) + bias_down

def reference(inputs, segments, ln1_scale, ln1_bias, w_qkv, b_query, b_value, w_proj, b_proj, ln2_scale, ln2_bias, w_up, b_up, w_down, b_down, cotangent):
    params = tuple((p.astype(jnp.float32) for p in (ln1_scale, ln1_bias, w_qkv, b_query, b_value, w_proj, b_proj, ln2_scale, ln2_bias, w_up, b_up, w_down, b_down)))
    seq_total = MICRO * SEQS
    x_all = inputs.astype(jnp.float32).reshape(seq_total, LENGTH, D)
    seg_all = segments.reshape(seq_total, LENGTH)
    cot_all = cotangent.astype(jnp.float32).reshape(seq_total, LENGTH, D)

    def step(running, element):
        x_rows, segment_row, cot_rows = element
        result, pull = jax.vjp(lambda a, b: block_layer(a, segment_row, b), x_rows, params)
        grad_x, grad_params = pull(cot_rows)
        running = jax.tree.map(lambda t, g: t + g, running, grad_params)
        return (running, (result.astype(jnp.bfloat16), grad_x.astype(jnp.bfloat16)))
    zeros = jax.tree.map(jnp.zeros_like, params)
    grads, (results, input_grads) = lax.scan(step, zeros, (x_all, seg_all, cot_all))
    return (results.reshape(inputs.shape), input_grads.reshape(inputs.shape), grads[0], grads[1], grads[2], grads[3], grads[4], grads[5], grads[6], grads[7], grads[8], grads[9], grads[10], grads[11], grads[12])
```

```python
import functools
import math

import jax
import jax.numpy as jnp
from jax import lax
from jax.experimental import pallas as pl
from jax.experimental.pallas import tpu as pltpu
from jax.sharding import PartitionSpec as P

HEADS = 12


NORM_EPS = 1e-06
SCORE_SCALE = 0.125
MASKED = -1e30


def layer_norm(values, scale_vec, bias_vec):
    center = values - jnp.mean(values, -1, keepdims=True)
    spread = jnp.mean(center * center, -1, keepdims=True)
    return center * lax.rsqrt(spread + NORM_EPS) * scale_vec + bias_vec


def gelu_tanh(values):
    return jax.nn.gelu(values, approximate=True)


def block_size(length_in, step_rows):
    blocked = step_rows
    while blocked * 2 <= 512 and length_in % (blocked * 2) == 0:
        blocked = blocked * 2
    return blocked


def to_heads(array, head_count):
    return array.reshape(array.shape[0], array.shape[1], head_count, -1)


def allowed_mask(seg_query, pos_query, seg_key, pos_key):
    same = seg_query[:, :, None] == seg_key[:, None, :]
    living = (seg_key[:, None, :] >= 0.0) | (pos_query[:, None] == pos_key[None, :])[None]
    return (same & living)[:, :, None, :]


def score_block(query_blk, key_blk, seg_query, pos_query, seg_key, pos_key):
    scores = (
        jnp.einsum("sqhd,skhd->sqhk", query_blk, key_blk, preferred_element_type=jnp.float32)
        * SCORE_SCALE
    )
    return (scores, allowed_mask(seg_query, pos_query, seg_key, pos_key))


def block_grads(
    query_blk,
    dout_blk,
    lse_blk,
    delta_blk,
    seg_query,
    pos_query,
    key_blk,
    value_blk,
    seg_key,
    pos_key,
):
    scores, allowed = score_block(query_blk, key_blk, seg_query, pos_query, seg_key, pos_key)
    probs = jnp.where(allowed, jnp.exp(scores - lse_blk[..., None]), 0.0)
    dprobs = jnp.einsum("sqhd,skhd->sqhk", dout_blk, value_blk, preferred_element_type=jnp.float32)
    dscores = (probs * (dprobs - delta_blk[..., None])).astype(jnp.bfloat16)
    return (dscores, probs.astype(jnp.bfloat16))


def key_side(
    query_blk,
    dout_blk,
    lse_blk,
    delta_blk,
    seg_query,
    pos_query,
    key_blk,
    value_blk,
    seg_key,
    pos_key,
):
    dscores, probs_low = block_grads(
        query_blk,
        dout_blk,
        lse_blk,
        delta_blk,
        seg_query,
        pos_query,
        key_blk,
        value_blk,
        seg_key,
        pos_key,
    )
    key_grad = (
        jnp.einsum("sqhk,sqhd->skhd", dscores, query_blk, preferred_element_type=jnp.float32)
        * SCORE_SCALE
    )
    value_grad = jnp.einsum(
        "sqhk,sqhd->skhd", probs_low, dout_blk, preferred_element_type=jnp.float32
    )
    return (key_grad, value_grad)


def contract_rows(left, right):
    return lax.dot_general(
        left, right, (((0,), (0,)), ((), ())), preferred_element_type=jnp.float32
    )


def contract_cols(left, right):
    return lax.dot_general(
        left, right, (((1,), (1,)), ((), ())), preferred_element_type=jnp.float32
    )


def per_device(
    inputs,
    segments,
    ln1_scale,
    ln1_bias,
    w_qkv,
    b_query,
    b_value,
    w_proj,
    b_proj,
    ln2_scale,
    ln2_bias,
    w_up,
    b_up,
    w_down,
    b_down,
    cotangent,
):
    micro_count, seq_dev, shard_len, model_width = inputs.shape
    head_count = HEADS
    head_width = model_width // head_count
    row_count = seq_dev * shard_len
    place = lax.axis_index("ctx")
    pos_local = place * shard_len + lax.iota(jnp.int32, shard_len)
    owned = (
        ln1_scale,
        ln1_bias,
        w_qkv,
        b_query,
        b_value,
        w_proj,
        b_proj,
        ln2_scale,
        ln2_bias,
        w_up,
        b_up,
        w_down,
        b_down,
    )
    summed_shards = None
    outputs_list = []
    input_grads = []
    for batch_num in range(micro_count):
        gathered = (
            lax.all_gather(owned[0], "fsdp", axis=0, tiled=True),
            lax.all_gather(owned[1], "fsdp", axis=0, tiled=True),
            lax.all_gather(owned[2], "fsdp", axis=0, tiled=True),
            lax.all_gather(owned[3], "fsdp", axis=0, tiled=True),
            lax.all_gather(owned[4], "fsdp", axis=0, tiled=True),
            lax.all_gather(owned[5], "fsdp", axis=0, tiled=True),
            lax.all_gather(owned[6], "fsdp", axis=0, tiled=True),
            lax.all_gather(owned[7], "fsdp", axis=0, tiled=True),
            lax.all_gather(owned[8], "fsdp", axis=0, tiled=True),
            lax.all_gather(owned[9], "fsdp", axis=0, tiled=True),
            lax.all_gather(owned[10], "fsdp", axis=0, tiled=True),
            lax.all_gather(owned[11], "fsdp", axis=0, tiled=True),
            lax.all_gather(owned[12], "fsdp", axis=0, tiled=True),
        )
        (
            gain_one,
            shift_one,
            w_qkv_all,
            bias_query,
            bias_value,
            w_proj_all,
            bias_proj,
            gain_two,
            shift_two,
            w_up_all,
            bias_up,
            w_down_all,
            bias_down,
        ) = gathered
        x_rows = inputs[batch_num].reshape(row_count, model_width).astype(jnp.float32)
        seg_local = segments[batch_num].astype(jnp.float32)
        cot_rows = cotangent[batch_num].reshape(row_count, model_width)
        normed_one, norm_one_pull = jax.vjp(
            layer_norm, x_rows, gain_one.astype(jnp.float32), shift_one.astype(jnp.float32)
        )
        hidden_one = normed_one.astype(jnp.bfloat16)
        projected = jnp.dot(hidden_one, w_qkv_all, preferred_element_type=jnp.float32)
        queries = (projected[:, :model_width] + bias_query.astype(jnp.float32)).astype(jnp.bfloat16)
        keys_loc = projected[:, model_width : 2 * model_width].astype(jnp.bfloat16)
        values_loc = (projected[:, 2 * model_width :] + bias_value.astype(jnp.float32)).astype(
            jnp.bfloat16
        )
        query_heads = queries.reshape(seq_dev, shard_len, head_count, head_width)
        shipped = (
            keys_loc.reshape(seq_dev, shard_len, model_width),
            values_loc.reshape(seq_dev, shard_len, model_width),
            seg_local.astype(jnp.bfloat16),
        )
        stat_shape = (seq_dev, shard_len, head_count)
        start_state = (
            jnp.full(stat_shape, MASKED, jnp.float32),
            jnp.zeros(stat_shape, jnp.float32),
            jnp.zeros((seq_dev, shard_len, head_count, head_width), jnp.float32),
        )
        key_part = lax.all_gather(shipped[0], "ctx", axis=1, tiled=True)
        value_part = lax.all_gather(shipped[1], "ctx", axis=1, tiled=True)
        seg_part = lax.all_gather(shipped[2], "ctx", axis=1, tiled=True)
        length_in = key_part.shape[1]
        step_len = block_size(length_in, shard_len)

        def forward_inner(turn, state):
            row_max, row_sum, weighted = state
            begin = turn * step_len
            key_blk = to_heads(lax.dynamic_slice_in_dim(key_part, begin, step_len, 1), head_count)
            value_blk = to_heads(
                lax.dynamic_slice_in_dim(value_part, begin, step_len, 1), head_count
            )
            seg_blk = lax.dynamic_slice_in_dim(seg_part, begin, step_len, 1).astype(jnp.float32)
            pos_blk = begin + lax.iota(jnp.int32, step_len)
            scores, allowed = score_block(
                query_heads, key_blk, seg_local, pos_local, seg_blk, pos_blk
            )
            scores = jnp.where(allowed, scores, MASKED)
            new_max = jnp.maximum(row_max, jnp.max(scores, -1))
            expo = jnp.where(allowed, jnp.exp(scores - new_max[..., None]), 0.0)
            factor = jnp.exp(row_max - new_max)
            row_sum = row_sum * factor + jnp.sum(expo, -1)
            weighted = weighted * factor[..., None] + jnp.einsum(
                "sqhk,skhd->sqhd",
                expo.astype(jnp.bfloat16),
                value_blk,
                preferred_element_type=jnp.float32,
            )
            return (new_max, row_sum, weighted)

        row_max, row_sum, weighted = lax.fori_loop(
            0, length_in // step_len, forward_inner, start_state
        )
        attended = weighted / row_sum[..., None]
        log_sum = row_max + jnp.log(row_sum)
        mixed = attended.reshape(row_count, model_width).astype(jnp.bfloat16)
        resid = (
            x_rows
            + jnp.dot(mixed, w_proj_all, preferred_element_type=jnp.float32)
            + bias_proj.astype(jnp.float32)
        )
        normed_two, norm_two_pull = jax.vjp(
            layer_norm, resid, gain_two.astype(jnp.float32), shift_two.astype(jnp.float32)
        )
        hidden_two = normed_two.astype(jnp.bfloat16)
        pre_act = jnp.dot(
            hidden_two, w_up_all, preferred_element_type=jnp.float32
        ) + bias_up.astype(jnp.float32)
        activ, gelu_pull = jax.vjp(gelu_tanh, pre_act)
        activ_low = activ.astype(jnp.bfloat16)
        result = (
            resid
            + jnp.dot(activ_low, w_down_all, preferred_element_type=jnp.float32)
            + bias_down.astype(jnp.float32)
        )
        outputs_list.append(result.astype(jnp.bfloat16).reshape(seq_dev, shard_len, model_width))
        d_activ = contract_cols(cot_rows, w_down_all)
        grad_down = contract_rows(activ_low, cot_rows)
        grad_bias_down = jnp.sum(cot_rows.astype(jnp.float32), 0)
        d_pre = gelu_pull(d_activ)[0].astype(jnp.bfloat16)
        grad_up = contract_rows(hidden_two, d_pre)
        grad_bias_up = jnp.sum(d_pre.astype(jnp.float32), 0)
        d_hidden_two = contract_cols(d_pre, w_up_all)
        d_resid_part, grad_gain_two, grad_shift_two = norm_two_pull(d_hidden_two)
        d_resid = cot_rows.astype(jnp.float32) + d_resid_part
        d_branch = d_resid.astype(jnp.bfloat16)
        grad_proj = contract_rows(mixed, d_branch)
        grad_bias_proj = jnp.sum(d_branch.astype(jnp.float32), 0)
        d_mixed = contract_cols(d_branch, w_proj_all).astype(jnp.bfloat16)
        dout_heads = d_mixed.reshape(seq_dev, shard_len, head_count, head_width)
        delta = jnp.sum(dout_heads.astype(jnp.float32) * attended, -1)
        zero_heads = jnp.zeros((seq_dev, shard_len, head_count, head_width), jnp.float32)
        key_all, value_all, seg_all = (
            lax.all_gather(shipped[0], "ctx", axis=1, tiled=True),
            lax.all_gather(shipped[1], "ctx", axis=1, tiled=True),
            lax.all_gather(shipped[2], "ctx", axis=1, tiled=True),
        )
        query_key_part = key_all
        query_value_part = value_all
        query_seg_part = seg_all
        query_length_in = query_key_part.shape[1]
        query_step_len = block_size(query_length_in, shard_len)

        def query_inner(turn, grad_in):
            begin = turn * query_step_len
            key_blk = to_heads(
                lax.dynamic_slice_in_dim(query_key_part, begin, query_step_len, 1), head_count
            )
            value_blk = to_heads(
                lax.dynamic_slice_in_dim(query_value_part, begin, query_step_len, 1), head_count
            )
            seg_blk = lax.dynamic_slice_in_dim(query_seg_part, begin, query_step_len, 1).astype(
                jnp.float32
            )
            pos_blk = 0 + begin + lax.iota(jnp.int32, query_step_len)
            dscores, probs_low = block_grads(
                query_heads,
                dout_heads,
                log_sum,
                delta,
                seg_local,
                pos_local,
                key_blk,
                value_blk,
                seg_blk,
                pos_blk,
            )
            return (
                grad_in
                + jnp.einsum(
                    "sqhk,skhd->sqhd", dscores, key_blk, preferred_element_type=jnp.float32
                )
                * SCORE_SCALE
            )

        query_grad = lax.fori_loop(0, query_length_in // query_step_len, query_inner, zero_heads)
        rows_in = shard_len * lax.axis_size("ctx")
        key_step_len = block_size(rows_in, shard_len)

        def one_block(turn):
            begin = turn * key_step_len
            key_blk = to_heads(
                lax.dynamic_slice_in_dim(key_all, begin, key_step_len, 1), head_count
            )
            value_blk = to_heads(
                lax.dynamic_slice_in_dim(value_all, begin, key_step_len, 1), head_count
            )
            seg_blk = lax.dynamic_slice_in_dim(seg_all, begin, key_step_len, 1).astype(jnp.float32)
            pos_blk = begin + lax.iota(jnp.int32, key_step_len)
            key_grad, value_grad = key_side(
                query_heads,
                dout_heads,
                log_sum,
                delta,
                seg_local,
                pos_local,
                key_blk,
                value_blk,
                seg_blk,
                pos_blk,
            )
            joined = jnp.stack(
                (
                    key_grad.reshape(seq_dev, key_step_len, model_width),
                    value_grad.reshape(seq_dev, key_step_len, model_width),
                ),
                2,
            )
            return joined.transpose(1, 0, 2, 3).reshape(key_step_len, seq_dev * 2 * model_width)

        blocks = lax.map(one_block, jnp.arange(rows_in // key_step_len, dtype=jnp.int32))
        own_terms = lax.psum_scatter(
            blocks.reshape(rows_in, seq_dev * 2 * model_width).astype(jnp.bfloat16),
            "ctx",
            scatter_dimension=0,
            tiled=True,
        ).astype(jnp.float32)
        own_terms = own_terms.reshape(shard_len, seq_dev, 2, model_width).transpose(1, 2, 0, 3)
        key_grad = own_terms[:, 0]
        value_grad = own_terms[:, 1]
        query_low = query_grad.reshape(row_count, model_width).astype(jnp.bfloat16)
        key_low = key_grad.reshape(row_count, model_width).astype(jnp.bfloat16)
        value_low = value_grad.reshape(row_count, model_width).astype(jnp.bfloat16)
        d_qkv = jnp.concatenate((query_low, key_low, value_low), 1)
        grad_qkv = contract_rows(hidden_one, d_qkv)
        grad_bias_query = jnp.sum(query_low.astype(jnp.float32), 0)
        grad_bias_value = jnp.sum(value_low.astype(jnp.float32), 0)
        d_hidden_one = contract_cols(d_qkv, w_qkv_all)
        d_input_part, grad_gain_one, grad_shift_one = norm_one_pull(d_hidden_one)
        input_grads.append(
            (d_resid + d_input_part).astype(jnp.bfloat16).reshape(seq_dev, shard_len, model_width)
        )
        local_grads = (
            grad_gain_one,
            grad_shift_one,
            grad_qkv,
            grad_bias_query,
            grad_bias_value,
            grad_proj,
            grad_bias_proj,
            grad_gain_two,
            grad_shift_two,
            grad_up,
            grad_bias_up,
            grad_down,
            grad_bias_down,
        )
        shard_part = (
            lax.psum_scatter(
                local_grads[0].astype(jnp.bfloat16), "fsdp", scatter_dimension=0, tiled=True
            ).astype(jnp.float32),
            lax.psum_scatter(
                local_grads[1].astype(jnp.bfloat16), "fsdp", scatter_dimension=0, tiled=True
            ).astype(jnp.float32),
            lax.psum_scatter(
                local_grads[2].astype(jnp.bfloat16), "fsdp", scatter_dimension=0, tiled=True
            ).astype(jnp.float32),
            lax.psum_scatter(
                local_grads[3].astype(jnp.bfloat16), "fsdp", scatter_dimension=0, tiled=True
            ).astype(jnp.float32),
            lax.psum_scatter(
                local_grads[4].astype(jnp.bfloat16), "fsdp", scatter_dimension=0, tiled=True
            ).astype(jnp.float32),
            lax.psum_scatter(
                local_grads[5].astype(jnp.bfloat16), "fsdp", scatter_dimension=0, tiled=True
            ).astype(jnp.float32),
            lax.psum_scatter(
                local_grads[6].astype(jnp.bfloat16), "fsdp", scatter_dimension=0, tiled=True
            ).astype(jnp.float32),
            lax.psum_scatter(
                local_grads[7].astype(jnp.bfloat16), "fsdp", scatter_dimension=0, tiled=True
            ).astype(jnp.float32),
            lax.psum_scatter(
                local_grads[8].astype(jnp.bfloat16), "fsdp", scatter_dimension=0, tiled=True
            ).astype(jnp.float32),
            lax.psum_scatter(
                local_grads[9].astype(jnp.bfloat16), "fsdp", scatter_dimension=0, tiled=True
            ).astype(jnp.float32),
            lax.psum_scatter(
                local_grads[10].astype(jnp.bfloat16), "fsdp", scatter_dimension=0, tiled=True
            ).astype(jnp.float32),
            lax.psum_scatter(
                local_grads[11].astype(jnp.bfloat16), "fsdp", scatter_dimension=0, tiled=True
            ).astype(jnp.float32),
            lax.psum_scatter(
                local_grads[12].astype(jnp.bfloat16), "fsdp", scatter_dimension=0, tiled=True
            ).astype(jnp.float32),
        )
        shard_part = (
            lax.psum(shard_part[0].astype(jnp.bfloat16), "ctx").astype(jnp.float32),
            lax.psum(shard_part[1].astype(jnp.bfloat16), "ctx").astype(jnp.float32),
            lax.psum(shard_part[2].astype(jnp.bfloat16), "ctx").astype(jnp.float32),
            lax.psum(shard_part[3].astype(jnp.bfloat16), "ctx").astype(jnp.float32),
            lax.psum(shard_part[4].astype(jnp.bfloat16), "ctx").astype(jnp.float32),
            lax.psum(shard_part[5].astype(jnp.bfloat16), "ctx").astype(jnp.float32),
            lax.psum(shard_part[6].astype(jnp.bfloat16), "ctx").astype(jnp.float32),
            lax.psum(shard_part[7].astype(jnp.bfloat16), "ctx").astype(jnp.float32),
            lax.psum(shard_part[8].astype(jnp.bfloat16), "ctx").astype(jnp.float32),
            lax.psum(shard_part[9].astype(jnp.bfloat16), "ctx").astype(jnp.float32),
            lax.psum(shard_part[10].astype(jnp.bfloat16), "ctx").astype(jnp.float32),
            lax.psum(shard_part[11].astype(jnp.bfloat16), "ctx").astype(jnp.float32),
            lax.psum(shard_part[12].astype(jnp.bfloat16), "ctx").astype(jnp.float32),
        )
        if summed_shards is None:
            summed_shards = shard_part
        else:
            summed_shards = tuple((old + new for old, new in zip(summed_shards, shard_part)))
    return (jnp.stack(outputs_list), jnp.stack(input_grads)) + tuple(summed_shards)


MESH = pl.DeviceIdType.MESH
F32 = jnp.float32
BF16 = jnp.bfloat16
GELU_A = math.sqrt(2.0 / math.pi)
GELU_B = 0.044715
LN1_S, LN1_B, B_Q, B_V, B_P, LN2_S, LN2_B, B_D, B_U = range(9)


def dot_nn(left, right):
    return lax.dot_general(left, right, (((1,), (0,)), ((), ())), preferred_element_type=F32)


def dot_nt(left, right):
    return lax.dot_general(left, right, (((1,), (1,)), ((), ())), preferred_element_type=F32)


def dot_tn(left, right):
    return lax.dot_general(left, right, (((0,), (0,)), ((), ())), preferred_element_type=F32)


def mult(value, factor):
    return pl.multiple_of(value, factor)


def loop_rows(total, step, body):
    def once(turn, carry):
        body(mult(turn * step, step))
        return carry

    lax.fori_loop(0, total // step, once, 0)


def norm_parts(values):
    center = values - jnp.mean(values, -1, keepdims=True)
    spread = jnp.mean(center * center, -1, keepdims=True)
    inv = lax.rsqrt(spread + NORM_EPS)
    return center * inv, inv


def norm_back(d_out, hat, inv, scale):
    d_hat = d_out * scale
    return inv * (
        d_hat - jnp.mean(d_hat, -1, keepdims=True) - hat * jnp.mean(d_hat * hat, -1, keepdims=True)
    )


def layer_kernel(
    inp, seg, pv, wq, wp, wu, wd, bu, cot,
    out_ref, din_ref, gd_ref, gu_ref, gp_ref, gq_ref, sg_ref,
    X, SEG, COT, H2, PV, WQ, WP, WU, WD, H1, Q, K, V, E, MB, ATT, LI, MIX, RES, ACT, DPRE,
    PDH, RDH, RDI, PO, RO, ROI, OUTB, DRES, DBR, DBX, DMS, DM, DOS, DLT, DQKV,
    GD, Z1D, ZSD, Z2D, ZFD, GU, RGU, Z1U, ZSU, Z2U, ZFU, GPP, RGP, GP, Z1P, ZSP, Z2P, ZFP,
    GQ, RGQ, GQF, Z1Q, ZSQ, Z2Q, ZFQ, PD1, RD1, DIN, SGP, SGS, SGB, SGF, SGZ, GBU,
    send_sem, recv_sem, local_sem,
):
    f = lax.axis_index("fsdp")
    c = lax.axis_index("ctx")
    z = c // 2
    h = c % 2
    o = 1 - h
    fpeers = (f + 1 - 2 * (f % 2), (f + 2) % 4, 3 - f)
    zpeers = (z + 1 - 2 * (z % 2), (z + 2) % 4, 3 - z)
    sib = (f, 2 * z + o)
    shard = inp.shape[1]
    half = 4 * shard
    rows_all = 2 * half
    wide = X.shape[1]
    hw = wide // 2
    kr = wide // 4
    own_rows = pl.ds(mult(h * half, half), half)
    oth_rows = pl.ds(mult(o * half, half), half)
    my_block = pl.ds(mult(h * half + z * shard, shard), shard)
    counts = [0, 0]

    def rc_make(src, dst, dev):
        i = counts[0]
        counts[0] += 1
        return pltpu.make_async_remote_copy(
            src_ref=src, dst_ref=dst, send_sem=send_sem.at[i], recv_sem=recv_sem.at[i],
            device_id=dev, device_id_type=MESH,
        )

    sent = []

    def rc(src, dst, dev):
        copy = rc_make(src, dst, dev)
        copy.start()
        sent.append(copy)
        return copy

    def lc(src, dst):
        i = counts[1]
        counts[1] += 1
        copy = pltpu.make_async_copy(src, dst, local_sem.at[i])
        copy.start()
        return copy

    def chunk_rows(j):
        return pl.ds(mult(j * rows_all + h * half, half), half)

    def chunk_other(j):
        return pl.ds(mult(j * rows_all + o * half, half), half)

    barrier = pltpu.get_barrier_semaphore()
    everyone = [(fp, c) for fp in fpeers] + [(f, 2 * zp + h) for zp in zpeers] + [sib]
    for dev in everyone:
        pl.semaphore_signal(barrier, inc=1, device_id=dev, device_id_type=MESH)
    pl.semaphore_wait(barrier, len(everyone))

    def cols(start):
        return pl.ds(mult(start, 128), hw)

    def krows(j):
        return pl.ds(mult(j * kr, kr), kr)

    x_in = [rc(inp.at[zp], X.at[my_block], (f, 2 * zp + h)) for zp in zpeers]
    s_in = [rc(seg.at[zp], SEG.at[my_block], (f, 2 * zp + h)) for zp in zpeers]
    pv_in = [rc(pv, PV.at[f], (fp, c)) for fp in fpeers]
    wq_in = [
        rc(wq.at[:, cols(b * wide + h * hw)], WQ.at[b, krows(f)], (fp, c))
        for b in range(3)
        for fp in fpeers
    ]
    cot_block = pl.ds(mult(f * rows_all + h * half + z * shard, shard), shard)
    c_in = [rc(cot.at[zp], COT.at[cot_block], (f, 2 * zp + h)) for zp in zpeers]
    x_own = lc(inp.at[z], X.at[my_block])
    s_own = lc(seg.at[z], SEG.at[my_block])
    pv_own = lc(pv, PV.at[f])
    wq_own = [lc(wq.at[:, cols(b * wide + h * hw)], WQ.at[b, krows(f)]) for b in range(3)]
    c_own = lc(cot.at[z], COT.at[cot_block])
    wd_own = lc(wd.at[pl.ds(mult(h * hw, hw), hw)], WD)
    wu_own = lc(wu.at[:, cols(f * wide + h * hw)], WU.at[krows(f)])
    wp_own = lc(wp.at[:, cols(h * hw)], WP.at[h, krows(f)])

    x_own.wait()
    s_own.wait()
    for copy in x_in + s_in:
        copy.wait_recv()
    x_sib = rc(X.at[own_rows], X.at[own_rows], sib)
    s_sib = rc(SEG.at[own_rows], SEG.at[own_rows], sib)
    pv_own.wait()
    for copy in pv_in:
        copy.wait_recv()
    vec = PV[0] + PV[1] + PV[2] + PV[3]
    PV[0] = vec

    def vector(i):
        return PV[0, i : i + 1, :]

    SGP[...] = jnp.zeros_like(SGP)
    GBU[...] = jnp.zeros_like(GBU)
    x_sib.wait_recv()
    s_sib.wait_recv()

    def ln1(r):
        hat, _ = norm_parts(X[pl.ds(r, 64), :].astype(F32))
        H1[pl.ds(r, 64), :] = (hat * vector(LN1_S) + vector(LN1_B)).astype(BF16)

    loop_rows(rows_all, 64, ln1)
    seg_row = jnp.transpose(SEG[...])[0:1, :]

    def mask(r):
        seg_col = SEG[pl.ds(r, 128), 0:1]
        place_q = r + lax.broadcasted_iota(jnp.int32, (128, rows_all), 0)
        place_k = lax.broadcasted_iota(jnp.int32, (128, rows_all), 1)
        allowed = (seg_col == seg_row) & ((seg_row >= 0.0) | (place_q == place_k))
        MB[pl.ds(r, 128), :] = jnp.where(allowed, 0.0, MASKED)

    loop_rows(rows_all, 128, mask)
    c_own.wait()
    for copy in c_in:
        copy.wait_recv()
    c_sib = rc(COT.at[chunk_rows(f)], COT.at[chunk_rows(f)], sib)

    for copy in wq_own:
        copy.wait()
    for copy in wq_in:
        copy.wait_recv()
    wp_own.wait()
    wp_in = [rc(wp.at[:, cols(h * hw)], WP.at[h, krows(f)], (fp, c)) for fp in fpeers]
    wu_in = [rc(wu.at[:, cols(fp * wide + h * hw)], WU.at[krows(f)], (fp, c)) for fp in fpeers]
    cot_in = [rc(COT.at[chunk_rows(f)], COT.at[chunk_rows(f)], (fp, c)) for fp in fpeers]
    bias_half = [PV[0, i : i + 1, cols(h * hw)] for i in (B_Q, B_V)]
    pairs = hw // 128
    for b, target in ((0, Q), (1, K), (2, V)):
        prod = dot_nn(H1[...], WQ[b])
        if b == 0:
            prod = (prod + bias_half[0]).astype(BF16) * SCORE_SCALE
        if b == 2:
            prod = prod + bias_half[1]
        prod = prod.astype(BF16)
        for p in range(pairs):
            target[p] = prod[:, p * 128 : (p + 1) * 128]

    lane = lax.broadcasted_iota(jnp.int32, (1, 128), 1)
    low_half = lane < 64

    def pick(s, values):
        keep = low_half if s == 0 else jnp.logical_not(low_half)
        return jnp.where(keep, values, jnp.zeros_like(values))

    mix_out = []
    for p in range(pairs):

        def attend(r, p=p):
            rows = pl.ds(r, 128)
            total = None
            for s in range(2):
                scores = dot_nt(pick(s, Q[p, rows, :]), K[p]) + MB[rows, :]
                top = jnp.max(scores, -1, keepdims=True)
                expo = jnp.exp(scores - top)
                inv = 1.0 / jnp.sum(expo, -1, keepdims=True)
                low = expo.astype(BF16)
                E[2 * p + s, rows, :] = low
                LI[2 * p + s, rows, :] = inv
                part = dot_nn(low, pick(s, V[p])) * inv
                total = part if total is None else total + part
            ATT[p, rows, :] = total
            MIX[3 * h + p, rows, :] = total.astype(BF16)

        loop_rows(rows_all, 128, attend)
        mix_out.append(rc(MIX.at[3 * h + p], MIX.at[3 * h + p], sib))

    for copy in wp_in:
        copy.wait_recv()
    wp_sib = rc(WP.at[h], WP.at[h], sib)
    for copy in mix_out:
        copy.wait_recv()
    wp_sib.wait_recv()

    def project(r):
        rows = pl.ds(mult(h * half + r, 64), 64)
        mixed = jnp.concatenate([MIX[g, rows, :] for g in range(2 * pairs)], axis=1)
        branch = jnp.concatenate([dot_nn(mixed, WP[k]) for k in range(2)], axis=1)
        resid = X[rows, :].astype(F32) + branch + vector(B_P)
        RES[pl.ds(r, 64), :] = resid
        hat, _ = norm_parts(resid)
        H2[pl.ds(mult(f * rows_all + h * half + r, 64), 64), :] = (
            hat * vector(LN2_S) + vector(LN2_B)
        ).astype(BF16)

    loop_rows(half, 64, project)
    h2_in = [rc(H2.at[chunk_rows(f)], H2.at[chunk_rows(f)], (fp, c)) for fp in fpeers]
    h2_sib = rc(H2.at[chunk_rows(f)], H2.at[chunk_rows(f)], sib)

    for copy in wu_in:
        copy.wait_recv()
    wu_own.wait()
    wd_own.wait()
    c_sib.wait_recv()
    h2_sib.wait_recv()
    bias_up = bu[h]

    def mlp(j):
        def block(r):
            rows = pl.ds(mult(j * rows_all + r, 128), 128)
            pre = dot_nn(H2[rows, :], WU[...]) + bias_up
            square = pre * pre
            tan = jnp.tanh(GELU_A * pre * (1.0 + GELU_B * square))
            low = (0.5 * pre * (1.0 + tan)).astype(BF16)
            slope = 0.5 * (1.0 + tan) + (0.5 * GELU_A) * pre * (1.0 - tan * tan) * (
                1.0 + (3.0 * GELU_B) * square
            )
            ACT[rows, :] = low
            d_pre = (dot_nt(COT[rows, :], WD[...]) * slope).astype(BF16)
            DPRE[rows, :] = d_pre
            GBU[...] += jnp.sum(d_pre.astype(F32), 0, keepdims=True)
            PDH[rows, :] = dot_nt(d_pre, WU[...]).astype(BF16)
            PO[rows, :] = dot_nn(low, WD[...]).astype(BF16)

        loop_rows(rows_all, 128, block)
        first = rc(PDH.at[chunk_other(j)], RDH.at[j], sib)
        second = rc(PO.at[chunk_other(j)], RO.at[j], sib)
        return first, second

    def join(buf, got, j):
        def block(r):
            rows = pl.ds(mult(j * rows_all + h * half + r, 64), 64)
            buf[rows, :] = (buf[rows, :].astype(F32) + got[j, pl.ds(r, 64), :].astype(F32)).astype(BF16)

        loop_rows(half, 64, block)

    own_pair = mlp(f)
    fwd = []
    for i, fp in enumerate(fpeers):
        cot_in[i].wait_recv()
        fwd.append(rc(COT.at[chunk_rows(fp)], COT.at[chunk_rows(fp)], sib))
    h2_fwd = []
    for i in range(2):
        h2_in[i].wait_recv()
        h2_fwd.append(rc(H2.at[chunk_rows(fpeers[i])], H2.at[chunk_rows(fpeers[i])], sib))
    pairs_out = []
    dh_in = []
    for i, fp in enumerate(fpeers):
        fwd[i].wait_recv()
        h2_fwd[i].wait_recv()
        pairs_out.append(mlp(fp))
        if i == 0:
            h2_in[2].wait_recv()
            h2_fwd.append(rc(H2.at[chunk_rows(fpeers[2])], H2.at[chunk_rows(fpeers[2])], sib))
        pairs_out[i][0].wait_recv()
        join(PDH, RDH, fp)
        dh_in.append(rc(PDH.at[chunk_rows(fp)], RDI.at[f], (fp, c)))
    o_in = []
    for i, fp in enumerate(fpeers):
        pairs_out[i][1].wait_recv()
        join(PO, RO, fp)
        o_in.append(rc(PO.at[chunk_rows(fp)], ROI.at[f], (fp, c)))

    inner = (z + 1) // 2 == 1
    outer = jnp.logical_not(inner)
    toward = (f, 2 * zpeers[0] + h)
    across = (f, 2 * zpeers[2] + h)

    class Chain:
        def __init__(self, own, z1, zs, z2, zf):
            self.own, self.z1, self.zs, self.z2, self.zf = own, z1, zs, z2, zf
            self.c1 = rc_make(own, z1, toward)
            self.c2 = rc_make(zs, z2, across)
            self.c3 = rc_make(zf.at[h], zf.at[h], toward)
            self.c4 = rc_make(zf.at[h], zf.at[h], sib)

        def first(self):
            @pl.when(outer)
            def _():
                self.c1.start()

        def second(self):
            @pl.when(inner)
            def _():
                self.c1.wait_recv()
                self.zs[...] = (self.own[...].astype(F32) + self.z1[...].astype(F32)).astype(BF16)
                self.c2.start()

        def third(self):
            @pl.when(inner)
            def _():
                self.c2.wait_recv()
                self.zf[h] = (self.zs[...].astype(F32) + self.z2[...].astype(F32)).astype(BF16)
                self.c3.start()

        def fourth(self):
            @pl.when(outer)
            def _():
                self.c3.wait_recv()
                self.c1.wait_send()

            @pl.when(inner)
            def _():
                self.c2.wait_send()
                self.c3.wait_send()

            self.c4.start()

        def fifth(self):
            self.c4.wait_recv()
            self.c4.wait_send()

    GD[...] = dot_tn(ACT[...], COT[...]).astype(BF16)
    chain_d = Chain(GD, Z1D, ZSD, Z2D, ZFD)
    chain_d.first()
    GU[...] = dot_tn(H2[...], DPRE[...]).astype(BF16)
    gu_in = [rc(GU.at[krows(fp)], RGU.at[f], (fp, c)) for fp in fpeers]
    RGU[f] = GU[krows(f), :]
    SGP[B_U : B_U + 1, cols(h * hw)] = GBU[...]

    own_pair[0].wait_recv()
    for copy in dh_in:
        copy.wait_recv()

    def ln2_back(r):
        rows = pl.ds(r, 64)
        mine = pl.ds(mult(f * rows_all + h * half + r, 64), 64)
        d_h2 = PDH[mine, :].astype(F32) + RDH[f, rows, :].astype(F32)
        for fp in fpeers:
            d_h2 = d_h2 + RDI[fp, rows, :].astype(F32)
        hat, inv = norm_parts(RES[rows, :])
        SGP[LN2_S : LN2_S + 1, :] += jnp.sum(d_h2 * hat, 0, keepdims=True)
        SGP[LN2_B : LN2_B + 1, :] += jnp.sum(d_h2, 0, keepdims=True)
        cot_rows = COT[mine, :].astype(F32)
        SGP[B_D : B_D + 1, :] += jnp.sum(cot_rows, 0, keepdims=True)
        d_resid = cot_rows + norm_back(d_h2, hat, inv, vector(LN2_S))
        DRES[rows, :] = d_resid
        low = d_resid.astype(BF16)
        SGP[B_P : B_P + 1, :] += jnp.sum(low.astype(F32), 0, keepdims=True)
        for k in range(2):
            DBR[k, rows, :] = low[:, k * hw : (k + 1) * hw]
        d_mixed = dot_nt(low[:, :hw], WP[0]) + dot_nt(low[:, hw:], WP[1])
        d_mixed = d_mixed.astype(BF16)
        for g in range(2 * pairs):
            DMS[g, rows, :] = d_mixed[:, g * 128 : (g + 1) * 128]

    loop_rows(half, 64, ln2_back)
    dm_sib = rc(DMS.at[pl.ds(3 * o, 3)], DM.at[:, own_rows, :], sib)
    dbr_sib = rc(DBR.at[o], DBX.at[own_rows], sib)
    DM[:, own_rows, :] = DMS[pl.ds(3 * h, 3)]
    DBX[own_rows, :] = DBR[h]
    chain_d.second()
    dbr_sib.wait_recv()
    mixed_all = jnp.concatenate([MIX[g] for g in range(2 * pairs)], axis=1)
    GPP[...] = dot_tn(mixed_all, DBX[...]).astype(BF16)
    gp_in = [rc(GPP.at[krows(fp)], RGP.at[f], (fp, c)) for fp in fpeers]
    dm_sib.wait_recv()

    def attention_back(p):
        def prepare(r):
            rows = pl.ds(r, 128)
            d_out = DM[p, rows, :].astype(F32)
            for s in range(2):
                scaled = pick(s, d_out * LI[2 * p + s, rows, :]).astype(BF16)
                DOS[s, rows, :] = scaled
                DLT[s, rows, :] = jnp.sum(scaled.astype(F32) * ATT[p, rows, :], -1, keepdims=True)

        loop_rows(rows_all, 128, prepare)
        here = slice(p * 128, (p + 1) * 128)
        d_value = dot_tn(E[2 * p], DOS[0]) + dot_tn(E[2 * p + 1], DOS[1])
        DQKV[2, :, here] = d_value.astype(BF16)

        def block(r):
            rows = pl.ds(r, 128)
            d_query = None
            for s in range(2):
                d_probs = dot_nt(DOS[s, rows, :], V[p])
                d_scores = (
                    E[2 * p + s, rows, :].astype(F32) * (d_probs - DLT[s, rows, :])
                ).astype(BF16)
                E[2 * p + s, rows, :] = d_scores
                part = dot_nn(d_scores, pick(s, K[p]))
                d_query = part if d_query is None else d_query + part
            DQKV[0, rows, here] = (d_query * SCORE_SCALE).astype(BF16)

        loop_rows(rows_all, 128, block)
        d_key = dot_tn(E[2 * p], pick(0, Q[p])) + dot_tn(E[2 * p + 1], pick(1, Q[p]))
        DQKV[1, :, here] = d_key.astype(BF16)

    attention_back(0)
    chain_d.third()
    for copy in gu_in:
        copy.wait_recv()
    chain_u = Chain(RGU, Z1U, ZSU, Z2U, ZFU)
    chain_u.first()
    attention_back(1)
    chain_d.fourth()
    own_pair[1].wait_recv()
    for copy in o_in:
        copy.wait_recv()

    def finish(r):
        rows = pl.ds(r, 64)
        mine = pl.ds(mult(f * rows_all + h * half + r, 64), 64)
        total = PO[mine, :].astype(F32) + RO[f, rows, :].astype(F32)
        for fp in fpeers:
            total = total + ROI[fp, rows, :].astype(F32)
        OUTB[rows, :] = (RES[rows, :] + total + vector(B_D)).astype(BF16)

    loop_rows(half, 64, finish)

    def block_of(zp):
        return pl.ds(mult(zp * shard, shard), shard)

    res_in = [rc(OUTB.at[block_of(zp)], out_ref.at[z], (f, 2 * zp + h)) for zp in zpeers]
    res_own = lc(OUTB.at[block_of(z)], out_ref.at[z])
    chain_u.second()
    for copy in gp_in:
        copy.wait_recv()

    def owned_sum(own, got):
        total = own.astype(F32)
        for fp in fpeers:
            total = total + got[fp].astype(F32)
        return total.astype(BF16)

    GP[...] = owned_sum(GPP[krows(f), :], RGP)
    chain_p = Chain(GP, Z1P, ZSP, Z2P, ZFP)
    chain_p.first()
    attention_back(2)
    chain_u.third()
    chain_p.second()

    for b in range(3):
        GQ[b] = dot_tn(H1[...], DQKV[b]).astype(BF16)
    gq_in = [rc(GQ.at[:, krows(fp), :], RGQ.at[f], (fp, c)) for fp in fpeers]
    PD1[...] = (
        dot_nt(DQKV[0], WQ[0]) + dot_nt(DQKV[1], WQ[1]) + dot_nt(DQKV[2], WQ[2])
    ).astype(BF16)
    d1_sib = rc(PD1.at[oth_rows], RD1, sib)
    for b, i in ((0, B_Q), (2, B_V)):
        SGP[i : i + 1, cols(h * hw)] = jnp.sum(DQKV[b].astype(F32), 0, keepdims=True)
    d1_sib.wait_recv()

    def ln1_back(r):
        rows = pl.ds(r, 64)
        mine = pl.ds(mult(h * half + r, 64), 64)
        d_h1 = PD1[mine, :].astype(F32) + RD1[rows, :].astype(F32)
        hat, inv = norm_parts(X[mine, :].astype(F32))
        SGP[LN1_S : LN1_S + 1, :] += jnp.sum(d_h1 * hat, 0, keepdims=True)
        SGP[LN1_B : LN1_B + 1, :] += jnp.sum(d_h1, 0, keepdims=True)
        DIN[rows, :] = (DRES[rows, :] + norm_back(d_h1, hat, inv, vector(LN1_S))).astype(BF16)

    loop_rows(half, 64, ln1_back)
    din_in = [rc(DIN.at[block_of(zp)], din_ref.at[z], (f, 2 * zp + h)) for zp in zpeers]
    din_own = lc(DIN.at[block_of(z)], din_ref.at[z])
    sg_sib = rc(SGP, SGS, sib)
    chain_u.fourth()
    chain_p.third()
    chain_p.fourth()
    sg_sib.wait_recv()
    SGB[f] = SGP[...] + SGS[...]
    sgf_in = [rc(SGB.at[f], SGB.at[f], (fp, c)) for fp in fpeers]

    for copy in gq_in:
        copy.wait_recv()
    for b in range(3):
        total = GQ[b, krows(f), :].astype(F32)
        for fp in fpeers:
            total = total + RGQ[fp, b].astype(F32)
        GQF[b] = total.astype(BF16)
    chain_q = Chain(GQF, Z1Q, ZSQ, Z2Q, ZFQ)
    chain_q.first()
    for copy in sgf_in:
        copy.wait_recv()
    plane = SGB[0] + SGB[1] + SGB[2] + SGB[3]
    row_id = lax.broadcasted_iota(jnp.int32, plane.shape, 0)
    SGZ[z] = jnp.where(row_id == B_U, SGB[f], plane)
    sgz_in = [rc(SGZ.at[z], SGZ.at[z], (f, 2 * zp + h)) for zp in zpeers]
    chain_q.second()
    chain_d.fifth()
    outs = [lc(ZFD.at[k], gd_ref.at[pl.ds(k * hw, hw)]) for k in range(2)]
    chain_u.fifth()
    outs += [
        lc(ZFU.at[k, s], gu_ref.at[:, pl.ds(s * wide + k * hw, hw)]) for k in range(2) for s in range(4)
    ]
    chain_p.fifth()
    outs += [lc(ZFP.at[k], gp_ref.at[:, pl.ds(k * hw, hw)]) for k in range(2)]
    chain_q.third()
    for copy in sgz_in:
        copy.wait_recv()
    sg_ref[...] = SGZ[0] + SGZ[1] + SGZ[2] + SGZ[3]
    chain_q.fourth()
    chain_q.fifth()
    outs += [
        lc(ZFQ.at[k, b], gq_ref.at[:, pl.ds(b * wide + k * hw, hw)]) for k in range(2) for b in range(3)
    ]
    for copy in res_in + din_in:
        copy.wait_recv()
    for copy in outs + [res_own, din_own]:
        copy.wait()
    for copy in sent:
        copy.wait_send()


def fast_device(
    inputs, segments, ln1_scale, ln1_bias, w_qkv, b_query, b_value, w_proj, b_proj,
    ln2_scale, ln2_bias, w_up, b_up, w_down, b_down, cotangent,
):
    micro_count, seq_dev, shard, wide = inputs.shape
    seqs = micro_count * seq_dev
    rows_all = 8 * shard
    half = rows_all // 2
    hw = wide // 2
    kr = wide // 4
    pairs = hw // 128
    heads = 2 * pairs
    f = lax.axis_index("fsdp")
    vectors = jnp.stack(
        (ln1_scale, ln1_bias, b_query, b_value, b_proj, ln2_scale, ln2_bias, b_down)
    ).astype(F32)
    spot = lax.broadcasted_iota(jnp.int32, (8, wide), 1) // kr == f
    packed = jnp.where(spot, jnp.tile(vectors, (1, 4)), 0.0)
    seg_wide = jnp.broadcast_to(
        segments.reshape(seqs, shard, 1).astype(F32), (seqs, shard, 128)
    )

    def vm(*shape, dtype=BF16):
        return pltpu.VMEM(shape, dtype)

    f32 = functools.partial(vm, dtype=F32)
    scratch = [
        vm(rows_all, wide), f32(rows_all, 128), vm(4 * rows_all, wide), vm(4 * rows_all, wide),
        f32(4, 8, wide), vm(3, wide, hw), vm(2, wide, hw), vm(wide, hw), vm(hw, wide),
        vm(rows_all, wide), vm(pairs, rows_all, 128), vm(pairs, rows_all, 128),
        vm(pairs, rows_all, 128), vm(heads, rows_all, rows_all), f32(rows_all, rows_all),
        f32(pairs, rows_all, 128), f32(heads, rows_all, 1), vm(2 * pairs, rows_all, 128),
        f32(half, wide), vm(4 * rows_all, hw), vm(4 * rows_all, hw),
        vm(4 * rows_all, wide), vm(4, half, wide), vm(4, half, wide),
        vm(4 * rows_all, wide), vm(4, half, wide), vm(4, half, wide), vm(half, wide),
        f32(half, wide), vm(2, half, hw), vm(rows_all, hw), vm(2 * pairs, half, 128),
        vm(pairs, rows_all, 128), vm(2, rows_all, 128), f32(2, rows_all, 1),
        vm(3, rows_all, hw),
        vm(hw, wide), vm(hw, wide), vm(hw, wide), vm(hw, wide), vm(2, hw, wide),
        vm(wide, hw), vm(4, kr, hw), vm(4, kr, hw), vm(4, kr, hw), vm(4, kr, hw), vm(2, 4, kr, hw),
        vm(wide, hw), vm(4, kr, hw), vm(kr, hw), vm(kr, hw), vm(kr, hw), vm(kr, hw), vm(2, kr, hw),
        vm(3, wide, hw), vm(4, 3, kr, hw), vm(3, kr, hw), vm(3, kr, hw), vm(3, kr, hw),
        vm(3, kr, hw), vm(2, 3, kr, hw),
        vm(rows_all, wide), vm(half, wide), vm(half, wide),
        f32(16, wide), f32(16, wide), f32(4, 16, wide), f32(16, wide), f32(4, 16, wide), f32(1, hw),
        pltpu.SemaphoreType.DMA((112,)), pltpu.SemaphoreType.DMA((112,)),
        pltpu.SemaphoreType.DMA((40,)),
    ]
    hbm = pl.BlockSpec(memory_space=pl.ANY)
    vmem = pl.BlockSpec(memory_space=pltpu.VMEM)
    tokens = jax.ShapeDtypeStruct((seqs, shard, wide), BF16)
    results = pl.pallas_call(
        layer_kernel,
        out_shape=(
            tokens, tokens,
            jax.ShapeDtypeStruct(w_down.shape, BF16), jax.ShapeDtypeStruct(w_up.shape, BF16),
            jax.ShapeDtypeStruct(w_proj.shape, BF16), jax.ShapeDtypeStruct(w_qkv.shape, BF16),
            jax.ShapeDtypeStruct((16, wide), F32),
        ),
        in_specs=[hbm] * 7 + [vmem, hbm],
        out_specs=(hbm,) * 6 + (vmem,),
        scratch_shapes=scratch,
        compiler_params=pltpu.CompilerParams(
            collective_id=0, has_side_effects=True, vmem_limit_bytes=62 << 20
        ),
    )(
        inputs.reshape(tokens.shape), seg_wide, packed, w_qkv, w_proj, w_up, w_down,
        b_up.astype(F32).reshape(2, 1, hw), cotangent.reshape(tokens.shape),
    )
    out, d_input, g_down, g_up, g_proj, g_qkv, small = results
    mine = lax.dynamic_slice_in_dim(small[:8], f * kr, kr, 1)
    return (
        out.reshape(inputs.shape), d_input.reshape(inputs.shape),
        mine[LN1_S], mine[LN1_B], g_qkv.astype(F32), mine[B_Q], mine[B_V],
        g_proj.astype(F32), mine[B_P], mine[LN2_S], mine[LN2_B],
        g_up.astype(F32), small[B_U], g_down.astype(F32), mine[B_D],
    )


def fits_fast(mesh, inputs, w_up):
    micro_count, seqs, length, wide = inputs.shape
    return (
        mesh.shape["fsdp"] == 4
        and mesh.shape["ctx"] == 8
        and micro_count * (seqs // 4) == 4
        and length == 512
        and wide == 768
        and w_up.shape == (wide, 4 * wide)
        and HEADS * 64 == wide
    )


def solution(mesh):
    placed = (
        P(None, "fsdp", "ctx", None),
        P(None, "fsdp", "ctx"),
        P("fsdp"),
        P("fsdp"),
        P("fsdp", None),
        P("fsdp"),
        P("fsdp"),
        P("fsdp", None),
        P("fsdp"),
        P("fsdp"),
        P("fsdp"),
        P("fsdp", None),
        P("fsdp"),
        P("fsdp", None),
        P("fsdp"),
        P(None, "fsdp", "ctx", None),
    )
    def layer(*args):
        chosen = fast_device if fits_fast(mesh, args[0], args[11]) else per_device
        return spread(chosen)(*args)

    spread = functools.partial(
        jax.shard_map,
        mesh=mesh,
        in_specs=placed,
        out_specs=(
            P(None, "fsdp", "ctx", None),
            P(None, "fsdp", "ctx", None),
            P("fsdp"),
            P("fsdp"),
            P("fsdp", None),
            P("fsdp"),
            P("fsdp"),
            P("fsdp", None),
            P("fsdp"),
            P("fsdp"),
            P("fsdp"),
            P("fsdp", None),
            P("fsdp"),
            P("fsdp", None),
            P("fsdp"),
        ),
        check_vma=False,
    )
    return layer
```

```python
import functools
import math

import jax
import jax.numpy as jnp
from jax import lax
from jax.experimental import pallas as pl
from jax.experimental.pallas import tpu as pltpu
from jax.sharding import PartitionSpec as P

HEADS = 12


NORM_EPS = 1e-06
SCORE_SCALE = 0.125
MASKED = -1e30


def layer_norm(values, scale_vec, bias_vec):
    center = values - jnp.mean(values, -1, keepdims=True)
    spread = jnp.mean(center * center, -1, keepdims=True)
    return center * lax.rsqrt(spread + NORM_EPS) * scale_vec + bias_vec


def gelu_tanh(values):
    return jax.nn.gelu(values, approximate=True)


def block_size(length_in, step_rows):
    blocked = step_rows
    while blocked * 2 <= 512 and length_in % (blocked * 2) == 0:
        blocked = blocked * 2
    return blocked


def to_heads(array, head_count):
    return array.reshape(array.shape[0], array.shape[1], head_count, -1)


def allowed_mask(seg_query, pos_query, seg_key, pos_key):
    same = seg_query[:, :, None] == seg_key[:, None, :]
    living = (seg_key[:, None, :] >= 0.0) | (pos_query[:, None] == pos_key[None, :])[None]
    return (same & living)[:, :, None, :]


def score_block(query_blk, key_blk, seg_query, pos_query, seg_key, pos_key):
    scores = (
        jnp.einsum("sqhd,skhd->sqhk", query_blk, key_blk, preferred_element_type=jnp.float32)
        * SCORE_SCALE
    )
    return (scores, allowed_mask(seg_query, pos_query, seg_key, pos_key))


def block_grads(
    query_blk,
    dout_blk,
    lse_blk,
    delta_blk,
    seg_query,
    pos_query,
    key_blk,
    value_blk,
    seg_key,
    pos_key,
):
    scores, allowed = score_block(query_blk, key_blk, seg_query, pos_query, seg_key, pos_key)
    probs = jnp.where(allowed, jnp.exp(scores - lse_blk[..., None]), 0.0)
    dprobs = jnp.einsum("sqhd,skhd->sqhk", dout_blk, value_blk, preferred_element_type=jnp.float32)
    dscores = (probs * (dprobs - delta_blk[..., None])).astype(jnp.bfloat16)
    return (dscores, probs.astype(jnp.bfloat16))


def key_side(
    query_blk,
    dout_blk,
    lse_blk,
    delta_blk,
    seg_query,
    pos_query,
    key_blk,
    value_blk,
    seg_key,
    pos_key,
):
    dscores, probs_low = block_grads(
        query_blk,
        dout_blk,
        lse_blk,
        delta_blk,
        seg_query,
        pos_query,
        key_blk,
        value_blk,
        seg_key,
        pos_key,
    )
    key_grad = (
        jnp.einsum("sqhk,sqhd->skhd", dscores, query_blk, preferred_element_type=jnp.float32)
        * SCORE_SCALE
    )
    value_grad = jnp.einsum(
        "sqhk,sqhd->skhd", probs_low, dout_blk, preferred_element_type=jnp.float32
    )
    return (key_grad, value_grad)


def contract_rows(left, right):
    return lax.dot_general(
        left, right, (((0,), (0,)), ((), ())), preferred_element_type=jnp.float32
    )


def contract_cols(left, right):
    return lax.dot_general(
        left, right, (((1,), (1,)), ((), ())), preferred_element_type=jnp.float32
    )


def per_device(
    inputs,
    segments,
    ln1_scale,
    ln1_bias,
    w_qkv,
    b_query,
    b_value,
    w_proj,
    b_proj,
    ln2_scale,
    ln2_bias,
    w_up,
    b_up,
    w_down,
    b_down,
    cotangent,
):
    micro_count, seq_dev, shard_len, model_width = inputs.shape
    head_count = HEADS
    head_width = model_width // head_count
    row_count = seq_dev * shard_len
    place = lax.axis_index("ctx")
    pos_local = place * shard_len + lax.iota(jnp.int32, shard_len)
    owned = (
        ln1_scale,
        ln1_bias,
        w_qkv,
        b_query,
        b_value,
        w_proj,
        b_proj,
        ln2_scale,
        ln2_bias,
        w_up,
        b_up,
        w_down,
        b_down,
    )
    summed_shards = None
    outputs_list = []
    input_grads = []
    for batch_num in range(micro_count):
        gathered = (
            lax.all_gather(owned[0], "fsdp", axis=0, tiled=True),
            lax.all_gather(owned[1], "fsdp", axis=0, tiled=True),
            lax.all_gather(owned[2], "fsdp", axis=0, tiled=True),
            lax.all_gather(owned[3], "fsdp", axis=0, tiled=True),
            lax.all_gather(owned[4], "fsdp", axis=0, tiled=True),
            lax.all_gather(owned[5], "fsdp", axis=0, tiled=True),
            lax.all_gather(owned[6], "fsdp", axis=0, tiled=True),
            lax.all_gather(owned[7], "fsdp", axis=0, tiled=True),
            lax.all_gather(owned[8], "fsdp", axis=0, tiled=True),
            lax.all_gather(owned[9], "fsdp", axis=0, tiled=True),
            lax.all_gather(owned[10], "fsdp", axis=0, tiled=True),
            lax.all_gather(owned[11], "fsdp", axis=0, tiled=True),
            lax.all_gather(owned[12], "fsdp", axis=0, tiled=True),
        )
        (
            gain_one,
            shift_one,
            w_qkv_all,
            bias_query,
            bias_value,
            w_proj_all,
            bias_proj,
            gain_two,
            shift_two,
            w_up_all,
            bias_up,
            w_down_all,
            bias_down,
        ) = gathered
        x_rows = inputs[batch_num].reshape(row_count, model_width).astype(jnp.float32)
        seg_local = segments[batch_num].astype(jnp.float32)
        cot_rows = cotangent[batch_num].reshape(row_count, model_width)
        normed_one, norm_one_pull = jax.vjp(
            layer_norm, x_rows, gain_one.astype(jnp.float32), shift_one.astype(jnp.float32)
        )
        hidden_one = normed_one.astype(jnp.bfloat16)
        projected = jnp.dot(hidden_one, w_qkv_all, preferred_element_type=jnp.float32)
        queries = (projected[:, :model_width] + bias_query.astype(jnp.float32)).astype(jnp.bfloat16)
        keys_loc = projected[:, model_width : 2 * model_width].astype(jnp.bfloat16)
        values_loc = (projected[:, 2 * model_width :] + bias_value.astype(jnp.float32)).astype(
            jnp.bfloat16
        )
        query_heads = queries.reshape(seq_dev, shard_len, head_count, head_width)
        shipped = (
            keys_loc.reshape(seq_dev, shard_len, model_width),
            values_loc.reshape(seq_dev, shard_len, model_width),
            seg_local.astype(jnp.bfloat16),
        )
        stat_shape = (seq_dev, shard_len, head_count)
        start_state = (
            jnp.full(stat_shape, MASKED, jnp.float32),
            jnp.zeros(stat_shape, jnp.float32),
            jnp.zeros((seq_dev, shard_len, head_count, head_width), jnp.float32),
        )
        key_part = lax.all_gather(shipped[0], "ctx", axis=1, tiled=True)
        value_part = lax.all_gather(shipped[1], "ctx", axis=1, tiled=True)
        seg_part = lax.all_gather(shipped[2], "ctx", axis=1, tiled=True)
        length_in = key_part.shape[1]
        step_len = block_size(length_in, shard_len)

        def forward_inner(turn, state):
            row_max, row_sum, weighted = state
            begin = turn * step_len
            key_blk = to_heads(lax.dynamic_slice_in_dim(key_part, begin, step_len, 1), head_count)
            value_blk = to_heads(
                lax.dynamic_slice_in_dim(value_part, begin, step_len, 1), head_count
            )
            seg_blk = lax.dynamic_slice_in_dim(seg_part, begin, step_len, 1).astype(jnp.float32)
            pos_blk = begin + lax.iota(jnp.int32, step_len)
            scores, allowed = score_block(
                query_heads, key_blk, seg_local, pos_local, seg_blk, pos_blk
            )
            scores = jnp.where(allowed, scores, MASKED)
            new_max = jnp.maximum(row_max, jnp.max(scores, -1))
            expo = jnp.where(allowed, jnp.exp(scores - new_max[..., None]), 0.0)
            factor = jnp.exp(row_max - new_max)
            row_sum = row_sum * factor + jnp.sum(expo, -1)
            weighted = weighted * factor[..., None] + jnp.einsum(
                "sqhk,skhd->sqhd",
                expo.astype(jnp.bfloat16),
                value_blk,
                preferred_element_type=jnp.float32,
            )
            return (new_max, row_sum, weighted)

        row_max, row_sum, weighted = lax.fori_loop(
            0, length_in // step_len, forward_inner, start_state
        )
        attended = weighted / row_sum[..., None]
        log_sum = row_max + jnp.log(row_sum)
        mixed = attended.reshape(row_count, model_width).astype(jnp.bfloat16)
        resid = (
            x_rows
            + jnp.dot(mixed, w_proj_all, preferred_element_type=jnp.float32)
            + bias_proj.astype(jnp.float32)
        )
        normed_two, norm_two_pull = jax.vjp(
            layer_norm, resid, gain_two.astype(jnp.float32), shift_two.astype(jnp.float32)
        )
        hidden_two = normed_two.astype(jnp.bfloat16)
        pre_act = jnp.dot(
            hidden_two, w_up_all, preferred_element_type=jnp.float32
        ) + bias_up.astype(jnp.float32)
        activ, gelu_pull = jax.vjp(gelu_tanh, pre_act)
        activ_low = activ.astype(jnp.bfloat16)
        result = (
            resid
            + jnp.dot(activ_low, w_down_all, preferred_element_type=jnp.float32)
            + bias_down.astype(jnp.float32)
        )
        outputs_list.append(result.astype(jnp.bfloat16).reshape(seq_dev, shard_len, model_width))
        d_activ = contract_cols(cot_rows, w_down_all)
        grad_down = contract_rows(activ_low, cot_rows)
        grad_bias_down = jnp.sum(cot_rows.astype(jnp.float32), 0)
        d_pre = gelu_pull(d_activ)[0].astype(jnp.bfloat16)
        grad_up = contract_rows(hidden_two, d_pre)
        grad_bias_up = jnp.sum(d_pre.astype(jnp.float32), 0)
        d_hidden_two = contract_cols(d_pre, w_up_all)
        d_resid_part, grad_gain_two, grad_shift_two = norm_two_pull(d_hidden_two)
        d_resid = cot_rows.astype(jnp.float32) + d_resid_part
        d_branch = d_resid.astype(jnp.bfloat16)
        grad_proj = contract_rows(mixed, d_branch)
        grad_bias_proj = jnp.sum(d_branch.astype(jnp.float32), 0)
        d_mixed = contract_cols(d_branch, w_proj_all).astype(jnp.bfloat16)
        dout_heads = d_mixed.reshape(seq_dev, shard_len, head_count, head_width)
        delta = jnp.sum(dout_heads.astype(jnp.float32) * attended, -1)
        zero_heads = jnp.zeros((seq_dev, shard_len, head_count, head_width), jnp.float32)
        key_all, value_all, seg_all = (
            lax.all_gather(shipped[0], "ctx", axis=1, tiled=True),
            lax.all_gather(shipped[1], "ctx", axis=1, tiled=True),
            lax.all_gather(shipped[2], "ctx", axis=1, tiled=True),
        )
        query_key_part = key_all
        query_value_part = value_all
        query_seg_part = seg_all
        query_length_in = query_key_part.shape[1]
        query_step_len = block_size(query_length_in, shard_len)

        def query_inner(turn, grad_in):
            begin = turn * query_step_len
            key_blk = to_heads(
                lax.dynamic_slice_in_dim(query_key_part, begin, query_step_len, 1), head_count
            )
            value_blk = to_heads(
                lax.dynamic_slice_in_dim(query_value_part, begin, query_step_len, 1), head_count
            )
            seg_blk = lax.dynamic_slice_in_dim(query_seg_part, begin, query_step_len, 1).astype(
                jnp.float32
            )
            pos_blk = 0 + begin + lax.iota(jnp.int32, query_step_len)
            dscores, probs_low = block_grads(
                query_heads,
                dout_heads,
                log_sum,
                delta,
                seg_local,
                pos_local,
                key_blk,
                value_blk,
                seg_blk,
                pos_blk,
            )
            return (
                grad_in
                + jnp.einsum(
                    "sqhk,skhd->sqhd", dscores, key_blk, preferred_element_type=jnp.float32
                )
                * SCORE_SCALE
            )

        query_grad = lax.fori_loop(0, query_length_in // query_step_len, query_inner, zero_heads)
        rows_in = shard_len * lax.axis_size("ctx")
        key_step_len = block_size(rows_in, shard_len)

        def one_block(turn):
            begin = turn * key_step_len
            key_blk = to_heads(
                lax.dynamic_slice_in_dim(key_all, begin, key_step_len, 1), head_count
            )
            value_blk = to_heads(
                lax.dynamic_slice_in_dim(value_all, begin, key_step_len, 1), head_count
            )
            seg_blk = lax.dynamic_slice_in_dim(seg_all, begin, key_step_len, 1).astype(jnp.float32)
            pos_blk = begin + lax.iota(jnp.int32, key_step_len)
            key_grad, value_grad = key_side(
                query_heads,
                dout_heads,
                log_sum,
                delta,
                seg_local,
                pos_local,
                key_blk,
                value_blk,
                seg_blk,
                pos_blk,
            )
            joined = jnp.stack(
                (
                    key_grad.reshape(seq_dev, key_step_len, model_width),
                    value_grad.reshape(seq_dev, key_step_len, model_width),
                ),
                2,
            )
            return joined.transpose(1, 0, 2, 3).reshape(key_step_len, seq_dev * 2 * model_width)

        blocks = lax.map(one_block, jnp.arange(rows_in // key_step_len, dtype=jnp.int32))
        own_terms = lax.psum_scatter(
            blocks.reshape(rows_in, seq_dev * 2 * model_width).astype(jnp.bfloat16),
            "ctx",
            scatter_dimension=0,
            tiled=True,
        ).astype(jnp.float32)
        own_terms = own_terms.reshape(shard_len, seq_dev, 2, model_width).transpose(1, 2, 0, 3)
        key_grad = own_terms[:, 0]
        value_grad = own_terms[:, 1]
        query_low = query_grad.reshape(row_count, model_width).astype(jnp.bfloat16)
        key_low = key_grad.reshape(row_count, model_width).astype(jnp.bfloat16)
        value_low = value_grad.reshape(row_count, model_width).astype(jnp.bfloat16)
        d_qkv = jnp.concatenate((query_low, key_low, value_low), 1)
        grad_qkv = contract_rows(hidden_one, d_qkv)
        grad_bias_query = jnp.sum(query_low.astype(jnp.float32), 0)
        grad_bias_value = jnp.sum(value_low.astype(jnp.float32), 0)
        d_hidden_one = contract_cols(d_qkv, w_qkv_all)
        d_input_part, grad_gain_one, grad_shift_one = norm_one_pull(d_hidden_one)
        input_grads.append(
            (d_resid + d_input_part).astype(jnp.bfloat16).reshape(seq_dev, shard_len, model_width)
        )
        local_grads = (
            grad_gain_one,
            grad_shift_one,
            grad_qkv,
            grad_bias_query,
            grad_bias_value,
            grad_proj,
            grad_bias_proj,
            grad_gain_two,
            grad_shift_two,
            grad_up,
            grad_bias_up,
            grad_down,
            grad_bias_down,
        )
        shard_part = (
            lax.psum_scatter(
                local_grads[0].astype(jnp.bfloat16), "fsdp", scatter_dimension=0, tiled=True
            ).astype(jnp.float32),
            lax.psum_scatter(
                local_grads[1].astype(jnp.bfloat16), "fsdp", scatter_dimension=0, tiled=True
            ).astype(jnp.float32),
            lax.psum_scatter(
                local_grads[2].astype(jnp.bfloat16), "fsdp", scatter_dimension=0, tiled=True
            ).astype(jnp.float32),
            lax.psum_scatter(
                local_grads[3].astype(jnp.bfloat16), "fsdp", scatter_dimension=0, tiled=True
            ).astype(jnp.float32),
            lax.psum_scatter(
                local_grads[4].astype(jnp.bfloat16), "fsdp", scatter_dimension=0, tiled=True
            ).astype(jnp.float32),
            lax.psum_scatter(
                local_grads[5].astype(jnp.bfloat16), "fsdp", scatter_dimension=0, tiled=True
            ).astype(jnp.float32),
            lax.psum_scatter(
                local_grads[6].astype(jnp.bfloat16), "fsdp", scatter_dimension=0, tiled=True
            ).astype(jnp.float32),
            lax.psum_scatter(
                local_grads[7].astype(jnp.bfloat16), "fsdp", scatter_dimension=0, tiled=True
            ).astype(jnp.float32),
            lax.psum_scatter(
                local_grads[8].astype(jnp.bfloat16), "fsdp", scatter_dimension=0, tiled=True
            ).astype(jnp.float32),
            lax.psum_scatter(
                local_grads[9].astype(jnp.bfloat16), "fsdp", scatter_dimension=0, tiled=True
            ).astype(jnp.float32),
            lax.psum_scatter(
                local_grads[10].astype(jnp.bfloat16), "fsdp", scatter_dimension=0, tiled=True
            ).astype(jnp.float32),
            lax.psum_scatter(
                local_grads[11].astype(jnp.bfloat16), "fsdp", scatter_dimension=0, tiled=True
            ).astype(jnp.float32),
            lax.psum_scatter(
                local_grads[12].astype(jnp.bfloat16), "fsdp", scatter_dimension=0, tiled=True
            ).astype(jnp.float32),
        )
        shard_part = (
            lax.psum(shard_part[0].astype(jnp.bfloat16), "ctx").astype(jnp.float32),
            lax.psum(shard_part[1].astype(jnp.bfloat16), "ctx").astype(jnp.float32),
            lax.psum(shard_part[2].astype(jnp.bfloat16), "ctx").astype(jnp.float32),
            lax.psum(shard_part[3].astype(jnp.bfloat16), "ctx").astype(jnp.float32),
            lax.psum(shard_part[4].astype(jnp.bfloat16), "ctx").astype(jnp.float32),
            lax.psum(shard_part[5].astype(jnp.bfloat16), "ctx").astype(jnp.float32),
            lax.psum(shard_part[6].astype(jnp.bfloat16), "ctx").astype(jnp.float32),
            lax.psum(shard_part[7].astype(jnp.bfloat16), "ctx").astype(jnp.float32),
            lax.psum(shard_part[8].astype(jnp.bfloat16), "ctx").astype(jnp.float32),
            lax.psum(shard_part[9].astype(jnp.bfloat16), "ctx").astype(jnp.float32),
            lax.psum(shard_part[10].astype(jnp.bfloat16), "ctx").astype(jnp.float32),
            lax.psum(shard_part[11].astype(jnp.bfloat16), "ctx").astype(jnp.float32),
            lax.psum(shard_part[12].astype(jnp.bfloat16), "ctx").astype(jnp.float32),
        )
        if summed_shards is None:
            summed_shards = shard_part
        else:
            summed_shards = tuple((old + new for old, new in zip(summed_shards, shard_part)))
    return (jnp.stack(outputs_list), jnp.stack(input_grads)) + tuple(summed_shards)


MESH = pl.DeviceIdType.MESH
F32 = jnp.float32
BF16 = jnp.bfloat16
GELU_A = math.sqrt(2.0 / math.pi)
GELU_B = 0.044715
LN1_S, LN1_B, B_Q, B_V, B_P, LN2_S, LN2_B, B_D, B_U = range(9)


def dot_nn(left, right):
    return lax.dot_general(left, right, (((1,), (0,)), ((), ())), preferred_element_type=F32)


def dot_nt(left, right):
    return lax.dot_general(left, right, (((1,), (1,)), ((), ())), preferred_element_type=F32)


def dot_tn(left, right):
    return lax.dot_general(left, right, (((0,), (0,)), ((), ())), preferred_element_type=F32)


def mult(value, factor):
    return pl.multiple_of(value, factor)


def loop_rows(total, step, body):
    def once(turn, carry):
        body(mult(turn * step, step))
        return carry

    lax.fori_loop(0, total // step, once, 0)


def norm_parts(values):
    center = values - jnp.mean(values, -1, keepdims=True)
    spread = jnp.mean(center * center, -1, keepdims=True)
    inv = lax.rsqrt(spread + NORM_EPS)
    return center * inv, inv


def norm_back(d_out, hat, inv, scale):
    d_hat = d_out * scale
    return inv * (
        d_hat - jnp.mean(d_hat, -1, keepdims=True) - hat * jnp.mean(d_hat * hat, -1, keepdims=True)
    )


def layer_kernel(
    inp, seg, v0, v1, v2, v3, v4, v5, v6, v7, wq, wp, wu, wd, bu, cot,
    out_ref, din_ref, gd_ref, gu_ref, gp_ref, gq_ref, sg_ref,
    X, SEGS, SEGR, SEG, COT, H2, PV, VEC, WQ, WP, WU, WD, H1, Q, K, V, E, MB, ATT, LI, MIX, RES,
    ACT, DPRE, PDH, RDH, RDI, PO, RO, ROI, OUTB, DRES, DBR, DBX, DMS, DM, DOS, DLT, DQKV,
    GD, Z1D, ZSD, Z2D, ZFD, GU, Z1U, ZSU, Z2U, GUZ, ZFU, GPP, RGP, GP, Z1P, ZSP, Z2P, ZFP,
    GQ, RGQ, GQF, Z1Q, ZSQ, Z2Q, ZFQ, PD1, RD1, DIN, SGP, SGS, SGB, SGZ, GBU,
    send_sem, recv_sem, local_sem,
):
    f = lax.axis_index("fsdp")
    c = lax.axis_index("ctx")
    z = c // 2
    h = c % 2
    o = 1 - h
    fx, fy, fd = fpeers = (f + 1 - 2 * (f % 2), (f + 2) % 4, 3 - f)
    zpeers = (z + 1 - 2 * (z % 2), (z + 2) % 4, 3 - z)
    sib = (f, 2 * z + o)
    seq_dev = seg.shape[1]
    shard = inp.shape[1]
    half = 4 * shard
    rows_all = 2 * half
    wide = X.shape[1]
    hw = wide // 2
    kr = wide // 4
    pairs = hw // 128
    own_rows = pl.ds(mult(h * half, half), half)
    oth_rows = pl.ds(mult(o * half, half), half)
    my_block = pl.ds(mult(h * half + z * shard, shard), shard)
    counts = [0, 0]

    def rc_make(src, dst, dev):
        i = counts[0]
        counts[0] += 1
        return pltpu.make_async_remote_copy(
            src_ref=src, dst_ref=dst, send_sem=send_sem.at[i], recv_sem=recv_sem.at[i],
            device_id=dev, device_id_type=MESH,
        )

    sent = []

    def rc(src, dst, dev):
        copy = rc_make(src, dst, dev)
        copy.start()
        sent.append(copy)
        return copy

    def lc(src, dst):
        i = counts[1]
        counts[1] += 1
        copy = pltpu.make_async_copy(src, dst, local_sem.at[i])
        copy.start()
        return copy

    def chunk_rows(j):
        return pl.ds(mult(j * rows_all + h * half, half), half)

    def chunk_other(j):
        return pl.ds(mult(j * rows_all + o * half, half), half)

    def cols(start):
        return pl.ds(mult(start, 128), hw)

    def krows(j):
        return pl.ds(mult(j * kr, kr), kr)

    def hrows(j, i):
        return pl.ds(mult(j * kr + i * (kr // 2), kr // 2), kr // 2)

    def token_rows(j, i):
        return pl.ds(mult(j * rows_all + h * half + i * (half // 2), half // 2), half // 2)

    def block_of(zp):
        return pl.ds(mult(zp * shard, shard), shard)

    class Gather:
        def __init__(self, own, at):
            self.at = at
            self.to_x, self.to_y = {}, {}
            for first, second in ((0, 1), (1, 0)):
                self.to_x[first] = [rc(src, dst, (fx, c)) for src, dst in own(first)]
                self.to_y[second] = [rc(src, dst, (fy, c)) for src, dst in own(second)]

        def relay(self):
            for copy in self.to_x[0]:
                copy.wait_recv()
            self.far_y = rc(self.at(fx, 0), self.at(fx, 0), (fy, c))
            for copy in self.to_y[1]:
                copy.wait_recv()
            self.far_x = rc(self.at(fy, 1), self.at(fy, 1), (fx, c))

        def near(self):
            for copy in self.to_x[1] + self.to_y[0]:
                copy.wait_recv()

        def far(self):
            self.far_y.wait_recv()
            self.far_x.wait_recv()

    class Scatter:
        def __init__(self, part, got, last):
            self.part, self.got, self.last = part, got, last

        def near(self):
            self.a0 = rc(self.part(fx, 0), self.got(0, 0), (fx, c))
            self.b0 = rc(self.part(fy, 1), self.got(0, 1), (fy, c))

        def far(self):
            self.a1 = rc(self.part(fd, 0), self.got(1, 0), (fx, c))
            self.b1 = rc(self.part(fd, 1), self.got(1, 1), (fy, c))

        def relay(self):
            self.a1.wait_recv()
            mine = self.part(fy, 0)
            mine[...] = (mine[...].astype(F32) + self.got(1, 0)[...].astype(F32)).astype(BF16)
            self.a2 = rc(mine, self.last(0), (fy, c))
            self.b1.wait_recv()
            mine = self.part(fx, 1)
            mine[...] = (mine[...].astype(F32) + self.got(1, 1)[...].astype(F32)).astype(BF16)
            self.b2 = rc(mine, self.last(1), (fx, c))

        def wait(self):
            for copy in (self.a0, self.b0, self.a2, self.b2):
                copy.wait_recv()

    inner = (z + 1) // 2 == 1
    outer = jnp.logical_not(inner)
    toward = (f, 2 * zpeers[0] + h)
    across = (f, 2 * zpeers[2] + h)

    class Chain:
        def __init__(self, own, z1, zs, z2, zf):
            self.own, self.z1, self.zs, self.z2, self.zf = own, z1, zs, z2, zf
            self.c1 = rc_make(own, z1, toward)
            self.c2 = rc_make(zs, z2, across)
            self.c3 = rc_make(zf, zf, toward)

        def first(self):
            @pl.when(outer)
            def _():
                self.c1.start()

        def second(self):
            @pl.when(inner)
            def _():
                self.c1.wait_recv()
                self.zs[...] = (self.own[...].astype(F32) + self.z1[...].astype(F32)).astype(BF16)
                self.c2.start()

        def third(self):
            @pl.when(inner)
            def _():
                self.c2.wait_recv()
                self.zf[...] = (self.zs[...].astype(F32) + self.z2[...].astype(F32)).astype(BF16)
                self.c3.start()

        def fourth(self):
            @pl.when(outer)
            def _():
                self.c3.wait_recv()
                self.c1.wait_send()

            @pl.when(inner)
            def _():
                self.c2.wait_send()
                self.c3.wait_send()

            return self.zf

    stacked = jnp.concatenate(
        [v[...].astype(F32).reshape(1, kr) for v in (v0, v1, v2, v3, v4, v5, v6, v7)], axis=0
    )
    PV[f] = stacked
    for s in range(4):
        row = seg[s // seq_dev, s % seq_dev : s % seq_dev + 1, :].astype(F32)
        row = jnp.concatenate([row, jnp.zeros((1, 128 - shard), F32)], axis=1)
        SEGS[s] = jnp.broadcast_to(row, (8, 128))
    up_bias = bu[...].astype(F32).reshape(1, wide)
    bias_up = jnp.where(h == 0, up_bias[:, :hw], up_bias[:, hw:])

    barrier = pltpu.get_barrier_semaphore()
    everyone = [(fp, c) for fp in fpeers] + [(f, 2 * zp + h) for zp in zpeers] + [sib]
    for dev in everyone:
        pl.semaphore_signal(barrier, inc=1, device_id=dev, device_id_type=MESH)
    pl.semaphore_wait(barrier, len(everyone))

    def wq_own_part(i):
        return [
            (wq.at[hrows(0, i), cols(b * wide + h * hw)], WQ.at[b, hrows(f, i)]) for b in range(3)
        ]

    pv_in = [rc(PV.at[f], PV.at[f], (fp, c)) for fp in fpeers]
    wq_all = Gather(wq_own_part, lambda j, i: WQ.at[:, hrows(j, i), :])
    my_slot = 4 * h + z
    s_in = [rc(SEGS.at[zp], SEGR.at[my_slot], (f, 2 * zp + h)) for zp in zpeers]
    x_in = [rc(inp.at[zp], X.at[my_block], (f, 2 * zp + h)) for zp in zpeers]
    cot_block = pl.ds(mult(f * rows_all + h * half + z * shard, shard), shard)
    c_in = [rc(cot.at[zp], COT.at[cot_block], (f, 2 * zp + h)) for zp in zpeers]
    x_own = lc(inp.at[z], X.at[my_block])
    wq_own = [lc(wq.at[:, cols(b * wide + h * hw)], WQ.at[b, krows(f)]) for b in range(3)]
    wp_own = lc(wp.at[:, cols(h * hw)], WP.at[h, krows(f)])
    c_own = lc(cot.at[z], COT.at[cot_block])
    wd_own = lc(wd.at[pl.ds(mult(h * hw, hw), hw)], WD)
    wu_own = lc(wu.at[:, cols(f * wide + h * hw)], WU.at[krows(f)])
    SEGR[my_slot] = SEGS[z]
    SGP[...] = jnp.zeros_like(SGP)
    GBU[...] = jnp.zeros_like(GBU)
    wq_all.relay()
    wp_all = Gather(
        lambda i: [(wp.at[hrows(0, i), cols(h * hw)], WP.at[h, hrows(f, i)])],
        lambda j, i: WP.at[h, hrows(j, i)],
    )

    for copy in pv_in:
        copy.wait_recv()
    VEC[...] = jnp.concatenate([PV[j] for j in range(4)], axis=1)

    def vector(i):
        return VEC[i : i + 1, :]

    x_own.wait()
    for copy in s_in + x_in:
        copy.wait_recv()
    my_slots = pl.ds(4 * h, 4)
    s_sib = rc(SEGR.at[my_slots], SEGR.at[my_slots], sib)
    x_sib = rc(X.at[own_rows], X.at[own_rows], sib)

    def ln1(start):
        def block(r):
            rows = pl.ds(mult(start + r, 64), 64)
            hat, _ = norm_parts(X[rows, :].astype(F32))
            H1[rows, :] = (hat * vector(LN1_S) + vector(LN1_B)).astype(BF16)

        loop_rows(half, 64, block)

    ln1(h * half)
    s_sib.wait_recv()
    for b in range(8):
        turned = jnp.transpose(jnp.broadcast_to(SEGR[b][0:1, :], (128, 128)))
        SEG[pl.ds(b * shard, shard), :] = turned[:shard, :]
    seg_row = jnp.transpose(SEG[...])[0:1, :]

    def mask(r):
        rows = pl.ds(r, 128)
        seg_col = SEG[rows, 0:1]
        place_q = r + lax.broadcasted_iota(jnp.int32, (128, rows_all), 0)
        place_k = lax.broadcasted_iota(jnp.int32, (128, rows_all), 1)
        allowed = (seg_col == seg_row) & ((seg_row >= 0.0) | (place_q == place_k))
        MB[rows, :] = jnp.where(allowed, 0.0, MASKED)

    x_sib.wait_recv()
    ln1(o * half)
    loop_rows(rows_all, 128, mask)

    for copy in wq_own:
        copy.wait()
    wp_own.wait()
    wq_all.near()
    wq_all.far()
    wp_all.relay()
    wu_in = [rc(wu.at[:, cols(fp * wide + h * hw)], WU.at[krows(f)], (fp, c)) for fp in fpeers]
    bias_half = [
        jnp.where(h == 0, vector(i)[:, :hw], vector(i)[:, hw:]) for i in (B_Q, B_V)
    ]
    for b, target in ((0, Q), (1, K), (2, V)):
        prod = dot_nn(H1[...], WQ[b])
        if b == 0:
            prod = (prod + bias_half[0]).astype(BF16) * SCORE_SCALE
        if b == 2:
            prod = prod + bias_half[1]
        prod = prod.astype(BF16)
        for p in range(pairs):
            target[p] = prod[:, p * 128 : (p + 1) * 128]
    c_own.wait()
    for copy in c_in:
        copy.wait_recv()
    c_sib = rc(COT.at[chunk_rows(f)], COT.at[chunk_rows(f)], sib)

    low_half = lax.broadcasted_iota(jnp.int32, (1, 128), 1) < 64

    def pick(s, values):
        keep = low_half if s == 0 else jnp.logical_not(low_half)
        return jnp.where(keep, values, jnp.zeros_like(values))

    mix_out = []
    for p in range(pairs):

        def attend(r, p=p):
            rows = pl.ds(r, 128)
            total = None
            for s in range(2):
                scores = dot_nt(pick(s, Q[p, rows, :]), K[p]) + MB[rows, :]
                top = jnp.max(scores, -1, keepdims=True)
                expo = jnp.exp(scores - top)
                inv = 1.0 / jnp.sum(expo, -1, keepdims=True)
                low = expo.astype(BF16)
                E[2 * p + s, rows, :] = low
                LI[2 * p + s, rows, :] = inv
                part = dot_nn(low, pick(s, V[p])) * inv
                total = part if total is None else total + part
            ATT[p, rows, :] = total
            MIX[pairs * h + p, rows, :] = total.astype(BF16)

        loop_rows(rows_all, 128, attend)
        mix_out.append(rc(MIX.at[pairs * h + p], MIX.at[pairs * h + p], sib))
        if p == 0:
            cot_all = Gather(
                lambda i: [(COT.at[token_rows(f, i)], COT.at[token_rows(f, i)])],
                lambda j, i: COT.at[token_rows(j, i)],
            )

    wp_all.near()
    wp_all.far()
    wp_sib = rc(WP.at[h], WP.at[h], sib)
    for copy in mix_out:
        copy.wait_recv()
    wp_sib.wait_recv()

    def project(r):
        rows = pl.ds(mult(h * half + r, 64), 64)
        mixed = jnp.concatenate([MIX[g, rows, :] for g in range(2 * pairs)], axis=1)
        branch = jnp.concatenate([dot_nn(mixed, WP[k]) for k in range(2)], axis=1)
        resid = X[rows, :].astype(F32) + branch + vector(B_P)
        RES[pl.ds(r, 64), :] = resid
        hat, _ = norm_parts(resid)
        H2[pl.ds(mult(f * rows_all + h * half + r, 64), 64), :] = (
            hat * vector(LN2_S) + vector(LN2_B)
        ).astype(BF16)

    loop_rows(half, 64, project)
    h2_all = Gather(
        lambda i: [(H2.at[token_rows(f, i)], H2.at[token_rows(f, i)])],
        lambda j, i: H2.at[token_rows(j, i)],
    )
    h2_sib = rc(H2.at[chunk_rows(f)], H2.at[chunk_rows(f)], sib)
    cot_all.relay()

    for copy in wu_in:
        copy.wait_recv()
    wu_own.wait()
    wd_own.wait()
    c_sib.wait_recv()
    h2_sib.wait_recv()

    def mlp(j):
        def block(r):
            rows = pl.ds(mult(j * rows_all + r, 128), 128)
            pre = dot_nn(H2[rows, :], WU[...]) + bias_up
            square = pre * pre
            tan = jnp.tanh(GELU_A * pre * (1.0 + GELU_B * square))
            low = (0.5 * pre * (1.0 + tan)).astype(BF16)
            slope = 0.5 * (1.0 + tan) + (0.5 * GELU_A) * pre * (1.0 - tan * tan) * (
                1.0 + (3.0 * GELU_B) * square
            )
            ACT[rows, :] = low
            d_pre = (dot_nt(COT[rows, :], WD[...]) * slope).astype(BF16)
            DPRE[rows, :] = d_pre
            GBU[...] += jnp.sum(d_pre.astype(F32), 0, keepdims=True)
            PDH[rows, :] = dot_nt(d_pre, WU[...]).astype(BF16)
            PO[rows, :] = dot_nn(low, WD[...]).astype(BF16)

        loop_rows(rows_all, 128, block)
        first = rc(PDH.at[chunk_other(j)], RDH.at[j], sib)
        second = rc(PO.at[chunk_other(j)], RO.at[j], sib)
        return first, second

    def join(buf, got, j):
        def block(r):
            rows = pl.ds(mult(j * rows_all + h * half + r, 64), 64)
            buf[rows, :] = (buf[rows, :].astype(F32) + got[j, pl.ds(r, 64), :].astype(F32)).astype(BF16)

        loop_rows(half, 64, block)

    def across_core(buf, j):
        return rc(buf.at[chunk_rows(j)], buf.at[chunk_rows(j)], sib)

    own_pair = mlp(f)
    cot_all.near()
    cot_fwd = [across_core(COT, fx), across_core(COT, fy)]
    h2_all.relay()
    h2_all.near()
    h2_fwd = [across_core(H2, fx), across_core(H2, fy)]
    d_plane = Scatter(
        lambda j, i: PDH.at[token_rows(j, i)],
        lambda w, i: RDI.at[w, pl.ds(i * (half // 2), half // 2)],
        lambda i: RDI.at[2, pl.ds(i * (half // 2), half // 2)],
    )
    o_plane = Scatter(
        lambda j, i: PO.at[token_rows(j, i)],
        lambda w, i: ROI.at[w, pl.ds(i * (half // 2), half // 2)],
        lambda i: ROI.at[2, pl.ds(i * (half // 2), half // 2)],
    )
    cot_fwd[0].wait_recv()
    h2_fwd[0].wait_recv()
    x_pair = mlp(fx)
    cot_all.far()
    cot_fwd.append(across_core(COT, fd))
    cot_fwd[1].wait_recv()
    h2_fwd[1].wait_recv()
    y_pair = mlp(fy)
    h2_all.far()
    h2_fwd.append(across_core(H2, fd))
    x_pair[0].wait_recv()
    join(PDH, RDH, fx)
    y_pair[0].wait_recv()
    join(PDH, RDH, fy)
    d_plane.near()
    cot_fwd[2].wait_recv()
    h2_fwd[2].wait_recv()
    d_pair = mlp(fd)
    own_pair[0].wait_recv()
    join(PDH, RDH, f)
    d_pair[0].wait_recv()
    join(PDH, RDH, fd)
    d_plane.far()
    for pair, j in ((own_pair, f), (x_pair, fx), (y_pair, fy), (d_pair, fd)):
        pair[1].wait_recv()
        join(PO, RO, j)

    GD[...] = dot_tn(ACT[...], COT[...]).astype(BF16)
    chain_d, chain_u = [], []
    for i in range(2):
        part = pl.ds(i * (hw // 2), hw // 2)
        chain_d.append(
            Chain(GD.at[part], Z1D.at[part], ZSD.at[part], Z2D.at[part], ZFD.at[h, part])
        )
        chain_d[i].first()
    d_plane.relay()
    o_plane.near()
    o_plane.far()
    GU[...] = dot_tn(H2[...], DPRE[...]).astype(BF16)
    for i in range(2):
        part = pl.ds(i * hw, hw)
        chain_u.append(Chain(GU.at[part], Z1U.at[part], ZSU.at[part], Z2U.at[part], GUZ.at[part]))
        chain_u[i].first()
    SGP[B_U : B_U + 1, cols(h * hw)] = GBU[...]

    d_plane.wait()

    def ln2_back(r):
        rows = pl.ds(r, 64)
        mine = pl.ds(mult(f * rows_all + h * half + r, 64), 64)
        d_h2 = PDH[mine, :].astype(F32)
        for w in (0, 2):
            d_h2 = d_h2 + RDI[w, rows, :].astype(F32)
        hat, inv = norm_parts(RES[rows, :])
        SGP[LN2_S : LN2_S + 1, :] += jnp.sum(d_h2 * hat, 0, keepdims=True)
        SGP[LN2_B : LN2_B + 1, :] += jnp.sum(d_h2, 0, keepdims=True)
        cot_rows = COT[mine, :].astype(F32)
        SGP[B_D : B_D + 1, :] += jnp.sum(cot_rows, 0, keepdims=True)
        d_resid = cot_rows + norm_back(d_h2, hat, inv, vector(LN2_S))
        DRES[rows, :] = d_resid
        low = d_resid.astype(BF16)
        SGP[B_P : B_P + 1, :] += jnp.sum(low.astype(F32), 0, keepdims=True)
        for k in range(2):
            DBR[k, rows, :] = low[:, k * hw : (k + 1) * hw]
        d_mixed = dot_nt(low[:, :hw], WP[0]) + dot_nt(low[:, hw:], WP[1])
        d_mixed = d_mixed.astype(BF16)
        for g in range(2 * pairs):
            DMS[g, rows, :] = d_mixed[:, g * 128 : (g + 1) * 128]

    loop_rows(half, 64, ln2_back)
    dm_sib = rc(DMS.at[pl.ds(pairs * o, pairs)], DM.at[:, own_rows, :], sib)
    dbr_sib = rc(DBR.at[o], DBX.at[own_rows], sib)
    DM[:, own_rows, :] = DMS[pl.ds(pairs * h, pairs)]
    DBX[own_rows, :] = DBR[h]
    chain_d[0].second()
    dbr_sib.wait_recv()
    mixed_all = jnp.concatenate([MIX[g] for g in range(2 * pairs)], axis=1)
    GPP[...] = dot_tn(mixed_all, DBX[...]).astype(BF16)
    p_plane = Scatter(
        lambda j, i: GPP.at[hrows(j, i)],
        lambda w, i: RGP.at[w, hrows(0, i)],
        lambda i: RGP.at[2, hrows(0, i)],
    )
    p_plane.far()
    p_plane.near()
    dm_sib.wait_recv()

    def attention_back(p, steps):
        def prepare(r):
            rows = pl.ds(r, 128)
            d_out = DM[p, rows, :].astype(F32)
            for s in range(2):
                scaled = pick(s, d_out * LI[2 * p + s, rows, :]).astype(BF16)
                DOS[s, rows, :] = scaled
                DLT[s, rows, :] = jnp.sum(scaled.astype(F32) * ATT[p, rows, :], -1, keepdims=True)

        loop_rows(rows_all, 128, prepare)
        d_value = dot_tn(E[2 * p], DOS[0]) + dot_tn(E[2 * p + 1], DOS[1])
        DQKV[p, :, 256:384] = d_value.astype(BF16)
        for step in steps[0]:
            step()

        def block(r):
            rows = pl.ds(r, 128)
            d_query = None
            for s in range(2):
                d_probs = dot_nt(DOS[s, rows, :], V[p])
                d_scores = (
                    E[2 * p + s, rows, :].astype(F32) * (d_probs - DLT[s, rows, :])
                ).astype(BF16)
                E[2 * p + s, rows, :] = d_scores
                part = dot_nn(d_scores, pick(s, K[p]))
                d_query = part if d_query is None else d_query + part
            DQKV[p, rows, 0:128] = (d_query * SCORE_SCALE).astype(BF16)

        loop_rows(rows_all, 128, block)
        for step in steps[1]:
            step()
        d_key = dot_tn(E[2 * p], pick(0, Q[p])) + dot_tn(E[2 * p + 1], pick(1, Q[p]))
        DQKV[p, :, 128:256] = d_key.astype(BF16)
        GQ[p] = dot_tn(H1[...], DQKV[p]).astype(BF16)
        plane = Scatter(
            lambda j, i: GQ.at[p, hrows(j, i)],
            lambda w, i: RGQ.at[p, w, hrows(0, i)],
            lambda i: RGQ.at[p, 2, hrows(0, i)],
        )
        for step in steps[2]:
            step()
        plane.far()
        plane.near()
        here = pl.ds(mult(h * hw + p * 128, 128), 128)
        for b, i in ((0, B_Q), (2, B_V)):
            SGP[i : i + 1, here] = jnp.sum(
                DQKV[p, :, b * 128 : (b + 1) * 128].astype(F32), 0, keepdims=True
            )
        return plane

    kept = {}

    def finish_out():
        o_plane.wait()

        def finish(r):
            rows = pl.ds(r, 64)
            mine = pl.ds(mult(f * rows_all + h * half + r, 64), 64)
            total = PO[mine, :].astype(F32)
            for w in (0, 2):
                total = total + ROI[w, rows, :].astype(F32)
            OUTB[rows, :] = (RES[rows, :] + total + vector(B_D)).astype(BF16)

        loop_rows(half, 64, finish)
        kept["res"] = [rc(OUTB.at[block_of(zp)], out_ref.at[z], (f, 2 * zp + h)) for zp in zpeers]
        kept["res_own"] = lc(OUTB.at[block_of(z)], out_ref.at[z])

    q_plane = []
    q_plane.append(
        attention_back(0, ([chain_d[0].third], [chain_d[1].second], [o_plane.relay]))
    )
    q_plane.append(
        attention_back(1, ([p_plane.relay], [chain_u[0].second, chain_d[1].third], []))
    )
    q_plane.append(
        attention_back(2, ([q_plane[0].relay], [finish_out, chain_u[1].second], [chain_u[0].third]))
    )

    def joined(b):
        return jnp.concatenate([DQKV[p, :, b * 128 : (b + 1) * 128] for p in range(pairs)], axis=1)

    PD1[...] = (
        dot_nt(joined(0), WQ[0]) + dot_nt(joined(1), WQ[1]) + dot_nt(joined(2), WQ[2])
    ).astype(BF16)
    d1_sib = rc(PD1.at[oth_rows], RD1, sib)
    zf_d = [chain.fourth() for chain in chain_d]
    d_sib = rc(ZFD.at[h], ZFD.at[h], sib)
    q_plane[1].relay()
    p_plane.wait()
    GP[...] = (
        GPP[krows(f), :].astype(F32) + RGP[0].astype(F32) + RGP[2].astype(F32)
    ).astype(BF16)
    chain_p = Chain(GP, Z1P, ZSP, Z2P, ZFP.at[h])
    chain_p.first()
    d1_sib.wait_recv()

    def ln1_back(r):
        rows = pl.ds(r, 64)
        mine = pl.ds(mult(h * half + r, 64), 64)
        d_h1 = PD1[mine, :].astype(F32) + RD1[rows, :].astype(F32)
        hat, inv = norm_parts(X[mine, :].astype(F32))
        SGP[LN1_S : LN1_S + 1, :] += jnp.sum(d_h1 * hat, 0, keepdims=True)
        SGP[LN1_B : LN1_B + 1, :] += jnp.sum(d_h1, 0, keepdims=True)
        DIN[rows, :] = (DRES[rows, :] + norm_back(d_h1, hat, inv, vector(LN1_S))).astype(BF16)

    loop_rows(half, 64, ln1_back)
    sg_sib = rc(SGP, SGS, sib)

    chain_q = []

    def q_own(b):
        q_plane[b].wait()
        GQF[b] = (
            GQ[b, krows(f), :].astype(F32) + RGQ[b, 0].astype(F32) + RGQ[b, 2].astype(F32)
        ).astype(BF16)
        chain_q.append(Chain(GQF.at[b], Z1Q.at[b], ZSQ.at[b], Z2Q.at[b], ZFQ.at[h, b]))
        chain_q[b].first()

    q_own(0)
    din_in = [rc(DIN.at[block_of(zp)], din_ref.at[z], (f, 2 * zp + h)) for zp in zpeers]
    din_own = lc(DIN.at[block_of(z)], din_ref.at[z])
    chain_u[1].third()
    chain_p.second()
    sg_sib.wait_recv()
    SGB[f] = SGP[...] + SGS[...]
    sgf_in = [rc(SGB.at[f], SGB.at[f], (fp, c)) for fp in fpeers]
    q_plane[2].relay()
    chain_u[0].fourth()
    chain_p.third()
    chain_q[0].second()
    q_own(1)
    chain_u[1].fourth()
    gu_out = [rc(GUZ.at[krows(fp)], ZFU.at[h, f], (fp, c)) for fp in fpeers]
    ZFU[h, f] = GUZ[krows(f), :]
    chain_q[0].third()
    chain_q[1].second()
    for copy in sgf_in:
        copy.wait_recv()
    plane = SGB[0] + SGB[1] + SGB[2] + SGB[3]
    row_id = lax.broadcasted_iota(jnp.int32, plane.shape, 0)
    SGZ[z] = jnp.where(row_id == B_U, SGB[f], plane)
    sgz_in = [rc(SGZ.at[z], SGZ.at[z], (f, 2 * zp + h)) for zp in zpeers]
    zf_p = chain_p.fourth()
    p_sib = rc(zf_p, zf_p, sib)
    q_own(2)
    chain_q[1].third()
    chain_q[2].second()
    d_sib.wait_recv()
    outs = [lc(ZFD.at[k], gd_ref.at[pl.ds(k * hw, hw)]) for k in range(2)]
    p_sib.wait_recv()
    outs += [lc(ZFP.at[k], gp_ref.at[:, pl.ds(k * hw, hw)]) for k in range(2)]
    for copy in gu_out:
        copy.wait_recv()
    u_sib = rc(ZFU.at[h], ZFU.at[h], sib)
    q_sib = []
    for b in range(2):
        zf_q = chain_q[b].fourth()
        q_sib.append(rc(zf_q, zf_q, sib))
    u_sib.wait_recv()
    outs += [
        lc(ZFU.at[k, s], gu_ref.at[:, pl.ds(s * wide + k * hw, hw)]) for k in range(2) for s in range(4)
    ]
    chain_q[2].third()
    for copy in sgz_in:
        copy.wait_recv()
    sg_ref[...] = SGZ[0] + SGZ[1] + SGZ[2] + SGZ[3]
    zf_q = chain_q[2].fourth()
    q_sib.append(rc(zf_q, zf_q, sib))
    for p in range(3):
        q_sib[p].wait_recv()
        outs += [
            lc(
                ZFQ.at[k, p, :, pl.ds(b * 128, 128)],
                gq_ref.at[:, pl.ds(b * wide + k * hw + p * 128, 128)],
            )
            for k in range(2)
            for b in range(3)
        ]
    for copy in kept["res"] + din_in:
        copy.wait_recv()
    for copy in outs + [kept["res_own"], din_own]:
        copy.wait()
    for copy in sent:
        copy.wait_send()


def widen_kernel(
    out_in, din_in, gd_in, gu_in, gp_in, gq_in, sg_hbm,
    out_ref, din_ref, s0, s1, gq_ref, s2, s3, gp_ref, s4, s5, s6, gu_ref, b_up_ref, gd_ref, s7,
    sg_in, LT, LD, LU, LP, LQ, FD, FU, FP, FQ, sems,
):
    f = lax.axis_index("fsdp")
    counts = [0]

    def lc(src, dst):
        copy = pltpu.make_async_copy(src, dst, sems.at[counts[0]])
        counts[0] += 1
        copy.start()
        return copy

    def halves(ref):
        rows = ref.shape[0] // 2
        return [pl.ds(i * rows, rows) for i in range(2)]

    small = lc(sg_hbm, sg_in)
    work = []
    for src, low, wide, dst in (
        (gd_in, LD, FD, gd_ref), (gu_in, LU, FU, gu_ref), (gq_in, LQ, FQ, gq_ref), (gp_in, LP, FP, gp_ref)
    ):
        for part in halves(src):
            work.append((lc(src.at[part], low.at[part]), low.at[part], wide.at[part], dst.at[part]))
    tokens = [lc(out_in, LT.at[0]), lc(din_in, LT.at[1])]
    passed = []
    kr = s0.shape[0]
    small.wait()
    total = sg_in[0:8, 0:kr]
    for j in range(1, 4):
        total = jnp.where(f == j, sg_in[0:8, j * kr : (j + 1) * kr], total)
    for i, ref in enumerate((s0, s1, s2, s3, s4, s5, s6, s7)):
        ref[...] = total[i : i + 1, :].reshape(kr)
    b_up_ref[...] = sg_in[B_U : B_U + 1, :].reshape(sg_in.shape[1])
    for copy, src, dst in zip(tokens, (LT.at[0], LT.at[1]), (out_ref, din_ref)):
        copy.wait()
        passed.append(lc(src, dst))
    for copy, low, wide, dst in work:
        copy.wait()
        wide[...] = low[...].astype(F32)
        passed.append(lc(wide, dst))
    for copy in passed:
        copy.wait()


def fast_device(
    inputs, segments, ln1_scale, ln1_bias, w_qkv, b_query, b_value, w_proj, b_proj,
    ln2_scale, ln2_bias, w_up, b_up, w_down, b_down, cotangent,
):
    micro_count, seq_dev, shard, wide = inputs.shape
    seqs = micro_count * seq_dev
    rows_all = 8 * shard
    half = rows_all // 2
    hw = wide // 2
    kr = wide // 4
    pairs = hw // 128
    heads = 2 * pairs

    def vm(*shape, dtype=BF16):
        return pltpu.VMEM(shape, dtype)

    f32 = functools.partial(vm, dtype=F32)
    tall = 4 * rows_all
    scratch = [
        vm(rows_all, wide), f32(4, 8, 128), f32(8, 8, 128), f32(rows_all, 128),
        vm(tall, wide), vm(tall, wide), f32(4, 8, kr), f32(8, wide),
        vm(3, wide, hw), vm(2, wide, hw), vm(wide, hw), vm(hw, wide),
        vm(rows_all, wide), vm(pairs, rows_all, 128), vm(pairs, rows_all, 128),
        vm(pairs, rows_all, 128), vm(heads, rows_all, rows_all), f32(rows_all, rows_all),
        f32(pairs, rows_all, 128), f32(heads, rows_all, 1), vm(2 * pairs, rows_all, 128),
        f32(half, wide),
        vm(tall, hw), vm(tall, hw),
        vm(tall, wide), vm(4, half, wide), vm(3, half, wide),
        vm(tall, wide), vm(4, half, wide), vm(3, half, wide), vm(half, wide),
        f32(half, wide), vm(2, half, hw), vm(rows_all, hw), vm(2 * pairs, half, 128),
        vm(pairs, rows_all, 128), vm(2, rows_all, 128), f32(2, rows_all, 1),
        vm(pairs, rows_all, hw),
        vm(hw, wide), vm(hw, wide), vm(hw, wide), vm(hw, wide), vm(2, hw, wide),
        vm(wide, hw), vm(wide, hw), vm(wide, hw), vm(wide, hw), vm(wide, hw), vm(2, 4, kr, hw),
        vm(wide, hw), vm(3, kr, hw), vm(kr, hw), vm(kr, hw), vm(kr, hw), vm(kr, hw), vm(2, kr, hw),
        vm(pairs, wide, hw), vm(pairs, 3, kr, hw), vm(pairs, kr, hw), vm(pairs, kr, hw),
        vm(pairs, kr, hw), vm(pairs, kr, hw), vm(2, pairs, kr, hw),
        vm(rows_all, wide), vm(half, wide), vm(half, wide),
        f32(16, wide), f32(16, wide), f32(4, 16, wide), f32(4, 16, wide), f32(1, hw),
        pltpu.SemaphoreType.DMA((176,)), pltpu.SemaphoreType.DMA((176,)),
        pltpu.SemaphoreType.DMA((48,)),
    ]
    hbm = pl.BlockSpec(memory_space=pl.ANY)
    vmem = pl.BlockSpec(memory_space=pltpu.VMEM)
    tokens = jax.ShapeDtypeStruct((seqs, shard, wide), BF16)
    small = jax.ShapeDtypeStruct((16, wide), F32)
    grads = (w_down, w_up, w_proj, w_qkv)
    results = pl.pallas_call(
        layer_kernel,
        out_shape=(tokens, tokens) + tuple(jax.ShapeDtypeStruct(w.shape, BF16) for w in grads) + (small,),
        in_specs=[hbm] + [vmem] * 9 + [hbm] * 4 + [vmem, hbm],
        out_specs=(hbm,) * 6 + (vmem,),
        scratch_shapes=scratch,
        compiler_params=pltpu.CompilerParams(
            collective_id=0, has_side_effects=True, vmem_limit_bytes=62 << 20
        ),
    )(
        inputs.reshape(tokens.shape), segments, ln1_scale, ln1_bias, b_query, b_value, b_proj,
        ln2_scale, ln2_bias, b_down, w_qkv, w_proj, w_up, w_down, b_up, cotangent.reshape(tokens.shape),
    )
    part = jax.ShapeDtypeStruct((kr,), F32)

    def full(w):
        return jax.ShapeDtypeStruct(w.shape, F32)

    out, d_input, *rest = pl.pallas_call(
        widen_kernel,
        out_shape=(
            tokens, tokens, part, part, full(w_qkv), part, part, full(w_proj), part, part, part,
            full(w_up), jax.ShapeDtypeStruct((wide,), F32), full(w_down), part,
        ),
        in_specs=[pl.BlockSpec(memory_space=pltpu.HBM)] * 7,
        out_specs=(hbm, hbm, vmem, vmem, hbm, vmem, vmem, hbm, vmem, vmem, vmem, hbm, vmem, hbm, vmem),
        scratch_shapes=[pltpu.VMEM(small.shape, F32), pltpu.VMEM((2,) + tokens.shape, BF16)]
        + [pltpu.VMEM(w.shape, BF16) for w in grads]
        + [pltpu.VMEM(w.shape, F32) for w in grads]
        + [pltpu.SemaphoreType.DMA((32,))],
        compiler_params=pltpu.CompilerParams(vmem_limit_bytes=62 << 20),
    )(*results)
    return (out.reshape(inputs.shape), d_input.reshape(inputs.shape), *rest)


def fits_fast(mesh, inputs, w_up):
    micro_count, seqs, length, wide = inputs.shape
    return (
        mesh.shape["fsdp"] == 4
        and mesh.shape["ctx"] == 8
        and micro_count * (seqs // 4) == 4
        and length == 512
        and wide == 768
        and w_up.shape == (wide, 4 * wide)
        and HEADS * 64 == wide
    )


def solution(mesh):
    placed = (
        P(None, "fsdp", "ctx", None),
        P(None, "fsdp", "ctx"),
        P("fsdp"),
        P("fsdp"),
        P("fsdp", None),
        P("fsdp"),
        P("fsdp"),
        P("fsdp", None),
        P("fsdp"),
        P("fsdp"),
        P("fsdp"),
        P("fsdp", None),
        P("fsdp"),
        P("fsdp", None),
        P("fsdp"),
        P(None, "fsdp", "ctx", None),
    )
    spread = functools.partial(
        jax.shard_map,
        mesh=mesh,
        in_specs=placed,
        out_specs=(
            P(None, "fsdp", "ctx", None),
            P(None, "fsdp", "ctx", None),
            P("fsdp"),
            P("fsdp"),
            P("fsdp", None),
            P("fsdp"),
            P("fsdp"),
            P("fsdp", None),
            P("fsdp"),
            P("fsdp"),
            P("fsdp"),
            P("fsdp", None),
            P("fsdp"),
            P("fsdp", None),
            P("fsdp"),
        ),
        check_vma=False,
    )

    def layer(*args):
        chosen = fast_device if fits_fast(mesh, args[0], args[11]) else per_device
        return spread(chosen)(*args)

    return layer
```

```python
import functools
import math

import jax
import jax.numpy as jnp
from jax import lax
from jax.experimental import pallas as pl
from jax.experimental.pallas import tpu as pltpu
from jax.sharding import PartitionSpec as P

HEADS = 12


NORM_EPS = 1e-06
SCORE_SCALE = 0.125
MASKED = -1e30


def layer_norm(values, scale_vec, bias_vec):
    center = values - jnp.mean(values, -1, keepdims=True)
    spread = jnp.mean(center * center, -1, keepdims=True)
    return center * lax.rsqrt(spread + NORM_EPS) * scale_vec + bias_vec


def gelu_tanh(values):
    return jax.nn.gelu(values, approximate=True)


def block_size(length_in, step_rows):
    blocked = step_rows
    while blocked * 2 <= 512 and length_in % (blocked * 2) == 0:
        blocked = blocked * 2
    return blocked


def to_heads(array, head_count):
    return array.reshape(array.shape[0], array.shape[1], head_count, -1)


def allowed_mask(seg_query, pos_query, seg_key, pos_key):
    same = seg_query[:, :, None] == seg_key[:, None, :]
    living = (seg_key[:, None, :] >= 0.0) | (pos_query[:, None] == pos_key[None, :])[None]
    return (same & living)[:, :, None, :]


def score_block(query_blk, key_blk, seg_query, pos_query, seg_key, pos_key):
    scores = (
        jnp.einsum("sqhd,skhd->sqhk", query_blk, key_blk, preferred_element_type=jnp.float32)
        * SCORE_SCALE
    )
    return (scores, allowed_mask(seg_query, pos_query, seg_key, pos_key))


def block_grads(
    query_blk,
    dout_blk,
    lse_blk,
    delta_blk,
    seg_query,
    pos_query,
    key_blk,
    value_blk,
    seg_key,
    pos_key,
):
    scores, allowed = score_block(query_blk, key_blk, seg_query, pos_query, seg_key, pos_key)
    probs = jnp.where(allowed, jnp.exp(scores - lse_blk[..., None]), 0.0)
    dprobs = jnp.einsum("sqhd,skhd->sqhk", dout_blk, value_blk, preferred_element_type=jnp.float32)
    dscores = (probs * (dprobs - delta_blk[..., None])).astype(jnp.bfloat16)
    return (dscores, probs.astype(jnp.bfloat16))


def key_side(
    query_blk,
    dout_blk,
    lse_blk,
    delta_blk,
    seg_query,
    pos_query,
    key_blk,
    value_blk,
    seg_key,
    pos_key,
):
    dscores, probs_low = block_grads(
        query_blk,
        dout_blk,
        lse_blk,
        delta_blk,
        seg_query,
        pos_query,
        key_blk,
        value_blk,
        seg_key,
        pos_key,
    )
    key_grad = (
        jnp.einsum("sqhk,sqhd->skhd", dscores, query_blk, preferred_element_type=jnp.float32)
        * SCORE_SCALE
    )
    value_grad = jnp.einsum(
        "sqhk,sqhd->skhd", probs_low, dout_blk, preferred_element_type=jnp.float32
    )
    return (key_grad, value_grad)


def contract_rows(left, right):
    return lax.dot_general(
        left, right, (((0,), (0,)), ((), ())), preferred_element_type=jnp.float32
    )


def contract_cols(left, right):
    return lax.dot_general(
        left, right, (((1,), (1,)), ((), ())), preferred_element_type=jnp.float32
    )


def per_device(
    inputs,
    segments,
    ln1_scale,
    ln1_bias,
    w_qkv,
    b_query,
    b_value,
    w_proj,
    b_proj,
    ln2_scale,
    ln2_bias,
    w_up,
    b_up,
    w_down,
    b_down,
    cotangent,
):
    micro_count, seq_dev, shard_len, model_width = inputs.shape
    head_count = HEADS
    head_width = model_width // head_count
    row_count = seq_dev * shard_len
    place = lax.axis_index("ctx")
    pos_local = place * shard_len + lax.iota(jnp.int32, shard_len)
    owned = (
        ln1_scale,
        ln1_bias,
        w_qkv,
        b_query,
        b_value,
        w_proj,
        b_proj,
        ln2_scale,
        ln2_bias,
        w_up,
        b_up,
        w_down,
        b_down,
    )
    summed_shards = None
    outputs_list = []
    input_grads = []
    for batch_num in range(micro_count):
        gathered = (
            lax.all_gather(owned[0], "fsdp", axis=0, tiled=True),
            lax.all_gather(owned[1], "fsdp", axis=0, tiled=True),
            lax.all_gather(owned[2], "fsdp", axis=0, tiled=True),
            lax.all_gather(owned[3], "fsdp", axis=0, tiled=True),
            lax.all_gather(owned[4], "fsdp", axis=0, tiled=True),
            lax.all_gather(owned[5], "fsdp", axis=0, tiled=True),
            lax.all_gather(owned[6], "fsdp", axis=0, tiled=True),
            lax.all_gather(owned[7], "fsdp", axis=0, tiled=True),
            lax.all_gather(owned[8], "fsdp", axis=0, tiled=True),
            lax.all_gather(owned[9], "fsdp", axis=0, tiled=True),
            lax.all_gather(owned[10], "fsdp", axis=0, tiled=True),
            lax.all_gather(owned[11], "fsdp", axis=0, tiled=True),
            lax.all_gather(owned[12], "fsdp", axis=0, tiled=True),
        )
        (
            gain_one,
            shift_one,
            w_qkv_all,
            bias_query,
            bias_value,
            w_proj_all,
            bias_proj,
            gain_two,
            shift_two,
            w_up_all,
            bias_up,
            w_down_all,
            bias_down,
        ) = gathered
        x_rows = inputs[batch_num].reshape(row_count, model_width).astype(jnp.float32)
        seg_local = segments[batch_num].astype(jnp.float32)
        cot_rows = cotangent[batch_num].reshape(row_count, model_width)
        normed_one, norm_one_pull = jax.vjp(
            layer_norm, x_rows, gain_one.astype(jnp.float32), shift_one.astype(jnp.float32)
        )
        hidden_one = normed_one.astype(jnp.bfloat16)
        projected = jnp.dot(hidden_one, w_qkv_all, preferred_element_type=jnp.float32)
        queries = (projected[:, :model_width] + bias_query.astype(jnp.float32)).astype(jnp.bfloat16)
        keys_loc = projected[:, model_width : 2 * model_width].astype(jnp.bfloat16)
        values_loc = (projected[:, 2 * model_width :] + bias_value.astype(jnp.float32)).astype(
            jnp.bfloat16
        )
        query_heads = queries.reshape(seq_dev, shard_len, head_count, head_width)
        shipped = (
            keys_loc.reshape(seq_dev, shard_len, model_width),
            values_loc.reshape(seq_dev, shard_len, model_width),
            seg_local.astype(jnp.bfloat16),
        )
        stat_shape = (seq_dev, shard_len, head_count)
        start_state = (
            jnp.full(stat_shape, MASKED, jnp.float32),
            jnp.zeros(stat_shape, jnp.float32),
            jnp.zeros((seq_dev, shard_len, head_count, head_width), jnp.float32),
        )
        key_part = lax.all_gather(shipped[0], "ctx", axis=1, tiled=True)
        value_part = lax.all_gather(shipped[1], "ctx", axis=1, tiled=True)
        seg_part = lax.all_gather(shipped[2], "ctx", axis=1, tiled=True)
        length_in = key_part.shape[1]
        step_len = block_size(length_in, shard_len)

        def forward_inner(turn, state):
            row_max, row_sum, weighted = state
            begin = turn * step_len
            key_blk = to_heads(lax.dynamic_slice_in_dim(key_part, begin, step_len, 1), head_count)
            value_blk = to_heads(
                lax.dynamic_slice_in_dim(value_part, begin, step_len, 1), head_count
            )
            seg_blk = lax.dynamic_slice_in_dim(seg_part, begin, step_len, 1).astype(jnp.float32)
            pos_blk = begin + lax.iota(jnp.int32, step_len)
            scores, allowed = score_block(
                query_heads, key_blk, seg_local, pos_local, seg_blk, pos_blk
            )
            scores = jnp.where(allowed, scores, MASKED)
            new_max = jnp.maximum(row_max, jnp.max(scores, -1))
            expo = jnp.where(allowed, jnp.exp(scores - new_max[..., None]), 0.0)
            factor = jnp.exp(row_max - new_max)
            row_sum = row_sum * factor + jnp.sum(expo, -1)
            weighted = weighted * factor[..., None] + jnp.einsum(
                "sqhk,skhd->sqhd",
                expo.astype(jnp.bfloat16),
                value_blk,
                preferred_element_type=jnp.float32,
            )
            return (new_max, row_sum, weighted)

        row_max, row_sum, weighted = lax.fori_loop(
            0, length_in // step_len, forward_inner, start_state
        )
        attended = weighted / row_sum[..., None]
        log_sum = row_max + jnp.log(row_sum)
        mixed = attended.reshape(row_count, model_width).astype(jnp.bfloat16)
        resid = (
            x_rows
            + jnp.dot(mixed, w_proj_all, preferred_element_type=jnp.float32)
            + bias_proj.astype(jnp.float32)
        )
        normed_two, norm_two_pull = jax.vjp(
            layer_norm, resid, gain_two.astype(jnp.float32), shift_two.astype(jnp.float32)
        )
        hidden_two = normed_two.astype(jnp.bfloat16)
        pre_act = jnp.dot(
            hidden_two, w_up_all, preferred_element_type=jnp.float32
        ) + bias_up.astype(jnp.float32)
        activ, gelu_pull = jax.vjp(gelu_tanh, pre_act)
        activ_low = activ.astype(jnp.bfloat16)
        result = (
            resid
            + jnp.dot(activ_low, w_down_all, preferred_element_type=jnp.float32)
            + bias_down.astype(jnp.float32)
        )
        outputs_list.append(result.astype(jnp.bfloat16).reshape(seq_dev, shard_len, model_width))
        d_activ = contract_cols(cot_rows, w_down_all)
        grad_down = contract_rows(activ_low, cot_rows)
        grad_bias_down = jnp.sum(cot_rows.astype(jnp.float32), 0)
        d_pre = gelu_pull(d_activ)[0].astype(jnp.bfloat16)
        grad_up = contract_rows(hidden_two, d_pre)
        grad_bias_up = jnp.sum(d_pre.astype(jnp.float32), 0)
        d_hidden_two = contract_cols(d_pre, w_up_all)
        d_resid_part, grad_gain_two, grad_shift_two = norm_two_pull(d_hidden_two)
        d_resid = cot_rows.astype(jnp.float32) + d_resid_part
        d_branch = d_resid.astype(jnp.bfloat16)
        grad_proj = contract_rows(mixed, d_branch)
        grad_bias_proj = jnp.sum(d_branch.astype(jnp.float32), 0)
        d_mixed = contract_cols(d_branch, w_proj_all).astype(jnp.bfloat16)
        dout_heads = d_mixed.reshape(seq_dev, shard_len, head_count, head_width)
        delta = jnp.sum(dout_heads.astype(jnp.float32) * attended, -1)
        zero_heads = jnp.zeros((seq_dev, shard_len, head_count, head_width), jnp.float32)
        key_all, value_all, seg_all = (
            lax.all_gather(shipped[0], "ctx", axis=1, tiled=True),
            lax.all_gather(shipped[1], "ctx", axis=1, tiled=True),
            lax.all_gather(shipped[2], "ctx", axis=1, tiled=True),
        )
        query_key_part = key_all
        query_value_part = value_all
        query_seg_part = seg_all
        query_length_in = query_key_part.shape[1]
        query_step_len = block_size(query_length_in, shard_len)

        def query_inner(turn, grad_in):
            begin = turn * query_step_len
            key_blk = to_heads(
                lax.dynamic_slice_in_dim(query_key_part, begin, query_step_len, 1), head_count
            )
            value_blk = to_heads(
                lax.dynamic_slice_in_dim(query_value_part, begin, query_step_len, 1), head_count
            )
            seg_blk = lax.dynamic_slice_in_dim(query_seg_part, begin, query_step_len, 1).astype(
                jnp.float32
            )
            pos_blk = 0 + begin + lax.iota(jnp.int32, query_step_len)
            dscores, probs_low = block_grads(
                query_heads,
                dout_heads,
                log_sum,
                delta,
                seg_local,
                pos_local,
                key_blk,
                value_blk,
                seg_blk,
                pos_blk,
            )
            return (
                grad_in
                + jnp.einsum(
                    "sqhk,skhd->sqhd", dscores, key_blk, preferred_element_type=jnp.float32
                )
                * SCORE_SCALE
            )

        query_grad = lax.fori_loop(0, query_length_in // query_step_len, query_inner, zero_heads)
        rows_in = shard_len * lax.axis_size("ctx")
        key_step_len = block_size(rows_in, shard_len)

        def one_block(turn):
            begin = turn * key_step_len
            key_blk = to_heads(
                lax.dynamic_slice_in_dim(key_all, begin, key_step_len, 1), head_count
            )
            value_blk = to_heads(
                lax.dynamic_slice_in_dim(value_all, begin, key_step_len, 1), head_count
            )
            seg_blk = lax.dynamic_slice_in_dim(seg_all, begin, key_step_len, 1).astype(jnp.float32)
            pos_blk = begin + lax.iota(jnp.int32, key_step_len)
            key_grad, value_grad = key_side(
                query_heads,
                dout_heads,
                log_sum,
                delta,
                seg_local,
                pos_local,
                key_blk,
                value_blk,
                seg_blk,
                pos_blk,
            )
            joined = jnp.stack(
                (
                    key_grad.reshape(seq_dev, key_step_len, model_width),
                    value_grad.reshape(seq_dev, key_step_len, model_width),
                ),
                2,
            )
            return joined.transpose(1, 0, 2, 3).reshape(key_step_len, seq_dev * 2 * model_width)

        blocks = lax.map(one_block, jnp.arange(rows_in // key_step_len, dtype=jnp.int32))
        own_terms = lax.psum_scatter(
            blocks.reshape(rows_in, seq_dev * 2 * model_width).astype(jnp.bfloat16),
            "ctx",
            scatter_dimension=0,
            tiled=True,
        ).astype(jnp.float32)
        own_terms = own_terms.reshape(shard_len, seq_dev, 2, model_width).transpose(1, 2, 0, 3)
        key_grad = own_terms[:, 0]
        value_grad = own_terms[:, 1]
        query_low = query_grad.reshape(row_count, model_width).astype(jnp.bfloat16)
        key_low = key_grad.reshape(row_count, model_width).astype(jnp.bfloat16)
        value_low = value_grad.reshape(row_count, model_width).astype(jnp.bfloat16)
        d_qkv = jnp.concatenate((query_low, key_low, value_low), 1)
        grad_qkv = contract_rows(hidden_one, d_qkv)
        grad_bias_query = jnp.sum(query_low.astype(jnp.float32), 0)
        grad_bias_value = jnp.sum(value_low.astype(jnp.float32), 0)
        d_hidden_one = contract_cols(d_qkv, w_qkv_all)
        d_input_part, grad_gain_one, grad_shift_one = norm_one_pull(d_hidden_one)
        input_grads.append(
            (d_resid + d_input_part).astype(jnp.bfloat16).reshape(seq_dev, shard_len, model_width)
        )
        local_grads = (
            grad_gain_one,
            grad_shift_one,
            grad_qkv,
            grad_bias_query,
            grad_bias_value,
            grad_proj,
            grad_bias_proj,
            grad_gain_two,
            grad_shift_two,
            grad_up,
            grad_bias_up,
            grad_down,
            grad_bias_down,
        )
        shard_part = (
            lax.psum_scatter(
                local_grads[0].astype(jnp.bfloat16), "fsdp", scatter_dimension=0, tiled=True
            ).astype(jnp.float32),
            lax.psum_scatter(
                local_grads[1].astype(jnp.bfloat16), "fsdp", scatter_dimension=0, tiled=True
            ).astype(jnp.float32),
            lax.psum_scatter(
                local_grads[2].astype(jnp.bfloat16), "fsdp", scatter_dimension=0, tiled=True
            ).astype(jnp.float32),
            lax.psum_scatter(
                local_grads[3].astype(jnp.bfloat16), "fsdp", scatter_dimension=0, tiled=True
            ).astype(jnp.float32),
            lax.psum_scatter(
                local_grads[4].astype(jnp.bfloat16), "fsdp", scatter_dimension=0, tiled=True
            ).astype(jnp.float32),
            lax.psum_scatter(
                local_grads[5].astype(jnp.bfloat16), "fsdp", scatter_dimension=0, tiled=True
            ).astype(jnp.float32),
            lax.psum_scatter(
                local_grads[6].astype(jnp.bfloat16), "fsdp", scatter_dimension=0, tiled=True
            ).astype(jnp.float32),
            lax.psum_scatter(
                local_grads[7].astype(jnp.bfloat16), "fsdp", scatter_dimension=0, tiled=True
            ).astype(jnp.float32),
            lax.psum_scatter(
                local_grads[8].astype(jnp.bfloat16), "fsdp", scatter_dimension=0, tiled=True
            ).astype(jnp.float32),
            lax.psum_scatter(
                local_grads[9].astype(jnp.bfloat16), "fsdp", scatter_dimension=0, tiled=True
            ).astype(jnp.float32),
            lax.psum_scatter(
                local_grads[10].astype(jnp.bfloat16), "fsdp", scatter_dimension=0, tiled=True
            ).astype(jnp.float32),
            lax.psum_scatter(
                local_grads[11].astype(jnp.bfloat16), "fsdp", scatter_dimension=0, tiled=True
            ).astype(jnp.float32),
            lax.psum_scatter(
                local_grads[12].astype(jnp.bfloat16), "fsdp", scatter_dimension=0, tiled=True
            ).astype(jnp.float32),
        )
        shard_part = (
            lax.psum(shard_part[0].astype(jnp.bfloat16), "ctx").astype(jnp.float32),
            lax.psum(shard_part[1].astype(jnp.bfloat16), "ctx").astype(jnp.float32),
            lax.psum(shard_part[2].astype(jnp.bfloat16), "ctx").astype(jnp.float32),
            lax.psum(shard_part[3].astype(jnp.bfloat16), "ctx").astype(jnp.float32),
            lax.psum(shard_part[4].astype(jnp.bfloat16), "ctx").astype(jnp.float32),
            lax.psum(shard_part[5].astype(jnp.bfloat16), "ctx").astype(jnp.float32),
            lax.psum(shard_part[6].astype(jnp.bfloat16), "ctx").astype(jnp.float32),
            lax.psum(shard_part[7].astype(jnp.bfloat16), "ctx").astype(jnp.float32),
            lax.psum(shard_part[8].astype(jnp.bfloat16), "ctx").astype(jnp.float32),
            lax.psum(shard_part[9].astype(jnp.bfloat16), "ctx").astype(jnp.float32),
            lax.psum(shard_part[10].astype(jnp.bfloat16), "ctx").astype(jnp.float32),
            lax.psum(shard_part[11].astype(jnp.bfloat16), "ctx").astype(jnp.float32),
            lax.psum(shard_part[12].astype(jnp.bfloat16), "ctx").astype(jnp.float32),
        )
        if summed_shards is None:
            summed_shards = shard_part
        else:
            summed_shards = tuple((old + new for old, new in zip(summed_shards, shard_part)))
    return (jnp.stack(outputs_list), jnp.stack(input_grads)) + tuple(summed_shards)


MESH = pl.DeviceIdType.MESH
F32 = jnp.float32
BF16 = jnp.bfloat16
GELU_A = math.sqrt(2.0 / math.pi)
GELU_B = 0.044715
LN1_S, LN1_B, B_Q, B_V, B_P, LN2_S, LN2_B, B_D, B_U, B_U1 = range(10)


def dot_nn(left, right):
    return lax.dot_general(left, right, (((1,), (0,)), ((), ())), preferred_element_type=F32)


def dot_nt(left, right):
    return lax.dot_general(left, right, (((1,), (1,)), ((), ())), preferred_element_type=F32)


def dot_tn(left, right):
    return lax.dot_general(left, right, (((0,), (0,)), ((), ())), preferred_element_type=F32)


def mult(value, factor):
    return pl.multiple_of(value, factor)


def loop_rows(total, step, body):
    def once(turn, carry):
        body(mult(turn * step, step))
        return carry

    lax.fori_loop(0, total // step, once, 0)


def norm_parts(values):
    center = values - jnp.mean(values, -1, keepdims=True)
    spread = jnp.mean(center * center, -1, keepdims=True)
    inv = lax.rsqrt(spread + NORM_EPS)
    return center * inv, inv


def norm_back(d_out, hat, inv, scale):
    d_hat = d_out * scale
    return inv * (
        d_hat - jnp.mean(d_hat, -1, keepdims=True) - hat * jnp.mean(d_hat * hat, -1, keepdims=True)
    )


def layer_kernel(
    inp, seg, v0, v1, v2, v3, v4, v5, v6, v7, wq, wp, wu, wd, bu, cot,
    out_ref, din_ref, gd_ref, gu_ref, gp_ref, gq_ref, sg_ref,
    X, SEGS, SEGR, SEG, COT, H2, PV, VEC, WQ, WP, WU, WD, H1, Q, K, V, E, MB, ATT, LI, MIX, RES,
    ACT, SLOPE, DPRE, PDH, RDH, RDI, PO, RO, ROI, OUTB, DRES, DBR, DBX, DMS, DM, DOS, DLT, DQKV,
    GD, RGD, GDS, Z1D, ZSD, Z2D, ZFD, GU, RGU, GUS, Z1U, ZSU, Z2U, GUZ, ZFU,
    GPP, RGP, GP, Z1P, ZSP, Z2P, ZFP,
    GQ, RGQ, GQF, Z1Q, ZSQ, Z2Q, ZFQ, PD1, RD1, DIN, SGP, SGS, SGT, SGB, SGZ, GBU,
    send_sem, recv_sem, local_sem,
):
    f = lax.axis_index("fsdp")
    c = lax.axis_index("ctx")
    z = c // 2
    h = c % 2
    o = 1 - h
    fx, fy, fd = fpeers = (f + 1 - 2 * (f % 2), (f + 2) % 4, 3 - f)
    px = f % 2
    py = f // 2
    qx = 1 - px
    qy = 1 - py
    zpeers = (z + 1 - 2 * (z % 2), (z + 2) % 4, 3 - z)
    sib = (f, 2 * z + o)
    seq_dev = seg.shape[1]
    shard = inp.shape[1]
    half = 4 * shard
    rows_all = 2 * half
    wide = X.shape[1]
    hw = wide // 2
    kr = wide // 4
    pairs = hw // 128
    own_rows = pl.ds(mult(h * half, half), half)
    oth_rows = pl.ds(mult(o * half, half), half)
    my_block = pl.ds(mult(h * half + z * shard, shard), shard)
    counts = [0, 0]

    def rc_make(src, dst, dev):
        i = counts[0]
        counts[0] += 1
        return pltpu.make_async_remote_copy(
            src_ref=src, dst_ref=dst, send_sem=send_sem.at[i], recv_sem=recv_sem.at[i],
            device_id=dev, device_id_type=MESH,
        )

    sent = []

    def rc(src, dst, dev):
        copy = rc_make(src, dst, dev)
        copy.start()
        sent.append(copy)
        return copy

    def lc(src, dst):
        i = counts[1]
        counts[1] += 1
        copy = pltpu.make_async_copy(src, dst, local_sem.at[i])
        copy.start()
        return copy

    def chunk_rows(j):
        return pl.ds(mult(j * rows_all + h * half, half), half)

    def chunk_other(j):
        return pl.ds(mult(j * rows_all + o * half, half), half)

    def half_rows(j, core, i):
        return pl.ds(mult(j * rows_all + core * half + i * (half // 2), half // 2), half // 2)

    def slot(s):
        return pl.ds(mult(s * hw, hw), hw)

    def cols(start):
        return pl.ds(mult(start, 128), hw)

    def krows(j):
        return pl.ds(mult(j * kr, kr), kr)

    def hrows(j, i):
        return pl.ds(mult(j * kr + i * (kr // 2), kr // 2), kr // 2)

    def block_of(zp):
        return pl.ds(mult(zp * shard, shard), shard)

    class Gather:
        def __init__(self, own, at):
            self.at = at
            self.to_x, self.to_y = {}, {}
            for first, second in ((0, 1), (1, 0)):
                self.to_x[first] = [rc(src, dst, (fx, c)) for src, dst in own(first)]
                self.to_y[second] = [rc(src, dst, (fy, c)) for src, dst in own(second)]

        def relay(self):
            for copy in self.to_x[0]:
                copy.wait_recv()
            self.far_y = rc(self.at(fx, 0), self.at(fx, 0), (fy, c))
            for copy in self.to_y[1]:
                copy.wait_recv()
            self.far_x = rc(self.at(fy, 1), self.at(fy, 1), (fx, c))

        def near(self):
            for copy in self.to_x[1] + self.to_y[0]:
                copy.wait_recv()

        def far(self):
            self.far_y.wait_recv()
            self.far_x.wait_recv()

    class Scatter:
        def __init__(self, part, got, last):
            self.part, self.got, self.last = part, got, last

        def near(self):
            self.a0 = rc(self.part(fx, 0), self.got(0, 0), (fx, c))
            self.b0 = rc(self.part(fy, 1), self.got(0, 1), (fy, c))

        def far(self):
            self.a1 = rc(self.part(fd, 0), self.got(1, 0), (fx, c))
            self.b1 = rc(self.part(fd, 1), self.got(1, 1), (fy, c))

        def relay(self):
            self.a1.wait_recv()
            mine = self.part(fy, 0)
            mine[...] = (mine[...].astype(F32) + self.got(1, 0)[...].astype(F32)).astype(BF16)
            self.a2 = rc(mine, self.last(0), (fy, c))
            self.b1.wait_recv()
            mine = self.part(fx, 1)
            mine[...] = (mine[...].astype(F32) + self.got(1, 1)[...].astype(F32)).astype(BF16)
            self.b2 = rc(mine, self.last(1), (fx, c))

        def wait(self):
            for copy in (self.a0, self.b0, self.a2, self.b2):
                copy.wait_recv()

    class ScatterX:
        def __init__(self, part, got, last):
            self.part, self.got, self.last = part, got, last

        def near(self):
            self.a0 = rc(self.part(fx), self.got(0), (fx, c))

        def far(self):
            self.a1 = rc(self.part(fd), self.got(1), (fx, c))

        def relay(self):
            self.a1.wait_recv()
            mine = self.part(fy)
            mine[...] = (mine[...].astype(F32) + self.got(1)[...].astype(F32)).astype(BF16)
            self.a2 = rc(mine, self.last, (fy, c))

        def wait(self):
            self.a0.wait_recv()
            self.a2.wait_recv()

    inner = (z + 1) // 2 == 1
    outer = jnp.logical_not(inner)
    toward = (f, 2 * zpeers[0] + h)
    across = (f, 2 * zpeers[2] + h)

    class Chain:
        def __init__(self, own, z1, zs, z2, zf):
            self.own, self.z1, self.zs, self.z2, self.zf = own, z1, zs, z2, zf
            self.c1 = rc_make(own, z1, toward)
            self.c2 = rc_make(zs, z2, across)
            self.c3 = rc_make(zf, zf, toward)

        def first(self):
            @pl.when(outer)
            def _():
                self.c1.start()

        def second(self):
            @pl.when(inner)
            def _():
                self.c1.wait_recv()
                self.zs[...] = (self.own[...].astype(F32) + self.z1[...].astype(F32)).astype(BF16)
                self.c2.start()

        def third(self):
            @pl.when(inner)
            def _():
                self.c2.wait_recv()
                self.zf[...] = (self.zs[...].astype(F32) + self.z2[...].astype(F32)).astype(BF16)
                self.c3.start()

        def fourth(self):
            @pl.when(outer)
            def _():
                self.c3.wait_recv()
                self.c1.wait_send()

            @pl.when(inner)
            def _():
                self.c2.wait_send()
                self.c3.wait_send()

            return self.zf

    stacked = jnp.concatenate(
        [v[...].astype(F32).reshape(1, kr) for v in (v0, v1, v2, v3, v4, v5, v6, v7)], axis=0
    )
    up_own = bu[...].astype(F32).reshape(1, wide)
    up_rows = [up_own[:, i * kr : (i + 1) * kr] for i in range(4)]
    PV[f] = jnp.concatenate([stacked] + up_rows + [jnp.zeros((4, kr), F32)], axis=0)
    for s in range(4):
        row = seg[s // seq_dev, s % seq_dev : s % seq_dev + 1, :].astype(F32)
        row = jnp.concatenate([row, jnp.zeros((1, 128 - shard), F32)], axis=1)
        SEGS[s] = jnp.broadcast_to(row, (8, 128))

    barrier = pltpu.get_barrier_semaphore()
    everyone = [(fp, c) for fp in fpeers] + [(f, 2 * zp + h) for zp in zpeers] + [sib]
    for dev in everyone:
        pl.semaphore_signal(barrier, inc=1, device_id=dev, device_id_type=MESH)
    pl.semaphore_wait(barrier, len(everyone))

    def wq_own_part(i):
        return [
            (wq.at[hrows(0, i), cols(b * wide + h * hw)], WQ.at[b, hrows(f, i)]) for b in range(3)
        ]

    pv_in = [rc(PV.at[f], PV.at[f], (fp, c)) for fp in fpeers]
    wq_all = Gather(wq_own_part, lambda j, i: WQ.at[:, hrows(j, i), :])
    my_slot = 4 * h + z
    s_in = [rc(SEGS.at[zp], SEGR.at[my_slot], (f, 2 * zp + h)) for zp in zpeers]
    x_in = [rc(inp.at[zp], X.at[my_block], (f, 2 * zp + h)) for zp in zpeers]
    c_in = [rc(cot.at[zp], COT.at[my_block], (f, 2 * zp + h)) for zp in zpeers]
    x_own = lc(inp.at[z], X.at[my_block])
    wq_own = [lc(wq.at[:, cols(b * wide + h * hw)], WQ.at[b, krows(f)]) for b in range(3)]
    wp_own = lc(wp.at[:, cols(h * hw)], WP.at[h, krows(f)])
    c_own = lc(cot.at[z], COT.at[my_block])
    wd_own = lc(wd.at[slot(h)], WD.at[slot(py)])

    def wu_strips(x_to):
        return [
            (wu.at[:, cols((2 * s + x_to) * wide + h * hw)], WU.at[krows(f), pl.ds(s * hw, hw)])
            for s in range(2)
        ]

    wu_own = [lc(src, dst) for src, dst in wu_strips(px)]
    SEGR[my_slot] = SEGS[z]
    SGP[...] = jnp.zeros_like(SGP)
    GBU[...] = jnp.zeros_like(GBU)
    wq_all.relay()
    wp_all = Gather(
        lambda i: [(wp.at[hrows(0, i), cols(h * hw)], WP.at[h, hrows(f, i)])],
        lambda j, i: WP.at[h, hrows(j, i)],
    )
    zq = z % 2
    pair_z = (f, 2 * zpeers[0] + h)
    wu_x = [
        rc(
            wu.at[hrows(0, zq), cols((2 * s + qx) * wide + h * hw)],
            WU.at[hrows(f, zq), pl.ds(s * hw, hw)],
            (fx, c),
        )
        for s in range(2)
    ]
    wu_y = [rc(src, dst, (fy, c)) for src, dst in wu_strips(px)]

    for copy in pv_in:
        copy.wait_recv()
    VEC[...] = jnp.concatenate([PV[j] for j in range(4)], axis=1)
    up_parts = []
    for s in range(2):
        shard_vec = PV[2 * s + px]
        for i in range(2):
            up_parts.append(jnp.where(h == 0, shard_vec[8 + i : 9 + i], shard_vec[10 + i : 11 + i]))
    bias_up = jnp.concatenate(up_parts, axis=1)

    def vector(i):
        return VEC[i : i + 1, :]

    x_own.wait()
    for copy in s_in + x_in:
        copy.wait_recv()
    my_slots = pl.ds(4 * h, 4)
    s_sib = rc(SEGR.at[my_slots], SEGR.at[my_slots], sib)
    x_sib = rc(X.at[own_rows], X.at[own_rows], sib)

    def ln1(start):
        def block(r):
            rows = pl.ds(mult(start + r, 64), 64)
            hat, _ = norm_parts(X[rows, :].astype(F32))
            H1[rows, :] = (hat * vector(LN1_S) + vector(LN1_B)).astype(BF16)

        loop_rows(half, 64, block)

    ln1(h * half)
    s_sib.wait_recv()
    for b in range(8):
        turned = jnp.transpose(jnp.broadcast_to(SEGR[b][0:1, :], (128, 128)))
        SEG[pl.ds(b * shard, shard), :] = turned[:shard, :]
    seg_row = jnp.transpose(SEG[...])[0:1, :]

    def mask(r):
        rows = pl.ds(r, 128)
        seg_col = SEG[rows, 0:1]
        place_q = r + lax.broadcasted_iota(jnp.int32, (128, rows_all), 0)
        place_k = lax.broadcasted_iota(jnp.int32, (128, rows_all), 1)
        allowed = (seg_col == seg_row) & ((seg_row >= 0.0) | (place_q == place_k))
        MB[rows, :] = jnp.where(allowed, 0.0, MASKED)

    x_sib.wait_recv()
    ln1(o * half)
    loop_rows(rows_all, 128, mask)

    for copy in wq_own:
        copy.wait()
    wp_own.wait()
    wq_all.near()
    wq_all.far()
    wp_all.relay()
    bias_half = [
        jnp.where(h == 0, vector(i)[:, :hw], vector(i)[:, hw:]) for i in (B_Q, B_V)
    ]
    for b, target in ((0, Q), (1, K), (2, V)):
        prod = dot_nn(H1[...], WQ[b])
        if b == 0:
            prod = (prod + bias_half[0]).astype(BF16) * SCORE_SCALE
        if b == 2:
            prod = prod + bias_half[1]
        prod = prod.astype(BF16)
        for p in range(pairs):
            target[p] = prod[:, p * 128 : (p + 1) * 128]
    c_own.wait()
    for copy in c_in:
        copy.wait_recv()
    c_sib = rc(COT.at[own_rows], COT.at[own_rows], sib)
    cot_in = rc(COT.at[own_rows], COT.at[chunk_rows(1)], (fx, c))

    low_half = lax.broadcasted_iota(jnp.int32, (1, 128), 1) < 64

    def pick(s, values):
        keep = low_half if s == 0 else jnp.logical_not(low_half)
        return jnp.where(keep, values, jnp.zeros_like(values))

    mix_out = []
    for p in range(pairs):

        def attend(r, p=p):
            rows = pl.ds(r, 128)
            total = None
            for s in range(2):
                scores = dot_nt(pick(s, Q[p, rows, :]), K[p]) + MB[rows, :]
                top = jnp.max(scores, -1, keepdims=True)
                expo = jnp.exp(scores - top)
                inv = 1.0 / jnp.sum(expo, -1, keepdims=True)
                low = expo.astype(BF16)
                E[2 * p + s, rows, :] = low
                LI[2 * p + s, rows, :] = inv
                part = dot_nn(low, pick(s, V[p])) * inv
                total = part if total is None else total + part
            ATT[p, rows, :] = total
            MIX[pairs * h + p, rows, :] = total.astype(BF16)

        loop_rows(rows_all, 128, attend)
        mix_out.append(rc(MIX.at[pairs * h + p], MIX.at[pairs * h + p], sib))

    for copy in wu_x:
        copy.wait_recv()
    wu_far = rc(WU.at[hrows(fx, zq)], WU.at[hrows(fx, zq)], (fy, c))
    wu_pair = [rc(WU.at[hrows(fx, zq)], WU.at[hrows(fx, zq)], pair_z)]
    wd_in = rc(wd.at[slot(h)], WD.at[slot(py)], (fy, c))

    wp_all.near()
    wp_all.far()
    wp_sib = rc(WP.at[h], WP.at[h], sib)
    for copy in mix_out:
        copy.wait_recv()
    wp_sib.wait_recv()

    def project(r):
        rows = pl.ds(mult(h * half + r, 64), 64)
        mixed = jnp.concatenate([MIX[g, rows, :] for g in range(2 * pairs)], axis=1)
        branch = jnp.concatenate([dot_nn(mixed, WP[k]) for k in range(2)], axis=1)
        resid = X[rows, :].astype(F32) + branch + vector(B_P)
        RES[pl.ds(r, 64), :] = resid
        hat, _ = norm_parts(resid)
        H2[rows, :] = (
            hat * vector(LN2_S) + vector(LN2_B)
        ).astype(BF16)

    loop_rows(half, 64, project)
    h2_in = [
        rc(H2.at[half_rows(0, h, i)], H2.at[half_rows(1, h, i)], (fx, c)) for i in range(2)
    ]
    h2_sib = rc(H2.at[own_rows], H2.at[own_rows], sib)
    wu_far.wait_recv()
    wu_pair.append(rc(WU.at[hrows(fd, zq)], WU.at[hrows(fd, zq)], pair_z))

    def up(start, count):
        def block(r):
            rows = pl.ds(mult(start + r, 128), 128)
            pre = dot_nn(H2[rows, :], WU[...]) + bias_up
            square = pre * pre
            tan = jnp.tanh(GELU_A * pre * (1.0 + GELU_B * square))
            ACT[rows, :] = (0.5 * pre * (1.0 + tan)).astype(BF16)
            SLOPE[rows, :] = 0.5 * (1.0 + tan) + (0.5 * GELU_A) * pre * (1.0 - tan * tan) * (
                1.0 + (3.0 * GELU_B) * square
            )

        loop_rows(count, 128, block)

    def back(start, count):
        def block(r):
            rows = pl.ds(mult(start + r, 128), 128)
            d_pre = (dot_nt(COT[rows, :], WD[...]) * SLOPE[rows, :]).astype(BF16)
            DPRE[rows, :] = d_pre
            GBU[...] += jnp.sum(d_pre.astype(F32), 0, keepdims=True)
            PDH[rows, :] = dot_nt(d_pre, WU[...]).astype(BF16)

        loop_rows(count, 128, block)

    def start_of(j, core, i):
        return j * rows_all + core * half + i * (half // 2)

    class Owned:
        def __init__(self, mine, got, total, copy, z1, zs, z2, zf):
            self.mine, self.got, self.copy, self.total = mine, got, copy, total
            self.chain = Chain(total, z1, zs, z2, zf)
            self.second, self.third, self.fourth = (
                self.chain.second, self.chain.third, self.chain.fourth
            )

        def first(self):
            self.copy.wait_recv()
            self.total[...] = (self.mine[...].astype(F32) + self.got[...].astype(F32)).astype(BF16)
            self.chain.first()

    quarter = hw // 4

    def owned(part_of, got, total, z1, zs, z2, zf):
        made = []
        for i in range(4):
            part = pl.ds(i * quarter, quarter)

            def rows(s, i=i):
                return pl.ds(mult(s * hw + i * quarter, quarter), quarter)

            copy = rc(part_of.at[rows(qy)], got.at[part], (fy, c))
            made.append(
                Owned(
                    part_of.at[rows(py)], got.at[part], total.at[part], copy,
                    z1.at[part], zs.at[part], z2.at[part], zf.at[part],
                )
            )
        return made

    def down(j):
        rows = pl.ds(j * rows_all, rows_all)
        PO[rows, :] = dot_nn(ACT[rows, :], WD[...]).astype(BF16)
        return rc(PO.at[chunk_other(j)], RO.at[j], sib)

    def join(buf, got, j):
        def block(r):
            rows = pl.ds(mult(j * rows_all + h * half + r, 64), 64)
            buf[rows, :] = (buf[rows, :].astype(F32) + got[j, pl.ds(r, 64), :].astype(F32)).astype(BF16)

        loop_rows(half, 64, block)

    for copy in wu_own + [wd_own]:
        copy.wait()
    for copy in wu_y + wu_pair + [c_sib, h2_sib]:
        copy.wait_recv()
    up(0, rows_all)
    cot_in.wait_recv()
    cot_fwd = rc(COT.at[chunk_rows(1)], COT.at[chunk_rows(1)], sib)

    def arrive(i):
        h2_in[i].wait_recv()
        return rc(H2.at[half_rows(1, h, i)], H2.at[half_rows(1, h, i)], sib)

    def partial(i):
        return rc(PDH.at[half_rows(1, o, i)], RDH.at[1, pl.ds(i * (half // 2), half // 2)], sib)

    def pass_on(i, copy):
        copy.wait_recv()
        for r in range(0, half // 2, 64):
            rows = pl.ds(mult(start_of(1, h, i) + r, 64), 64)
            got = RDH[1, i * (half // 2) + r : i * (half // 2) + r + 64, :]
            PDH[rows, :] = (PDH[rows, :].astype(F32) + got.astype(F32)).astype(BF16)
        return rc(PDH.at[half_rows(1, h, i)], RDI.at[pl.ds(i * (half // 2), half // 2)], (fx, c))

    h2_fwd = [arrive(0)]
    up(start_of(1, h, 0), half // 2)
    h2_fwd[0].wait_recv()
    up(start_of(1, o, 0), half // 2)
    cot_fwd.wait_recv()
    wd_in.wait_recv()
    h2_fwd.append(arrive(1))
    back(start_of(1, o, 0), half // 2)
    far_dh = [partial(0)]
    back(start_of(1, h, 0), half // 2)
    h2_fwd[1].wait_recv()
    up(start_of(1, o, 1), half // 2)
    dh_in = [pass_on(0, far_dh[0])]
    up(start_of(1, h, 1), half // 2)
    GD[slot(qy), :] = dot_tn(ACT[:, slot(qy)], COT[...]).astype(BF16)
    chain_d = owned(GD, RGD, GDS, Z1D, ZSD, Z2D, ZFD.at[h])
    back(start_of(1, o, 1), half // 2)
    far_dh.append(partial(1))
    back(start_of(1, h, 1), half // 2)
    dh_in.append(pass_on(1, far_dh[1]))

    GD[slot(py), :] = dot_tn(ACT[:, slot(py)], COT[...]).astype(BF16)
    chain_d[0].first()
    far_o = down(1)
    back(0, rows_all)
    own_dh = rc(PDH.at[oth_rows], RDH.at[0], sib)
    chain_d[1].first()
    far_o.wait_recv()
    join(PO, RO, 1)
    o_in = rc(PO.at[chunk_rows(1)], ROI, (fx, c))
    GU[slot(qy), :] = dot_tn(H2[:, slot(qy)], DPRE[...]).astype(BF16)
    chain_u = owned(GU, RGU, GUS, Z1U, ZSU, Z2U, GUZ)
    chain_z = chain_d + chain_u
    for s in range(2):
        SGP[B_U + s : B_U + s + 1, cols(h * hw)] = GBU[:, s * hw : (s + 1) * hw]
    chain_z[0].second()
    own_dh.wait_recv()


    def ln2_back(r):
        rows = pl.ds(mult(r, 64), 64)
        mine = pl.ds(mult(h * half + r, 64), 64)
        d_h2 = PDH[mine, :].astype(F32) + RDH[0, rows, :].astype(F32) + RDI[rows, :].astype(F32)
        hat, inv = norm_parts(RES[rows, :])
        SGP[LN2_S : LN2_S + 1, :] += jnp.sum(d_h2 * hat, 0, keepdims=True)
        SGP[LN2_B : LN2_B + 1, :] += jnp.sum(d_h2, 0, keepdims=True)
        cot_rows = COT[mine, :].astype(F32)
        SGP[B_D : B_D + 1, :] += jnp.sum(cot_rows, 0, keepdims=True)
        d_resid = cot_rows + norm_back(d_h2, hat, inv, vector(LN2_S))
        DRES[rows, :] = d_resid
        low = d_resid.astype(BF16)
        SGP[B_P : B_P + 1, :] += jnp.sum(low.astype(F32), 0, keepdims=True)
        for k in range(2):
            DBR[k, rows, :] = low[:, k * hw : (k + 1) * hw]
        d_mixed = dot_nt(low[:, :hw], WP[0]) + dot_nt(low[:, hw:], WP[1])
        d_mixed = d_mixed.astype(BF16)
        for g in range(2 * pairs):
            DMS[g, rows, :] = d_mixed[:, g * 128 : (g + 1) * 128]

    for i in range(2):
        dh_in[i].wait_recv()
        loop_rows(half // 2, 64, lambda r, i=i: ln2_back(i * (half // 2) + r))
    dm_sib = rc(DMS.at[pl.ds(pairs * o, pairs)], DM.at[:, own_rows, :], sib)
    dbr_sib = rc(DBR.at[o], DBX.at[own_rows], sib)
    DM[:, own_rows, :] = DMS[pl.ds(pairs * h, pairs)]
    DBX[own_rows, :] = DBR[h]
    chain_z[2].first()
    chain_z[1].second()
    GU[slot(py), :] = dot_tn(H2[:, slot(py)], DPRE[...]).astype(BF16)
    own_o = down(0)
    chain_z[3].first()
    own_o.wait_recv()
    join(PO, RO, 0)
    chain_z[0].third()
    dbr_sib.wait_recv()
    mixed_all = jnp.concatenate([MIX[g] for g in range(2 * pairs)], axis=1)
    GPP[...] = dot_tn(mixed_all, DBX[...]).astype(BF16)
    p_plane = ScatterX(lambda j: GPP.at[krows(j)], lambda w: RGP.at[w], RGP.at[2])
    p_plane.far()
    p_plane.near()
    dm_sib.wait_recv()

    def attention_back(p, steps):
        def prepare(r):
            rows = pl.ds(r, 128)
            d_out = DM[p, rows, :].astype(F32)
            for s in range(2):
                scaled = pick(s, d_out * LI[2 * p + s, rows, :]).astype(BF16)
                DOS[s, rows, :] = scaled
                DLT[s, rows, :] = jnp.sum(scaled.astype(F32) * ATT[p, rows, :], -1, keepdims=True)

        loop_rows(rows_all, 128, prepare)
        d_value = dot_tn(E[2 * p], DOS[0]) + dot_tn(E[2 * p + 1], DOS[1])
        DQKV[p, :, 256:384] = d_value.astype(BF16)
        for step in steps[0]:
            step()

        def block(r):
            rows = pl.ds(r, 128)
            d_query = None
            for s in range(2):
                d_probs = dot_nt(DOS[s, rows, :], V[p])
                d_scores = (
                    E[2 * p + s, rows, :].astype(F32) * (d_probs - DLT[s, rows, :])
                ).astype(BF16)
                E[2 * p + s, rows, :] = d_scores
                part = dot_nn(d_scores, pick(s, K[p]))
                d_query = part if d_query is None else d_query + part
            DQKV[p, rows, 0:128] = (d_query * SCORE_SCALE).astype(BF16)

        loop_rows(rows_all, 128, block)
        for step in steps[1]:
            step()
        d_key = dot_tn(E[2 * p], pick(0, Q[p])) + dot_tn(E[2 * p + 1], pick(1, Q[p]))
        DQKV[p, :, 128:256] = d_key.astype(BF16)
        GQ[p] = dot_tn(H1[...], DQKV[p]).astype(BF16)
        if p < 2:
            plane = ScatterX(
                lambda j: GQ.at[p, krows(j)], lambda w: RGQ.at[p, w], RGQ.at[p, 2]
            )
        else:
            plane = Scatter(
                lambda j, i: GQ.at[p, hrows(j, i)],
                lambda w, i: RGQ.at[p, w, hrows(0, i)],
                lambda i: RGQ.at[p, 2, hrows(0, i)],
            )
        for step in steps[2]:
            step()
        plane.far()
        plane.near()
        here = pl.ds(mult(h * hw + p * 128, 128), 128)
        for b, i in ((0, B_Q), (2, B_V)):
            SGP[i : i + 1, here] = jnp.sum(
                DQKV[p, :, b * 128 : (b + 1) * 128].astype(F32), 0, keepdims=True
            )
        return plane

    kept = {}

    def finish_out():
        o_in.wait_recv()

        def finish(r):
            rows = pl.ds(r, 64)
            mine = pl.ds(mult(h * half + r, 64), 64)
            total = PO[mine, :].astype(F32) + ROI[rows, :].astype(F32)
            OUTB[rows, :] = (RES[rows, :] + total + vector(B_D)).astype(BF16)

        loop_rows(half, 64, finish)
        kept["res_own"] = lc(OUTB.at[block_of(z)], out_ref.at[z])

    def first(i):
        return chain_z[i].first

    def second(i):
        return chain_z[i].second

    def third(i):
        return chain_z[i].third

    kept["res"] = []

    def send_out(i):
        def send():
            zp = zpeers[i]
            kept["res"].append(rc(OUTB.at[block_of(zp)], out_ref.at[z], (f, 2 * zp + h)))

        return send

    q_plane = []
    q_plane.append(
        attention_back(
            0, ([second(2), first(4)], [third(1), second(3)], [first(5), third(2)])
        )
    )
    q_plane.append(
        attention_back(
            1,
            ([second(4), first(6), finish_out, send_out(1)], [third(3), send_out(2)], [second(5), send_out(0)]),
        )
    )
    q_plane.append(
        attention_back(
            2,
            ([first(7), second(6), p_plane.relay], [third(4)], [third(5), q_plane[0].relay]),
        )
    )

    def joined(b):
        return jnp.concatenate([DQKV[p, :, b * 128 : (b + 1) * 128] for p in range(pairs)], axis=1)

    PD1[...] = (
        dot_nt(joined(0), WQ[0]) + dot_nt(joined(1), WQ[1]) + dot_nt(joined(2), WQ[2])
    ).astype(BF16)
    d1_sib = rc(PD1.at[oth_rows], RD1, sib)
    links = []

    def start_chain(mine, z1, zs, z2, zf, pieces):
        rows = kr // pieces
        made = []
        for i in range(pieces):
            part = pl.ds(i * rows, rows)
            made.append(Chain(mine.at[part], z1.at[part], zs.at[part], z2.at[part], zf.at[part]))
            made[i].first()
        links.append((made, zf))

    def own_p():
        p_plane.wait()
        GP[...] = (
            GPP[krows(f), :].astype(F32) + RGP[0].astype(F32) + RGP[2].astype(F32)
        ).astype(BF16)
        start_chain(GP, Z1P, ZSP, Z2P, ZFP.at[h], 1)

    def own_q(b, pieces):
        q_plane[b].wait()
        GQF[b] = (
            GQ[b, krows(f), :].astype(F32) + RGQ[b, 0].astype(F32) + RGQ[b, 2].astype(F32)
        ).astype(BF16)
        start_chain(GQF.at[b], Z1Q.at[b], ZSQ.at[b], Z2Q.at[b], ZFQ.at[h, b], pieces)

    def step_two(i):
        for chain in links[i][0]:
            chain.second()

    def step_three(i):
        for chain in links[i][0]:
            chain.third()

    def step_four(i):
        for chain in links[i][0]:
            chain.fourth()
        return rc(links[i][1], links[i][1], sib)

    second(7)()
    own_p()
    d1_sib.wait_recv()

    def ln1_back(r):
        rows = pl.ds(r, 64)
        mine = pl.ds(mult(h * half + r, 64), 64)
        d_h1 = PD1[mine, :].astype(F32) + RD1[rows, :].astype(F32)
        hat, inv = norm_parts(X[mine, :].astype(F32))
        SGP[LN1_S : LN1_S + 1, :] += jnp.sum(d_h1 * hat, 0, keepdims=True)
        SGP[LN1_B : LN1_B + 1, :] += jnp.sum(d_h1, 0, keepdims=True)
        DIN[rows, :] = (DRES[rows, :] + norm_back(d_h1, hat, inv, vector(LN1_S))).astype(BF16)

    loop_rows(half, 64, ln1_back)
    sg_sib = rc(SGP, SGS, sib)
    third(6)()
    q_plane[1].relay()
    own_q(0, 1)
    step_two(0)
    din_in = [rc(DIN.at[block_of(zp)], din_ref.at[z], (f, 2 * zp + h)) for zp in zpeers]
    din_own = lc(DIN.at[block_of(z)], din_ref.at[z])
    sg_sib.wait_recv()
    small = SGP[...] + SGS[...]
    for j in range(4):
        units = small[B_U + j // 2 : B_U + j // 2 + 1]
        units = jnp.where(px == j % 2, units, jnp.zeros_like(units))
        SGT[j] = jnp.concatenate(
            [small[:8, j * kr : (j + 1) * kr]]
            + [units[:, i * kr : (i + 1) * kr] for i in range(4)]
            + [jnp.zeros((4, kr), F32)],
            axis=0,
        )
    SGB[f] = SGT[f]
    sgf_in = [rc(SGT.at[fp], SGB.at[f], (fp, c)) for fp in fpeers]
    q_plane[2].relay()
    third(7)()
    own_q(1, 1)
    step_two(1)
    step_three(0)
    for chain in chain_d:
        chain.fourth()
    d_sib = rc(ZFD.at[h], ZFD.at[h], sib)
    for copy in sgf_in:
        copy.wait_recv()
    SGZ[z] = SGB[0] + SGB[1] + SGB[2] + SGB[3]
    sgz_in = [rc(SGZ.at[z], SGZ.at[z], (f, 2 * zp + h)) for zp in zpeers]
    own_q(2, 2)
    step_two(2)
    step_three(1)
    for chain in chain_u:
        chain.fourth()
    gu_out = rc(GUZ.at[krows(qx)], ZFU.at[h, px], (fx, c))
    ZFU[h, px] = GUZ[krows(px), :]
    p_sib = step_four(0)
    d_sib.wait_recv()
    outs = [lc(ZFD.at[k], gd_ref.at[pl.ds(k * hw, hw)]) for k in range(2)]
    step_two(3)
    step_three(2)
    q_sib = [step_four(1)]
    for copy in sgz_in:
        copy.wait_recv()
    sg_ref[...] = SGZ[0] + SGZ[1] + SGZ[2] + SGZ[3]
    p_sib.wait_recv()
    outs += [lc(ZFP.at[k], gp_ref.at[:, pl.ds(k * hw, hw)]) for k in range(2)]
    gu_out.wait_recv()
    u_sib = rc(ZFU.at[h], ZFU.at[h], sib)
    step_three(3)
    q_sib.append(step_four(2))
    u_sib.wait_recv()
    outs += [
        lc(
            ZFU.at[k, x_of, :, pl.ds(s * hw, hw)],
            gu_ref.at[:, pl.ds((2 * s + x_of) * wide + k * hw, hw)],
        )
        for k in range(2)
        for s in range(2)
        for x_of in range(2)
    ]
    q_sib.append(step_four(3))
    for p in range(3):
        q_sib[p].wait_recv()
        outs += [
            lc(
                ZFQ.at[k, p, :, pl.ds(b * 128, 128)],
                gq_ref.at[:, pl.ds(b * wide + k * hw + p * 128, 128)],
            )
            for k in range(2)
            for b in range(3)
        ]
    for copy in kept["res"] + din_in:
        copy.wait_recv()
    for copy in outs + [kept["res_own"], din_own]:
        copy.wait()
    for copy in sent:
        copy.wait_send()


def widen_kernel(
    out_in, din_in, gd_in, gu_in, gp_in, gq_in, sg_hbm,
    out_ref, din_ref, s0, s1, gq_ref, s2, s3, gp_ref, s4, s5, s6, gu_ref, b_up_ref, gd_ref, s7,
    sg_in, LT, LD, LU, LP, LQ, FD, FU, FP, FQ, sems,
):
    counts = [0]

    def lc(src, dst):
        copy = pltpu.make_async_copy(src, dst, sems.at[counts[0]])
        counts[0] += 1
        copy.start()
        return copy

    def halves(ref):
        rows = ref.shape[0] // 2
        return [pl.ds(i * rows, rows) for i in range(2)]

    small = lc(sg_hbm, sg_in)
    work = []
    for src, low, wide, dst in (
        (gd_in, LD, FD, gd_ref), (gu_in, LU, FU, gu_ref), (gq_in, LQ, FQ, gq_ref), (gp_in, LP, FP, gp_ref)
    ):
        for part in halves(src):
            work.append((lc(src.at[part], low.at[part]), low.at[part], wide.at[part], dst.at[part]))
    tokens = [lc(out_in, LT.at[0]), lc(din_in, LT.at[1])]
    passed = []
    kr = s0.shape[0]
    small.wait()
    for i, ref in enumerate((s0, s1, s2, s3, s4, s5, s6, s7)):
        ref[...] = sg_in[i : i + 1, :].reshape(kr)
    b_up_ref[...] = jnp.concatenate([sg_in[i : i + 1, :] for i in range(8, 12)], axis=1).reshape(4 * kr)
    for copy, src, dst in zip(tokens, (LT.at[0], LT.at[1]), (out_ref, din_ref)):
        copy.wait()
        passed.append(lc(src, dst))
    for copy, low, wide, dst in work:
        copy.wait()
        wide[...] = low[...].astype(F32)
        passed.append(lc(wide, dst))
    for copy in passed:
        copy.wait()


def fast_device(
    inputs, segments, ln1_scale, ln1_bias, w_qkv, b_query, b_value, w_proj, b_proj,
    ln2_scale, ln2_bias, w_up, b_up, w_down, b_down, cotangent,
):
    micro_count, seq_dev, shard, wide = inputs.shape
    seqs = micro_count * seq_dev
    rows_all = 8 * shard
    half = rows_all // 2
    hw = wide // 2
    kr = wide // 4
    pairs = hw // 128
    heads = 2 * pairs

    def vm(*shape, dtype=BF16):
        return pltpu.VMEM(shape, dtype)

    f32 = functools.partial(vm, dtype=F32)
    pair_rows = 2 * rows_all
    scratch = [
        vm(rows_all, wide), f32(4, 8, 128), f32(8, 8, 128), f32(rows_all, 128),
        vm(pair_rows, wide), vm(pair_rows, wide), f32(4, 16, kr), f32(16, wide),
        vm(3, wide, hw), vm(2, wide, hw), vm(wide, wide), vm(wide, wide),
        vm(rows_all, wide), vm(pairs, rows_all, 128), vm(pairs, rows_all, 128),
        vm(pairs, rows_all, 128), vm(heads, rows_all, rows_all), f32(rows_all, rows_all),
        f32(pairs, rows_all, 128), f32(heads, rows_all, 1), vm(2 * pairs, rows_all, 128),
        f32(half, wide),
        vm(pair_rows, wide), f32(pair_rows, wide), vm(pair_rows, wide),
        vm(pair_rows, wide), vm(2, half, wide), vm(half, wide),
        vm(pair_rows, wide), vm(2, half, wide), vm(half, wide), vm(half, wide),
        f32(half, wide), vm(2, half, hw), vm(rows_all, hw), vm(2 * pairs, half, 128),
        vm(pairs, rows_all, 128), vm(2, rows_all, 128), f32(2, rows_all, 1),
        vm(pairs, rows_all, hw),
        vm(wide, wide), vm(hw, wide), vm(hw, wide), vm(hw, wide), vm(hw, wide), vm(hw, wide),
        vm(2, hw, wide),
        vm(wide, wide), vm(hw, wide), vm(hw, wide), vm(hw, wide), vm(hw, wide), vm(hw, wide),
        vm(hw, wide), vm(2, 2, kr, wide),
        vm(wide, hw), vm(3, kr, hw), vm(kr, hw), vm(kr, hw), vm(kr, hw), vm(kr, hw), vm(2, kr, hw),
        vm(pairs, wide, hw), vm(pairs, 3, kr, hw), vm(pairs, kr, hw), vm(pairs, kr, hw),
        vm(pairs, kr, hw), vm(pairs, kr, hw), vm(2, pairs, kr, hw),
        vm(rows_all, wide), vm(half, wide), vm(half, wide),
        f32(16, wide), f32(16, wide), f32(4, 16, kr), f32(4, 16, kr), f32(4, 16, kr), f32(1, wide),
        pltpu.SemaphoreType.DMA((216,)), pltpu.SemaphoreType.DMA((216,)),
        pltpu.SemaphoreType.DMA((64,)),
    ]
    hbm = pl.BlockSpec(memory_space=pl.ANY)
    vmem = pl.BlockSpec(memory_space=pltpu.VMEM)
    tokens = jax.ShapeDtypeStruct((seqs, shard, wide), BF16)
    small = jax.ShapeDtypeStruct((16, kr), F32)
    grads = (w_down, w_up, w_proj, w_qkv)
    results = pl.pallas_call(
        layer_kernel,
        out_shape=(tokens, tokens) + tuple(jax.ShapeDtypeStruct(w.shape, BF16) for w in grads) + (small,),
        in_specs=[hbm] + [vmem] * 9 + [hbm] * 4 + [vmem, hbm],
        out_specs=(hbm,) * 6 + (vmem,),
        scratch_shapes=scratch,
        compiler_params=pltpu.CompilerParams(
            collective_id=0, has_side_effects=True, vmem_limit_bytes=62 << 20
        ),
    )(
        inputs.reshape(tokens.shape), segments, ln1_scale, ln1_bias, b_query, b_value, b_proj,
        ln2_scale, ln2_bias, b_down, w_qkv, w_proj, w_up, w_down, b_up, cotangent.reshape(tokens.shape),
    )
    part = jax.ShapeDtypeStruct((kr,), F32)

    def full(w):
        return jax.ShapeDtypeStruct(w.shape, F32)

    out, d_input, *rest = pl.pallas_call(
        widen_kernel,
        out_shape=(
            tokens, tokens, part, part, full(w_qkv), part, part, full(w_proj), part, part, part,
            full(w_up), jax.ShapeDtypeStruct((wide,), F32), full(w_down), part,
        ),
        in_specs=[pl.BlockSpec(memory_space=pltpu.HBM)] * 7,
        out_specs=(hbm, hbm, vmem, vmem, hbm, vmem, vmem, hbm, vmem, vmem, vmem, hbm, vmem, hbm, vmem),
        scratch_shapes=[pltpu.VMEM(small.shape, F32), pltpu.VMEM((2,) + tokens.shape, BF16)]
        + [pltpu.VMEM(w.shape, BF16) for w in grads]
        + [pltpu.VMEM(w.shape, F32) for w in grads]
        + [pltpu.SemaphoreType.DMA((32,))],
        compiler_params=pltpu.CompilerParams(vmem_limit_bytes=62 << 20),
    )(*results)
    return (out.reshape(inputs.shape), d_input.reshape(inputs.shape), *rest)


def fits_fast(mesh, inputs, w_up):
    micro_count, seqs, length, wide = inputs.shape
    return (
        mesh.shape["fsdp"] == 4
        and mesh.shape["ctx"] == 8
        and micro_count * (seqs // 4) == 4
        and length == 512
        and wide == 768
        and w_up.shape == (wide, 4 * wide)
        and HEADS * 64 == wide
    )


def solution(mesh):
    placed = (
        P(None, "fsdp", "ctx", None),
        P(None, "fsdp", "ctx"),
        P("fsdp"),
        P("fsdp"),
        P("fsdp", None),
        P("fsdp"),
        P("fsdp"),
        P("fsdp", None),
        P("fsdp"),
        P("fsdp"),
        P("fsdp"),
        P("fsdp", None),
        P("fsdp"),
        P("fsdp", None),
        P("fsdp"),
        P(None, "fsdp", "ctx", None),
    )
    spread = functools.partial(
        jax.shard_map,
        mesh=mesh,
        in_specs=placed,
        out_specs=(
            P(None, "fsdp", "ctx", None),
            P(None, "fsdp", "ctx", None),
            P("fsdp"),
            P("fsdp"),
            P("fsdp", None),
            P("fsdp"),
            P("fsdp"),
            P("fsdp", None),
            P("fsdp"),
            P("fsdp"),
            P("fsdp"),
            P("fsdp", None),
            P("fsdp"),
            P("fsdp", None),
            P("fsdp"),
        ),
        check_vma=False,
    )

    def layer(*args):
        chosen = fast_device if fits_fast(mesh, args[0], args[11]) else per_device
        return spread(chosen)(*args)

    return layer
```

```python
import functools
import math

import jax
import jax.numpy as jnp
from jax import lax
from jax.experimental import pallas as pl
from jax.experimental.pallas import tpu as pltpu
from jax.sharding import PartitionSpec as P

HEADS = 12


NORM_EPS = 1e-06
SCORE_SCALE = 0.125
MASKED = -1e30


def layer_norm(values, scale_vec, bias_vec):
    center = values - jnp.mean(values, -1, keepdims=True)
    spread = jnp.mean(center * center, -1, keepdims=True)
    return center * lax.rsqrt(spread + NORM_EPS) * scale_vec + bias_vec


def gelu_tanh(values):
    return jax.nn.gelu(values, approximate=True)


def block_size(length_in, step_rows):
    blocked = step_rows
    while blocked * 2 <= 512 and length_in % (blocked * 2) == 0:
        blocked = blocked * 2
    return blocked


def to_heads(array, head_count):
    return array.reshape(array.shape[0], array.shape[1], head_count, -1)


def allowed_mask(seg_query, pos_query, seg_key, pos_key):
    same = seg_query[:, :, None] == seg_key[:, None, :]
    living = (seg_key[:, None, :] >= 0.0) | (pos_query[:, None] == pos_key[None, :])[None]
    return (same & living)[:, :, None, :]


def score_block(query_blk, key_blk, seg_query, pos_query, seg_key, pos_key):
    scores = (
        jnp.einsum("sqhd,skhd->sqhk", query_blk, key_blk, preferred_element_type=jnp.float32)
        * SCORE_SCALE
    )
    return (scores, allowed_mask(seg_query, pos_query, seg_key, pos_key))


def block_grads(
    query_blk,
    dout_blk,
    lse_blk,
    delta_blk,
    seg_query,
    pos_query,
    key_blk,
    value_blk,
    seg_key,
    pos_key,
):
    scores, allowed = score_block(query_blk, key_blk, seg_query, pos_query, seg_key, pos_key)
    probs = jnp.where(allowed, jnp.exp(scores - lse_blk[..., None]), 0.0)
    dprobs = jnp.einsum("sqhd,skhd->sqhk", dout_blk, value_blk, preferred_element_type=jnp.float32)
    dscores = (probs * (dprobs - delta_blk[..., None])).astype(jnp.bfloat16)
    return (dscores, probs.astype(jnp.bfloat16))


def key_side(
    query_blk,
    dout_blk,
    lse_blk,
    delta_blk,
    seg_query,
    pos_query,
    key_blk,
    value_blk,
    seg_key,
    pos_key,
):
    dscores, probs_low = block_grads(
        query_blk,
        dout_blk,
        lse_blk,
        delta_blk,
        seg_query,
        pos_query,
        key_blk,
        value_blk,
        seg_key,
        pos_key,
    )
    key_grad = (
        jnp.einsum("sqhk,sqhd->skhd", dscores, query_blk, preferred_element_type=jnp.float32)
        * SCORE_SCALE
    )
    value_grad = jnp.einsum(
        "sqhk,sqhd->skhd", probs_low, dout_blk, preferred_element_type=jnp.float32
    )
    return (key_grad, value_grad)


def contract_rows(left, right):
    return lax.dot_general(
        left, right, (((0,), (0,)), ((), ())), preferred_element_type=jnp.float32
    )


def contract_cols(left, right):
    return lax.dot_general(
        left, right, (((1,), (1,)), ((), ())), preferred_element_type=jnp.float32
    )


def per_device(
    inputs,
    segments,
    ln1_scale,
    ln1_bias,
    w_qkv,
    b_query,
    b_value,
    w_proj,
    b_proj,
    ln2_scale,
    ln2_bias,
    w_up,
    b_up,
    w_down,
    b_down,
    cotangent,
):
    micro_count, seq_dev, shard_len, model_width = inputs.shape
    head_count = HEADS
    head_width = model_width // head_count
    row_count = seq_dev * shard_len
    place = lax.axis_index("ctx")
    pos_local = place * shard_len + lax.iota(jnp.int32, shard_len)
    owned = (
        ln1_scale,
        ln1_bias,
        w_qkv,
        b_query,
        b_value,
        w_proj,
        b_proj,
        ln2_scale,
        ln2_bias,
        w_up,
        b_up,
        w_down,
        b_down,
    )
    summed_shards = None
    outputs_list = []
    input_grads = []
    for batch_num in range(micro_count):
        gathered = (
            lax.all_gather(owned[0], "fsdp", axis=0, tiled=True),
            lax.all_gather(owned[1], "fsdp", axis=0, tiled=True),
            lax.all_gather(owned[2], "fsdp", axis=0, tiled=True),
            lax.all_gather(owned[3], "fsdp", axis=0, tiled=True),
            lax.all_gather(owned[4], "fsdp", axis=0, tiled=True),
            lax.all_gather(owned[5], "fsdp", axis=0, tiled=True),
            lax.all_gather(owned[6], "fsdp", axis=0, tiled=True),
            lax.all_gather(owned[7], "fsdp", axis=0, tiled=True),
            lax.all_gather(owned[8], "fsdp", axis=0, tiled=True),
            lax.all_gather(owned[9], "fsdp", axis=0, tiled=True),
            lax.all_gather(owned[10], "fsdp", axis=0, tiled=True),
            lax.all_gather(owned[11], "fsdp", axis=0, tiled=True),
            lax.all_gather(owned[12], "fsdp", axis=0, tiled=True),
        )
        (
            gain_one,
            shift_one,
            w_qkv_all,
            bias_query,
            bias_value,
            w_proj_all,
            bias_proj,
            gain_two,
            shift_two,
            w_up_all,
            bias_up,
            w_down_all,
            bias_down,
        ) = gathered
        x_rows = inputs[batch_num].reshape(row_count, model_width).astype(jnp.float32)
        seg_local = segments[batch_num].astype(jnp.float32)
        cot_rows = cotangent[batch_num].reshape(row_count, model_width)
        normed_one, norm_one_pull = jax.vjp(
            layer_norm, x_rows, gain_one.astype(jnp.float32), shift_one.astype(jnp.float32)
        )
        hidden_one = normed_one.astype(jnp.bfloat16)
        projected = jnp.dot(hidden_one, w_qkv_all, preferred_element_type=jnp.float32)
        queries = (projected[:, :model_width] + bias_query.astype(jnp.float32)).astype(jnp.bfloat16)
        keys_loc = projected[:, model_width : 2 * model_width].astype(jnp.bfloat16)
        values_loc = (projected[:, 2 * model_width :] + bias_value.astype(jnp.float32)).astype(
            jnp.bfloat16
        )
        query_heads = queries.reshape(seq_dev, shard_len, head_count, head_width)
        shipped = (
            keys_loc.reshape(seq_dev, shard_len, model_width),
            values_loc.reshape(seq_dev, shard_len, model_width),
            seg_local.astype(jnp.bfloat16),
        )
        stat_shape = (seq_dev, shard_len, head_count)
        start_state = (
            jnp.full(stat_shape, MASKED, jnp.float32),
            jnp.zeros(stat_shape, jnp.float32),
            jnp.zeros((seq_dev, shard_len, head_count, head_width), jnp.float32),
        )
        key_part = lax.all_gather(shipped[0], "ctx", axis=1, tiled=True)
        value_part = lax.all_gather(shipped[1], "ctx", axis=1, tiled=True)
        seg_part = lax.all_gather(shipped[2], "ctx", axis=1, tiled=True)
        length_in = key_part.shape[1]
        step_len = block_size(length_in, shard_len)

        def forward_inner(turn, state):
            row_max, row_sum, weighted = state
            begin = turn * step_len
            key_blk = to_heads(lax.dynamic_slice_in_dim(key_part, begin, step_len, 1), head_count)
            value_blk = to_heads(
                lax.dynamic_slice_in_dim(value_part, begin, step_len, 1), head_count
            )
            seg_blk = lax.dynamic_slice_in_dim(seg_part, begin, step_len, 1).astype(jnp.float32)
            pos_blk = begin + lax.iota(jnp.int32, step_len)
            scores, allowed = score_block(
                query_heads, key_blk, seg_local, pos_local, seg_blk, pos_blk
            )
            scores = jnp.where(allowed, scores, MASKED)
            new_max = jnp.maximum(row_max, jnp.max(scores, -1))
            expo = jnp.where(allowed, jnp.exp(scores - new_max[..., None]), 0.0)
            factor = jnp.exp(row_max - new_max)
            row_sum = row_sum * factor + jnp.sum(expo, -1)
            weighted = weighted * factor[..., None] + jnp.einsum(
                "sqhk,skhd->sqhd",
                expo.astype(jnp.bfloat16),
                value_blk,
                preferred_element_type=jnp.float32,
            )
            return (new_max, row_sum, weighted)

        row_max, row_sum, weighted = lax.fori_loop(
            0, length_in // step_len, forward_inner, start_state
        )
        attended = weighted / row_sum[..., None]
        log_sum = row_max + jnp.log(row_sum)
        mixed = attended.reshape(row_count, model_width).astype(jnp.bfloat16)
        resid = (
            x_rows
            + jnp.dot(mixed, w_proj_all, preferred_element_type=jnp.float32)
            + bias_proj.astype(jnp.float32)
        )
        normed_two, norm_two_pull = jax.vjp(
            layer_norm, resid, gain_two.astype(jnp.float32), shift_two.astype(jnp.float32)
        )
        hidden_two = normed_two.astype(jnp.bfloat16)
        pre_act = jnp.dot(
            hidden_two, w_up_all, preferred_element_type=jnp.float32
        ) + bias_up.astype(jnp.float32)
        activ, gelu_pull = jax.vjp(gelu_tanh, pre_act)
        activ_low = activ.astype(jnp.bfloat16)
        result = (
            resid
            + jnp.dot(activ_low, w_down_all, preferred_element_type=jnp.float32)
            + bias_down.astype(jnp.float32)
        )
        outputs_list.append(result.astype(jnp.bfloat16).reshape(seq_dev, shard_len, model_width))
        d_activ = contract_cols(cot_rows, w_down_all)
        grad_down = contract_rows(activ_low, cot_rows)
        grad_bias_down = jnp.sum(cot_rows.astype(jnp.float32), 0)
        d_pre = gelu_pull(d_activ)[0].astype(jnp.bfloat16)
        grad_up = contract_rows(hidden_two, d_pre)
        grad_bias_up = jnp.sum(d_pre.astype(jnp.float32), 0)
        d_hidden_two = contract_cols(d_pre, w_up_all)
        d_resid_part, grad_gain_two, grad_shift_two = norm_two_pull(d_hidden_two)
        d_resid = cot_rows.astype(jnp.float32) + d_resid_part
        d_branch = d_resid.astype(jnp.bfloat16)
        grad_proj = contract_rows(mixed, d_branch)
        grad_bias_proj = jnp.sum(d_branch.astype(jnp.float32), 0)
        d_mixed = contract_cols(d_branch, w_proj_all).astype(jnp.bfloat16)
        dout_heads = d_mixed.reshape(seq_dev, shard_len, head_count, head_width)
        delta = jnp.sum(dout_heads.astype(jnp.float32) * attended, -1)
        zero_heads = jnp.zeros((seq_dev, shard_len, head_count, head_width), jnp.float32)
        key_all, value_all, seg_all = (
            lax.all_gather(shipped[0], "ctx", axis=1, tiled=True),
            lax.all_gather(shipped[1], "ctx", axis=1, tiled=True),
            lax.all_gather(shipped[2], "ctx", axis=1, tiled=True),
        )
        query_key_part = key_all
        query_value_part = value_all
        query_seg_part = seg_all
        query_length_in = query_key_part.shape[1]
        query_step_len = block_size(query_length_in, shard_len)

        def query_inner(turn, grad_in):
            begin = turn * query_step_len
            key_blk = to_heads(
                lax.dynamic_slice_in_dim(query_key_part, begin, query_step_len, 1), head_count
            )
            value_blk = to_heads(
                lax.dynamic_slice_in_dim(query_value_part, begin, query_step_len, 1), head_count
            )
            seg_blk = lax.dynamic_slice_in_dim(query_seg_part, begin, query_step_len, 1).astype(
                jnp.float32
            )
            pos_blk = 0 + begin + lax.iota(jnp.int32, query_step_len)
            dscores, probs_low = block_grads(
                query_heads,
                dout_heads,
                log_sum,
                delta,
                seg_local,
                pos_local,
                key_blk,
                value_blk,
                seg_blk,
                pos_blk,
            )
            return (
                grad_in
                + jnp.einsum(
                    "sqhk,skhd->sqhd", dscores, key_blk, preferred_element_type=jnp.float32
                )
                * SCORE_SCALE
            )

        query_grad = lax.fori_loop(0, query_length_in // query_step_len, query_inner, zero_heads)
        rows_in = shard_len * lax.axis_size("ctx")
        key_step_len = block_size(rows_in, shard_len)

        def one_block(turn):
            begin = turn * key_step_len
            key_blk = to_heads(
                lax.dynamic_slice_in_dim(key_all, begin, key_step_len, 1), head_count
            )
            value_blk = to_heads(
                lax.dynamic_slice_in_dim(value_all, begin, key_step_len, 1), head_count
            )
            seg_blk = lax.dynamic_slice_in_dim(seg_all, begin, key_step_len, 1).astype(jnp.float32)
            pos_blk = begin + lax.iota(jnp.int32, key_step_len)
            key_grad, value_grad = key_side(
                query_heads,
                dout_heads,
                log_sum,
                delta,
                seg_local,
                pos_local,
                key_blk,
                value_blk,
                seg_blk,
                pos_blk,
            )
            joined = jnp.stack(
                (
                    key_grad.reshape(seq_dev, key_step_len, model_width),
                    value_grad.reshape(seq_dev, key_step_len, model_width),
                ),
                2,
            )
            return joined.transpose(1, 0, 2, 3).reshape(key_step_len, seq_dev * 2 * model_width)

        blocks = lax.map(one_block, jnp.arange(rows_in // key_step_len, dtype=jnp.int32))
        own_terms = lax.psum_scatter(
            blocks.reshape(rows_in, seq_dev * 2 * model_width).astype(jnp.bfloat16),
            "ctx",
            scatter_dimension=0,
            tiled=True,
        ).astype(jnp.float32)
        own_terms = own_terms.reshape(shard_len, seq_dev, 2, model_width).transpose(1, 2, 0, 3)
        key_grad = own_terms[:, 0]
        value_grad = own_terms[:, 1]
        query_low = query_grad.reshape(row_count, model_width).astype(jnp.bfloat16)
        key_low = key_grad.reshape(row_count, model_width).astype(jnp.bfloat16)
        value_low = value_grad.reshape(row_count, model_width).astype(jnp.bfloat16)
        d_qkv = jnp.concatenate((query_low, key_low, value_low), 1)
        grad_qkv = contract_rows(hidden_one, d_qkv)
        grad_bias_query = jnp.sum(query_low.astype(jnp.float32), 0)
        grad_bias_value = jnp.sum(value_low.astype(jnp.float32), 0)
        d_hidden_one = contract_cols(d_qkv, w_qkv_all)
        d_input_part, grad_gain_one, grad_shift_one = norm_one_pull(d_hidden_one)
        input_grads.append(
            (d_resid + d_input_part).astype(jnp.bfloat16).reshape(seq_dev, shard_len, model_width)
        )
        local_grads = (
            grad_gain_one,
            grad_shift_one,
            grad_qkv,
            grad_bias_query,
            grad_bias_value,
            grad_proj,
            grad_bias_proj,
            grad_gain_two,
            grad_shift_two,
            grad_up,
            grad_bias_up,
            grad_down,
            grad_bias_down,
        )
        shard_part = (
            lax.psum_scatter(
                local_grads[0].astype(jnp.bfloat16), "fsdp", scatter_dimension=0, tiled=True
            ).astype(jnp.float32),
            lax.psum_scatter(
                local_grads[1].astype(jnp.bfloat16), "fsdp", scatter_dimension=0, tiled=True
            ).astype(jnp.float32),
            lax.psum_scatter(
                local_grads[2].astype(jnp.bfloat16), "fsdp", scatter_dimension=0, tiled=True
            ).astype(jnp.float32),
            lax.psum_scatter(
                local_grads[3].astype(jnp.bfloat16), "fsdp", scatter_dimension=0, tiled=True
            ).astype(jnp.float32),
            lax.psum_scatter(
                local_grads[4].astype(jnp.bfloat16), "fsdp", scatter_dimension=0, tiled=True
            ).astype(jnp.float32),
            lax.psum_scatter(
                local_grads[5].astype(jnp.bfloat16), "fsdp", scatter_dimension=0, tiled=True
            ).astype(jnp.float32),
            lax.psum_scatter(
                local_grads[6].astype(jnp.bfloat16), "fsdp", scatter_dimension=0, tiled=True
            ).astype(jnp.float32),
            lax.psum_scatter(
                local_grads[7].astype(jnp.bfloat16), "fsdp", scatter_dimension=0, tiled=True
            ).astype(jnp.float32),
            lax.psum_scatter(
                local_grads[8].astype(jnp.bfloat16), "fsdp", scatter_dimension=0, tiled=True
            ).astype(jnp.float32),
            lax.psum_scatter(
                local_grads[9].astype(jnp.bfloat16), "fsdp", scatter_dimension=0, tiled=True
            ).astype(jnp.float32),
            lax.psum_scatter(
                local_grads[10].astype(jnp.bfloat16), "fsdp", scatter_dimension=0, tiled=True
            ).astype(jnp.float32),
            lax.psum_scatter(
                local_grads[11].astype(jnp.bfloat16), "fsdp", scatter_dimension=0, tiled=True
            ).astype(jnp.float32),
            lax.psum_scatter(
                local_grads[12].astype(jnp.bfloat16), "fsdp", scatter_dimension=0, tiled=True
            ).astype(jnp.float32),
        )
        shard_part = (
            lax.psum(shard_part[0].astype(jnp.bfloat16), "ctx").astype(jnp.float32),
            lax.psum(shard_part[1].astype(jnp.bfloat16), "ctx").astype(jnp.float32),
            lax.psum(shard_part[2].astype(jnp.bfloat16), "ctx").astype(jnp.float32),
            lax.psum(shard_part[3].astype(jnp.bfloat16), "ctx").astype(jnp.float32),
            lax.psum(shard_part[4].astype(jnp.bfloat16), "ctx").astype(jnp.float32),
            lax.psum(shard_part[5].astype(jnp.bfloat16), "ctx").astype(jnp.float32),
            lax.psum(shard_part[6].astype(jnp.bfloat16), "ctx").astype(jnp.float32),
            lax.psum(shard_part[7].astype(jnp.bfloat16), "ctx").astype(jnp.float32),
            lax.psum(shard_part[8].astype(jnp.bfloat16), "ctx").astype(jnp.float32),
            lax.psum(shard_part[9].astype(jnp.bfloat16), "ctx").astype(jnp.float32),
            lax.psum(shard_part[10].astype(jnp.bfloat16), "ctx").astype(jnp.float32),
            lax.psum(shard_part[11].astype(jnp.bfloat16), "ctx").astype(jnp.float32),
            lax.psum(shard_part[12].astype(jnp.bfloat16), "ctx").astype(jnp.float32),
        )
        if summed_shards is None:
            summed_shards = shard_part
        else:
            summed_shards = tuple((old + new for old, new in zip(summed_shards, shard_part)))
    return (jnp.stack(outputs_list), jnp.stack(input_grads)) + tuple(summed_shards)


MESH = pl.DeviceIdType.MESH
F32 = jnp.float32
BF16 = jnp.bfloat16
GELU_A = math.sqrt(2.0 / math.pi)
GELU_B = 0.044715
LN1_S, LN1_B, B_Q, B_V, B_P, LN2_S, LN2_B, B_D, B_U, B_U1 = range(10)


def dot_nn(left, right):
    return lax.dot_general(left, right, (((1,), (0,)), ((), ())), preferred_element_type=F32)


def dot_nt(left, right):
    return lax.dot_general(left, right, (((1,), (1,)), ((), ())), preferred_element_type=F32)


def dot_tn(left, right):
    return lax.dot_general(left, right, (((0,), (0,)), ((), ())), preferred_element_type=F32)


def mult(value, factor):
    return pl.multiple_of(value, factor)


def loop_rows(total, step, body):
    def once(turn, carry):
        body(mult(turn * step, step))
        return carry

    lax.fori_loop(0, total // step, once, 0)


def norm_parts(values):
    center = values - jnp.mean(values, -1, keepdims=True)
    spread = jnp.mean(center * center, -1, keepdims=True)
    inv = lax.rsqrt(spread + NORM_EPS)
    return center * inv, inv


def norm_back(d_out, hat, inv, scale):
    d_hat = d_out * scale
    return inv * (
        d_hat - jnp.mean(d_hat, -1, keepdims=True) - hat * jnp.mean(d_hat * hat, -1, keepdims=True)
    )


def layer_kernel(
    inp, seg, v0, v1, v2, v3, v4, v5, v6, v7, wq, wp, wu, wd, bu, cot,
    out_ref, din_ref, gd_ref, gu_ref, gp_ref, gq_ref, sg_ref,
    X, SEGS, SEGR, SEG, COT, H2, PV, VEC, WQ, WP, WU, WD, H1, Q, K, V, E, MB, ATT, LI, MIX, RES,
    ACT, SLOPE, DPRE, PDH, RDH, RDI, PO, RO, ROI, OUTB, DRES, DBR, DBX, DMS, DM, DOS, DLT, DQKV,
    GD, RGD, GDS, Z1D, ZSD, Z2D, ZFD, GU, RGU, GUS, Z1U, ZSU, Z2U, GUZ, ZFU,
    GPP, RGP, GP, Z1P, ZSP, Z2P, ZFP,
    GQ, RGQ, GQF, Z1Q, ZSQ, Z2Q, ZFQ, PD1, RD1, DIN, SGP, SGS, SGT, SGB, SGZ, GBU,
    send_sem, recv_sem, local_sem,
):
    f = lax.axis_index("fsdp")
    c = lax.axis_index("ctx")
    z = c // 2
    h = c % 2
    o = 1 - h
    fx, fy, fd = fpeers = (f + 1 - 2 * (f % 2), (f + 2) % 4, 3 - f)
    px = f % 2
    py = f // 2
    qx = 1 - px
    qy = 1 - py
    zpeers = (z + 1 - 2 * (z % 2), (z + 2) % 4, 3 - z)
    sib = (f, 2 * z + o)
    seq_dev = seg.shape[1]
    shard = inp.shape[1]
    half = 4 * shard
    rows_all = 2 * half
    wide = X.shape[1]
    hw = wide // 2
    kr = wide // 4
    pairs = hw // 128
    own_rows = pl.ds(mult(h * half, half), half)
    oth_rows = pl.ds(mult(o * half, half), half)
    my_block = pl.ds(mult(h * half + z * shard, shard), shard)
    counts = [0, 0]

    def rc_make(src, dst, dev):
        i = counts[0]
        counts[0] += 1
        return pltpu.make_async_remote_copy(
            src_ref=src, dst_ref=dst, send_sem=send_sem.at[i], recv_sem=recv_sem.at[i],
            device_id=dev, device_id_type=MESH,
        )

    sent = []

    def rc(src, dst, dev):
        copy = rc_make(src, dst, dev)
        copy.start()
        sent.append(copy)
        return copy

    def lc(src, dst):
        i = counts[1]
        counts[1] += 1
        copy = pltpu.make_async_copy(src, dst, local_sem.at[i])
        copy.start()
        return copy

    def chunk_rows(j):
        return pl.ds(mult(j * rows_all + h * half, half), half)

    def chunk_other(j):
        return pl.ds(mult(j * rows_all + o * half, half), half)

    def half_rows(j, core, i):
        return pl.ds(mult(j * rows_all + core * half + i * (half // 2), half // 2), half // 2)

    def slot(s):
        return pl.ds(mult(s * hw, hw), hw)

    def cols(start):
        return pl.ds(mult(start, 128), hw)

    def krows(j):
        return pl.ds(mult(j * kr, kr), kr)

    def hrows(j, i):
        return pl.ds(mult(j * kr + i * (kr // 2), kr // 2), kr // 2)

    def block_of(zp):
        return pl.ds(mult(zp * shard, shard), shard)

    class Gather:
        def __init__(self, own, at):
            self.at = at
            self.to_x, self.to_y = {}, {}
            for first, second in ((0, 1), (1, 0)):
                self.to_x[first] = [rc(src, dst, (fx, c)) for src, dst in own(first)]
                self.to_y[second] = [rc(src, dst, (fy, c)) for src, dst in own(second)]

        def relay(self):
            for copy in self.to_x[0]:
                copy.wait_recv()
            self.far_y = rc(self.at(fx, 0), self.at(fx, 0), (fy, c))
            for copy in self.to_y[1]:
                copy.wait_recv()
            self.far_x = rc(self.at(fy, 1), self.at(fy, 1), (fx, c))

        def near(self):
            for copy in self.to_x[1] + self.to_y[0]:
                copy.wait_recv()

        def far(self):
            self.far_y.wait_recv()
            self.far_x.wait_recv()

    class Scatter:
        def __init__(self, part, got, last):
            self.part, self.got, self.last = part, got, last

        def near(self):
            self.a0 = rc(self.part(fx, 0), self.got(0, 0), (fx, c))
            self.b0 = rc(self.part(fy, 1), self.got(0, 1), (fy, c))

        def far(self):
            self.a1 = rc(self.part(fd, 0), self.got(1, 0), (fx, c))
            self.b1 = rc(self.part(fd, 1), self.got(1, 1), (fy, c))

        def relay(self):
            self.a1.wait_recv()
            mine = self.part(fy, 0)
            mine[...] = (mine[...].astype(F32) + self.got(1, 0)[...].astype(F32)).astype(BF16)
            self.a2 = rc(mine, self.last(0), (fy, c))
            self.b1.wait_recv()
            mine = self.part(fx, 1)
            mine[...] = (mine[...].astype(F32) + self.got(1, 1)[...].astype(F32)).astype(BF16)
            self.b2 = rc(mine, self.last(1), (fx, c))

        def wait(self):
            for copy in (self.a0, self.b0, self.a2, self.b2):
                copy.wait_recv()

    class ScatterX:
        def __init__(self, part, got, last):
            self.part, self.got, self.last = part, got, last

        def near(self):
            self.a0 = rc(self.part(fx), self.got(0), (fx, c))

        def far(self):
            self.a1 = rc(self.part(fd), self.got(1), (fx, c))

        def relay(self):
            self.a1.wait_recv()
            mine = self.part(fy)
            mine[...] = (mine[...].astype(F32) + self.got(1)[...].astype(F32)).astype(BF16)
            self.a2 = rc(mine, self.last, (fy, c))

        def wait(self):
            self.a0.wait_recv()
            self.a2.wait_recv()

    inner = (z + 1) // 2 == 1
    outer = jnp.logical_not(inner)
    toward = (f, 2 * zpeers[0] + h)
    across = (f, 2 * zpeers[2] + h)

    class Chain:
        def __init__(self, own, z1, zs, z2, zf):
            self.own, self.z1, self.zs, self.z2, self.zf = own, z1, zs, z2, zf
            self.c1 = rc_make(own, z1, toward)
            self.c2 = rc_make(zs, z2, across)
            self.c3 = rc_make(zf, zf, toward)

        def first(self):
            @pl.when(outer)
            def _():
                self.c1.start()

        def second(self):
            @pl.when(inner)
            def _():
                self.c1.wait_recv()
                self.zs[...] = (self.own[...].astype(F32) + self.z1[...].astype(F32)).astype(BF16)
                self.c2.start()

        def third(self):
            @pl.when(inner)
            def _():
                self.c2.wait_recv()
                self.zf[...] = (self.zs[...].astype(F32) + self.z2[...].astype(F32)).astype(BF16)
                self.c3.start()

        def fourth(self):
            @pl.when(outer)
            def _():
                self.c3.wait_recv()
                self.c1.wait_send()

            @pl.when(inner)
            def _():
                self.c2.wait_send()
                self.c3.wait_send()

            return self.zf

    stacked = jnp.concatenate(
        [v[...].astype(F32).reshape(1, kr) for v in (v0, v1, v2, v3, v4, v5, v6, v7)], axis=0
    )
    up_own = bu[...].astype(F32).reshape(1, wide)
    up_rows = [up_own[:, i * kr : (i + 1) * kr] for i in range(4)]
    PV[f] = jnp.concatenate([stacked] + up_rows + [jnp.zeros((4, kr), F32)], axis=0)
    for s in range(4):
        row = seg[s // seq_dev, s % seq_dev : s % seq_dev + 1, :].astype(F32)
        row = jnp.concatenate([row, jnp.zeros((1, 128 - shard), F32)], axis=1)
        SEGS[s] = jnp.broadcast_to(row, (8, 128))

    barrier = pltpu.get_barrier_semaphore()
    everyone = [(fp, c) for fp in fpeers] + [(f, 2 * zp + h) for zp in zpeers] + [sib]
    for dev in everyone:
        pl.semaphore_signal(barrier, inc=1, device_id=dev, device_id_type=MESH)
    pl.semaphore_wait(barrier, len(everyone))

    def wq_own_part(i):
        return [
            (wq.at[hrows(0, i), cols(b * wide + h * hw)], WQ.at[b, hrows(f, i)]) for b in range(3)
        ]

    pv_in = [rc(PV.at[f], PV.at[f], (fp, c)) for fp in fpeers]
    wq_all = Gather(wq_own_part, lambda j, i: WQ.at[:, hrows(j, i), :])
    my_slot = 4 * h + z
    s_in = [rc(SEGS.at[zp], SEGR.at[my_slot], (f, 2 * zp + h)) for zp in zpeers]
    x_in = [rc(inp.at[zp], X.at[my_block], (f, 2 * zp + h)) for zp in zpeers]
    c_in = [rc(cot.at[zp], COT.at[my_block], (f, 2 * zp + h)) for zp in zpeers]
    x_own = lc(inp.at[z], X.at[my_block])
    wq_own = [lc(wq.at[:, cols(b * wide + h * hw)], WQ.at[b, krows(f)]) for b in range(3)]
    wp_own = lc(wp.at[:, cols(h * hw)], WP.at[h, krows(f)])
    c_own = lc(cot.at[z], COT.at[my_block])
    wd_own = lc(wd.at[slot(h)], WD.at[slot(py)])

    def wu_strips(x_to):
        return [
            (wu.at[:, cols((2 * s + x_to) * wide + h * hw)], WU.at[krows(f), pl.ds(s * hw, hw)])
            for s in range(2)
        ]

    wu_own = [lc(src, dst) for src, dst in wu_strips(px)]
    SEGR[my_slot] = SEGS[z]
    SGP[...] = jnp.zeros_like(SGP)
    GBU[...] = jnp.zeros_like(GBU)
    wq_all.relay()
    wp_all = Gather(
        lambda i: [(wp.at[hrows(0, i), cols(h * hw)], WP.at[h, hrows(f, i)])],
        lambda j, i: WP.at[h, hrows(j, i)],
    )
    zq = z % 2
    pair_z = (f, 2 * zpeers[0] + h)
    wu_x = [
        rc(
            wu.at[hrows(0, zq), cols((2 * s + qx) * wide + h * hw)],
            WU.at[hrows(f, zq), pl.ds(s * hw, hw)],
            (fx, c),
        )
        for s in range(2)
    ]
    wu_y = [rc(src, dst, (fy, c)) for src, dst in wu_strips(px)]

    for copy in pv_in:
        copy.wait_recv()
    VEC[...] = jnp.concatenate([PV[j] for j in range(4)], axis=1)
    up_parts = []
    for s in range(2):
        shard_vec = PV[2 * s + px]
        for i in range(2):
            up_parts.append(jnp.where(h == 0, shard_vec[8 + i : 9 + i], shard_vec[10 + i : 11 + i]))
    bias_up = jnp.concatenate(up_parts, axis=1)

    def vector(i):
        return VEC[i : i + 1, :]

    x_own.wait()
    for copy in s_in + x_in:
        copy.wait_recv()
    my_slots = pl.ds(4 * h, 4)
    s_sib = rc(SEGR.at[my_slots], SEGR.at[my_slots], sib)
    x_sib = rc(X.at[own_rows], X.at[own_rows], sib)

    def ln1(start):
        def block(r):
            rows = pl.ds(mult(start + r, 64), 64)
            hat, _ = norm_parts(X[rows, :].astype(F32))
            H1[rows, :] = (hat * vector(LN1_S) + vector(LN1_B)).astype(BF16)

        loop_rows(half, 64, block)

    ln1(h * half)
    s_sib.wait_recv()
    for b in range(8):
        turned = jnp.transpose(jnp.broadcast_to(SEGR[b][0:1, :], (128, 128)))
        SEG[pl.ds(b * shard, shard), :] = turned[:shard, :]
    seg_row = jnp.transpose(SEG[...])[0:1, :]

    def mask(r):
        rows = pl.ds(r, 128)
        seg_col = SEG[rows, 0:1]
        place_q = r + lax.broadcasted_iota(jnp.int32, (128, rows_all), 0)
        place_k = lax.broadcasted_iota(jnp.int32, (128, rows_all), 1)
        allowed = (seg_col == seg_row) & ((seg_row >= 0.0) | (place_q == place_k))
        MB[rows, :] = jnp.where(allowed, 0.0, MASKED)

    x_sib.wait_recv()
    ln1(o * half)
    loop_rows(rows_all, 128, mask)

    for copy in wq_own:
        copy.wait()
    wp_own.wait()
    wq_all.near()
    wq_all.far()
    wp_all.relay()
    bias_half = [
        jnp.where(h == 0, vector(i)[:, :hw], vector(i)[:, hw:]) for i in (B_Q, B_V)
    ]
    for b, target in ((0, Q), (1, K), (2, V)):
        prod = dot_nn(H1[...], WQ[b])
        if b == 0:
            prod = (prod + bias_half[0]).astype(BF16) * SCORE_SCALE
        if b == 2:
            prod = prod + bias_half[1]
        prod = prod.astype(BF16)
        for p in range(pairs):
            target[p] = prod[:, p * 128 : (p + 1) * 128]
    c_own.wait()
    for copy in c_in:
        copy.wait_recv()
    c_sib = rc(COT.at[own_rows], COT.at[own_rows], sib)
    cot_in = rc(COT.at[own_rows], COT.at[chunk_rows(1)], (fx, c))

    low_half = lax.broadcasted_iota(jnp.int32, (1, 128), 1) < 64

    def pick(s, values):
        keep = low_half if s == 0 else jnp.logical_not(low_half)
        return jnp.where(keep, values, jnp.zeros_like(values))

    mix_out = []
    for p in range(pairs):

        def attend(r, p=p):
            rows = pl.ds(r, 128)
            total = None
            for s in range(2):
                scores = dot_nt(pick(s, Q[p, rows, :]), K[p]) + MB[rows, :]
                top = jnp.max(scores, -1, keepdims=True)
                expo = jnp.exp(scores - top)
                inv = 1.0 / jnp.sum(expo, -1, keepdims=True)
                low = expo.astype(BF16)
                E[2 * p + s, rows, :] = low
                LI[2 * p + s, rows, :] = inv
                part = dot_nn(low, pick(s, V[p])) * inv
                total = part if total is None else total + part
            ATT[p, rows, :] = total
            MIX[pairs * h + p, rows, :] = total.astype(BF16)

        loop_rows(rows_all, 128, attend)
        mix_out.append(rc(MIX.at[pairs * h + p], MIX.at[pairs * h + p], sib))

    for copy in wu_x:
        copy.wait_recv()
    wu_far = rc(WU.at[hrows(fx, zq)], WU.at[hrows(fx, zq)], (fy, c))
    wu_pair = [rc(WU.at[hrows(fx, zq)], WU.at[hrows(fx, zq)], pair_z)]
    wd_in = rc(wd.at[slot(h)], WD.at[slot(py)], (fy, c))

    wp_all.near()
    wp_all.far()
    wp_sib = rc(WP.at[h], WP.at[h], sib)
    for copy in mix_out:
        copy.wait_recv()
    wp_sib.wait_recv()

    def project(r):
        rows = pl.ds(mult(h * half + r, 64), 64)
        mixed = jnp.concatenate([MIX[g, rows, :] for g in range(2 * pairs)], axis=1)
        branch = jnp.concatenate([dot_nn(mixed, WP[k]) for k in range(2)], axis=1)
        resid = X[rows, :].astype(F32) + branch + vector(B_P)
        RES[pl.ds(r, 64), :] = resid
        hat, _ = norm_parts(resid)
        H2[rows, :] = (
            hat * vector(LN2_S) + vector(LN2_B)
        ).astype(BF16)

    loop_rows(half, 64, project)
    h2_in = [
        rc(H2.at[half_rows(0, h, i)], H2.at[half_rows(1, h, i)], (fx, c)) for i in range(2)
    ]
    h2_sib = rc(H2.at[own_rows], H2.at[own_rows], sib)
    wu_far.wait_recv()
    wu_pair.append(rc(WU.at[hrows(fd, zq)], WU.at[hrows(fd, zq)], pair_z))

    def up(start, count):
        def block(r):
            rows = pl.ds(mult(start + r, 128), 128)
            pre = dot_nn(H2[rows, :], WU[...]) + bias_up
            square = pre * pre
            tan = jnp.tanh(GELU_A * pre * (1.0 + GELU_B * square))
            ACT[rows, :] = (0.5 * pre * (1.0 + tan)).astype(BF16)
            SLOPE[rows, :] = 0.5 * (1.0 + tan) + (0.5 * GELU_A) * pre * (1.0 - tan * tan) * (
                1.0 + (3.0 * GELU_B) * square
            )

        loop_rows(count, 128, block)

    def back(start, count):
        def block(r):
            rows = pl.ds(mult(start + r, 128), 128)
            d_pre = (dot_nt(COT[rows, :], WD[...]) * SLOPE[rows, :]).astype(BF16)
            DPRE[rows, :] = d_pre
            GBU[...] += jnp.sum(d_pre.astype(F32), 0, keepdims=True)
            PDH[rows, :] = dot_nt(d_pre, WU[...]).astype(BF16)

        loop_rows(count, 128, block)

    def start_of(j, core, i):
        return j * rows_all + core * half + i * (half // 2)

    class Owned:
        def __init__(self, mine, got, total, copy, z1, zs, z2, zf):
            self.mine, self.got, self.copy, self.total = mine, got, copy, total
            self.chain = Chain(total, z1, zs, z2, zf)
            self.second, self.third, self.fourth = (
                self.chain.second, self.chain.third, self.chain.fourth
            )

        def first(self):
            self.copy.wait_recv()
            self.total[...] = (self.mine[...].astype(F32) + self.got[...].astype(F32)).astype(BF16)
            self.chain.first()

    quarter = hw // 4

    def owned(part_of, got, total, z1, zs, z2, zf):
        made = []
        for i in range(4):
            part = pl.ds(i * quarter, quarter)

            def rows(s, i=i):
                return pl.ds(mult(s * hw + i * quarter, quarter), quarter)

            copy = rc(part_of.at[rows(qy)], got.at[part], (fy, c))
            made.append(
                Owned(
                    part_of.at[rows(py)], got.at[part], total.at[part], copy,
                    z1.at[part], zs.at[part], z2.at[part], zf.at[part],
                )
            )
        return made

    def down(j):
        rows = pl.ds(j * rows_all, rows_all)
        PO[rows, :] = dot_nn(ACT[rows, :], WD[...]).astype(BF16)
        return rc(PO.at[chunk_other(j)], RO.at[j], sib)

    def join(buf, got, j):
        def block(r):
            rows = pl.ds(mult(j * rows_all + h * half + r, 64), 64)
            buf[rows, :] = (buf[rows, :].astype(F32) + got[j, pl.ds(r, 64), :].astype(F32)).astype(BF16)

        loop_rows(half, 64, block)

    for copy in wu_own + [wd_own]:
        copy.wait()
    for copy in wu_y + wu_pair + [c_sib, h2_sib]:
        copy.wait_recv()
    up(0, rows_all)
    cot_in.wait_recv()
    cot_fwd = rc(COT.at[chunk_rows(1)], COT.at[chunk_rows(1)], sib)

    def arrive(i):
        h2_in[i].wait_recv()
        return rc(H2.at[half_rows(1, h, i)], H2.at[half_rows(1, h, i)], sib)

    def partial(i):
        return rc(PDH.at[half_rows(1, o, i)], RDH.at[1, pl.ds(i * (half // 2), half // 2)], sib)

    def pass_on(i, copy):
        copy.wait_recv()
        for r in range(0, half // 2, 64):
            rows = pl.ds(mult(start_of(1, h, i) + r, 64), 64)
            got = RDH[1, i * (half // 2) + r : i * (half // 2) + r + 64, :]
            PDH[rows, :] = (PDH[rows, :].astype(F32) + got.astype(F32)).astype(BF16)
        return rc(PDH.at[half_rows(1, h, i)], RDI.at[pl.ds(i * (half // 2), half // 2)], (fx, c))

    h2_fwd = [arrive(0)]
    up(start_of(1, h, 0), half // 2)
    h2_fwd[0].wait_recv()
    up(start_of(1, o, 0), half // 2)
    cot_fwd.wait_recv()
    wd_in.wait_recv()
    h2_fwd.append(arrive(1))
    back(start_of(1, o, 0), half // 2)
    far_dh = [partial(0)]
    back(start_of(1, h, 0), half // 2)
    h2_fwd[1].wait_recv()
    up(start_of(1, o, 1), half // 2)
    dh_in = [pass_on(0, far_dh[0])]
    up(start_of(1, h, 1), half // 2)
    GD[slot(qy), :] = dot_tn(ACT[:, slot(qy)], COT[...]).astype(BF16)
    chain_d = owned(GD, RGD, GDS, Z1D, ZSD, Z2D, ZFD.at[h])
    back(start_of(1, o, 1), half // 2)
    far_dh.append(partial(1))
    back(start_of(1, h, 1), half // 2)
    dh_in.append(pass_on(1, far_dh[1]))

    GD[slot(py), :] = dot_tn(ACT[:, slot(py)], COT[...]).astype(BF16)
    chain_d[0].first()
    far_o = down(1)
    back(0, rows_all)
    own_dh = rc(PDH.at[oth_rows], RDH.at[0], sib)
    chain_d[1].first()
    far_o.wait_recv()
    join(PO, RO, 1)
    o_in = rc(PO.at[chunk_rows(1)], ROI, (fx, c))
    GU[slot(qy), :] = dot_tn(H2[:, slot(qy)], DPRE[...]).astype(BF16)
    chain_u = owned(GU, RGU, GUS, Z1U, ZSU, Z2U, GUZ)
    chain_z = chain_d + chain_u
    for s in range(2):
        SGP[B_U + s : B_U + s + 1, cols(h * hw)] = GBU[:, s * hw : (s + 1) * hw]
    chain_z[0].second()
    own_dh.wait_recv()


    def ln2_back(r):
        rows = pl.ds(mult(r, 64), 64)
        mine = pl.ds(mult(h * half + r, 64), 64)
        d_h2 = PDH[mine, :].astype(F32) + RDH[0, rows, :].astype(F32) + RDI[rows, :].astype(F32)
        hat, inv = norm_parts(RES[rows, :])
        SGP[LN2_S : LN2_S + 1, :] += jnp.sum(d_h2 * hat, 0, keepdims=True)
        SGP[LN2_B : LN2_B + 1, :] += jnp.sum(d_h2, 0, keepdims=True)
        cot_rows = COT[mine, :].astype(F32)
        SGP[B_D : B_D + 1, :] += jnp.sum(cot_rows, 0, keepdims=True)
        d_resid = cot_rows + norm_back(d_h2, hat, inv, vector(LN2_S))
        DRES[rows, :] = d_resid
        low = d_resid.astype(BF16)
        SGP[B_P : B_P + 1, :] += jnp.sum(low.astype(F32), 0, keepdims=True)
        for k in range(2):
            DBR[k, rows, :] = low[:, k * hw : (k + 1) * hw]
        d_mixed = dot_nt(low[:, :hw], WP[0]) + dot_nt(low[:, hw:], WP[1])
        d_mixed = d_mixed.astype(BF16)
        for g in range(2 * pairs):
            DMS[g, rows, :] = d_mixed[:, g * 128 : (g + 1) * 128]

    for i in range(2):
        dh_in[i].wait_recv()
        loop_rows(half // 2, 64, lambda r, i=i: ln2_back(i * (half // 2) + r))
    dm_sib = rc(DMS.at[pl.ds(pairs * o, pairs)], DM.at[:, own_rows, :], sib)
    dbr_sib = rc(DBR.at[o], DBX.at[own_rows], sib)
    DM[:, own_rows, :] = DMS[pl.ds(pairs * h, pairs)]
    DBX[own_rows, :] = DBR[h]
    chain_z[2].first()
    chain_z[1].second()
    GU[slot(py), :] = dot_tn(H2[:, slot(py)], DPRE[...]).astype(BF16)
    own_o = down(0)
    chain_z[3].first()
    own_o.wait_recv()
    join(PO, RO, 0)
    chain_z[0].third()
    dbr_sib.wait_recv()
    mixed_all = jnp.concatenate([MIX[g] for g in range(2 * pairs)], axis=1)
    GPP[...] = dot_tn(mixed_all, DBX[...]).astype(BF16)
    p_plane = ScatterX(lambda j: GPP.at[krows(j)], lambda w: RGP.at[w], RGP.at[2])
    p_plane.far()
    p_plane.near()
    dm_sib.wait_recv()

    def attention_back(p, steps):
        def prepare(r):
            rows = pl.ds(r, 128)
            d_out = DM[p, rows, :].astype(F32)
            for s in range(2):
                scaled = pick(s, d_out * LI[2 * p + s, rows, :]).astype(BF16)
                DOS[s, rows, :] = scaled
                DLT[s, rows, :] = jnp.sum(scaled.astype(F32) * ATT[p, rows, :], -1, keepdims=True)

        loop_rows(rows_all, 128, prepare)
        d_value = dot_tn(E[2 * p], DOS[0]) + dot_tn(E[2 * p + 1], DOS[1])
        DQKV[p, :, 256:384] = d_value.astype(BF16)
        for step in steps[0]:
            step()

        def block(r):
            rows = pl.ds(r, 128)
            d_query = None
            for s in range(2):
                d_probs = dot_nt(DOS[s, rows, :], V[p])
                d_scores = (
                    E[2 * p + s, rows, :].astype(F32) * (d_probs - DLT[s, rows, :])
                ).astype(BF16)
                E[2 * p + s, rows, :] = d_scores
                part = dot_nn(d_scores, pick(s, K[p]))
                d_query = part if d_query is None else d_query + part
            DQKV[p, rows, 0:128] = (d_query * SCORE_SCALE).astype(BF16)

        loop_rows(rows_all, 128, block)
        for step in steps[1]:
            step()
        d_key = dot_tn(E[2 * p], pick(0, Q[p])) + dot_tn(E[2 * p + 1], pick(1, Q[p]))
        DQKV[p, :, 128:256] = d_key.astype(BF16)
        GQ[p] = dot_tn(H1[...], DQKV[p]).astype(BF16)
        if p < 2:
            plane = ScatterX(
                lambda j: GQ.at[p, krows(j)], lambda w: RGQ.at[p, w], RGQ.at[p, 2]
            )
        else:
            plane = Scatter(
                lambda j, i: GQ.at[p, hrows(j, i)],
                lambda w, i: RGQ.at[p, w, hrows(0, i)],
                lambda i: RGQ.at[p, 2, hrows(0, i)],
            )
        for step in steps[2]:
            step()
        plane.far()
        plane.near()
        here = pl.ds(mult(h * hw + p * 128, 128), 128)
        for b, i in ((0, B_Q), (2, B_V)):
            SGP[i : i + 1, here] = jnp.sum(
                DQKV[p, :, b * 128 : (b + 1) * 128].astype(F32), 0, keepdims=True
            )
        return plane

    kept = {}

    def finish_out():
        o_in.wait_recv()

        def finish(r):
            rows = pl.ds(r, 64)
            mine = pl.ds(mult(h * half + r, 64), 64)
            total = PO[mine, :].astype(F32) + ROI[rows, :].astype(F32)
            OUTB[rows, :] = (RES[rows, :] + total + vector(B_D)).astype(BF16)

        loop_rows(half, 64, finish)
        kept["res_own"] = lc(OUTB.at[block_of(z)], out_ref.at[z])

    def first(i):
        return chain_z[i].first

    def second(i):
        return chain_z[i].second

    def third(i):
        return chain_z[i].third

    kept["res"] = []

    def send_out(i):
        def send():
            zp = zpeers[i]
            kept["res"].append(rc(OUTB.at[block_of(zp)], out_ref.at[z], (f, 2 * zp + h)))

        return send

    q_plane = []
    q_plane.append(
        attention_back(
            0, ([second(2), first(4)], [third(1), second(3)], [first(5), third(2)])
        )
    )
    q_plane.append(
        attention_back(
            1,
            ([second(4), first(6), finish_out, send_out(1)], [third(3), send_out(2)], [second(5), send_out(0)]),
        )
    )
    q_plane.append(
        attention_back(
            2,
            ([first(7), second(6), p_plane.relay], [third(4)], [third(5), q_plane[0].relay]),
        )
    )

    def joined(b):
        return jnp.concatenate([DQKV[p, :, b * 128 : (b + 1) * 128] for p in range(pairs)], axis=1)

    PD1[...] = (
        dot_nt(joined(0), WQ[0]) + dot_nt(joined(1), WQ[1]) + dot_nt(joined(2), WQ[2])
    ).astype(BF16)
    d1_sib = rc(PD1.at[oth_rows], RD1, sib)
    links = []

    def start_chain(mine, z1, zs, z2, zf, pieces):
        rows = kr // pieces
        made = []
        for i in range(pieces):
            part = pl.ds(i * rows, rows)
            made.append(Chain(mine.at[part], z1.at[part], zs.at[part], z2.at[part], zf.at[part]))
            made[i].first()
        links.append((made, zf))

    def own_p():
        p_plane.wait()
        GP[...] = (
            GPP[krows(f), :].astype(F32) + RGP[0].astype(F32) + RGP[2].astype(F32)
        ).astype(BF16)
        start_chain(GP, Z1P, ZSP, Z2P, ZFP.at[h], 1)

    def own_q(b, pieces):
        q_plane[b].wait()
        GQF[b] = (
            GQ[b, krows(f), :].astype(F32) + RGQ[b, 0].astype(F32) + RGQ[b, 2].astype(F32)
        ).astype(BF16)
        start_chain(GQF.at[b], Z1Q.at[b], ZSQ.at[b], Z2Q.at[b], ZFQ.at[h, b], pieces)

    def step_two(i):
        for chain in links[i][0]:
            chain.second()

    def step_three(i):
        for chain in links[i][0]:
            chain.third()

    def step_four(i):
        for chain in links[i][0]:
            chain.fourth()
        return rc(links[i][1], links[i][1], sib)

    second(7)()
    own_p()
    d1_sib.wait_recv()

    def ln1_back(r):
        rows = pl.ds(r, 64)
        mine = pl.ds(mult(h * half + r, 64), 64)
        d_h1 = PD1[mine, :].astype(F32) + RD1[rows, :].astype(F32)
        hat, inv = norm_parts(X[mine, :].astype(F32))
        SGP[LN1_S : LN1_S + 1, :] += jnp.sum(d_h1 * hat, 0, keepdims=True)
        SGP[LN1_B : LN1_B + 1, :] += jnp.sum(d_h1, 0, keepdims=True)
        DIN[rows, :] = (DRES[rows, :] + norm_back(d_h1, hat, inv, vector(LN1_S))).astype(BF16)

    loop_rows(half, 64, ln1_back)
    din_in = [rc(DIN.at[block_of(zp)], din_ref.at[z], (f, 2 * zp + h)) for zp in zpeers]
    din_own = lc(DIN.at[block_of(z)], din_ref.at[z])
    sg_sib = rc(SGP, SGS, sib)
    third(6)()
    q_plane[1].relay()
    own_q(0, 1)
    step_two(0)
    sg_sib.wait_recv()
    small = SGP[...] + SGS[...]
    for j in range(4):
        units = small[B_U + j // 2 : B_U + j // 2 + 1]
        units = jnp.where(px == j % 2, units, jnp.zeros_like(units))
        SGT[j] = jnp.concatenate(
            [small[:8, j * kr : (j + 1) * kr]]
            + [units[:, i * kr : (i + 1) * kr] for i in range(4)]
            + [jnp.zeros((4, kr), F32)],
            axis=0,
        )
    SGB[f] = SGT[f]
    sgf_in = [rc(SGT.at[fp], SGB.at[f], (fp, c)) for fp in fpeers]
    q_plane[2].relay()
    third(7)()
    own_q(1, 1)
    step_two(1)
    step_three(0)
    for chain in chain_d:
        chain.fourth()
    d_sib = rc(ZFD.at[h], ZFD.at[h], sib)
    for copy in sgf_in:
        copy.wait_recv()
    SGZ[z] = SGB[0] + SGB[1] + SGB[2] + SGB[3]
    sgz_in = [rc(SGZ.at[z], SGZ.at[z], (f, 2 * zp + h)) for zp in zpeers]
    for chain in chain_u:
        chain.fourth()
    gu_out = rc(GUZ.at[krows(qx)], ZFU.at[h, px], (fx, c))
    ZFU[h, px] = GUZ[krows(px), :]
    own_q(2, 2)
    step_two(2)
    step_three(1)
    p_sib = step_four(0)
    d_sib.wait_recv()
    outs = [lc(ZFD.at[k], gd_ref.at[pl.ds(k * hw, hw)]) for k in range(2)]
    step_two(3)
    step_three(2)
    q_sib = [step_four(1)]
    for copy in sgz_in:
        copy.wait_recv()
    sg_ref[...] = SGZ[0] + SGZ[1] + SGZ[2] + SGZ[3]
    p_sib.wait_recv()
    outs += [lc(ZFP.at[k], gp_ref.at[:, pl.ds(k * hw, hw)]) for k in range(2)]
    gu_out.wait_recv()
    u_sib = rc(ZFU.at[h], ZFU.at[h], sib)
    step_three(3)
    q_sib.append(step_four(2))
    u_sib.wait_recv()
    outs += [
        lc(
            ZFU.at[k, x_of, :, pl.ds(s * hw, hw)],
            gu_ref.at[:, pl.ds((2 * s + x_of) * wide + k * hw, hw)],
        )
        for k in range(2)
        for s in range(2)
        for x_of in range(2)
    ]
    q_sib.append(step_four(3))
    for p in range(3):
        q_sib[p].wait_recv()
        outs += [
            lc(
                ZFQ.at[k, p, :, pl.ds(b * 128, 128)],
                gq_ref.at[:, pl.ds(b * wide + k * hw + p * 128, 128)],
            )
            for k in range(2)
            for b in range(3)
        ]
    for copy in kept["res"] + din_in:
        copy.wait_recv()
    for copy in outs + [kept["res_own"], din_own]:
        copy.wait()
    for copy in sent:
        copy.wait_send()


def widen_kernel(
    out_in, din_in, gd_in, gu_in, gp_in, gq_in, sg_hbm,
    out_ref, din_ref, s0, s1, gq_ref, s2, s3, gp_ref, s4, s5, s6, gu_ref, b_up_ref, gd_ref, s7,
    sg_in, LT, LD, LU, LP, LQ, FD, FU, FP, FQ, sems,
):
    counts = [0]

    def lc(src, dst):
        copy = pltpu.make_async_copy(src, dst, sems.at[counts[0]])
        counts[0] += 1
        copy.start()
        return copy

    def halves(ref):
        rows = ref.shape[0] // 2
        return [pl.ds(i * rows, rows) for i in range(2)]

    small = lc(sg_hbm, sg_in)
    work = []
    for src, low, wide, dst in (
        (gd_in, LD, FD, gd_ref), (gu_in, LU, FU, gu_ref), (gq_in, LQ, FQ, gq_ref), (gp_in, LP, FP, gp_ref)
    ):
        for part in halves(src):
            work.append((lc(src.at[part], low.at[part]), low.at[part], wide.at[part], dst.at[part]))
    tokens = [lc(out_in, LT.at[0]), lc(din_in, LT.at[1])]
    passed = []
    kr = s0.shape[0]
    small.wait()
    for i, ref in enumerate((s0, s1, s2, s3, s4, s5, s6, s7)):
        ref[...] = sg_in[i : i + 1, :].reshape(kr)
    b_up_ref[...] = jnp.concatenate([sg_in[i : i + 1, :] for i in range(8, 12)], axis=1).reshape(4 * kr)
    for copy, src, dst in zip(tokens, (LT.at[0], LT.at[1]), (out_ref, din_ref)):
        copy.wait()
        passed.append(lc(src, dst))
    for copy, low, wide, dst in work:
        copy.wait()
        wide[...] = low[...].astype(F32)
        passed.append(lc(wide, dst))
    for copy in passed:
        copy.wait()


def fast_device(
    inputs, segments, ln1_scale, ln1_bias, w_qkv, b_query, b_value, w_proj, b_proj,
    ln2_scale, ln2_bias, w_up, b_up, w_down, b_down, cotangent,
):
    micro_count, seq_dev, shard, wide = inputs.shape
    seqs = micro_count * seq_dev
    rows_all = 8 * shard
    half = rows_all // 2
    hw = wide // 2
    kr = wide // 4
    pairs = hw // 128
    heads = 2 * pairs

    def vm(*shape, dtype=BF16):
        return pltpu.VMEM(shape, dtype)

    f32 = functools.partial(vm, dtype=F32)
    pair_rows = 2 * rows_all
    scratch = [
        vm(rows_all, wide), f32(4, 8, 128), f32(8, 8, 128), f32(rows_all, 128),
        vm(pair_rows, wide), vm(pair_rows, wide), f32(4, 16, kr), f32(16, wide),
        vm(3, wide, hw), vm(2, wide, hw), vm(wide, wide), vm(wide, wide),
        vm(rows_all, wide), vm(pairs, rows_all, 128), vm(pairs, rows_all, 128),
        vm(pairs, rows_all, 128), vm(heads, rows_all, rows_all), f32(rows_all, rows_all),
        f32(pairs, rows_all, 128), f32(heads, rows_all, 1), vm(2 * pairs, rows_all, 128),
        f32(half, wide),
        vm(pair_rows, wide), f32(pair_rows, wide), vm(pair_rows, wide),
        vm(pair_rows, wide), vm(2, half, wide), vm(half, wide),
        vm(pair_rows, wide), vm(2, half, wide), vm(half, wide), vm(half, wide),
        f32(half, wide), vm(2, half, hw), vm(rows_all, hw), vm(2 * pairs, half, 128),
        vm(pairs, rows_all, 128), vm(2, rows_all, 128), f32(2, rows_all, 1),
        vm(pairs, rows_all, hw),
        vm(wide, wide), vm(hw, wide), vm(hw, wide), vm(hw, wide), vm(hw, wide), vm(hw, wide),
        vm(2, hw, wide),
        vm(wide, wide), vm(hw, wide), vm(hw, wide), vm(hw, wide), vm(hw, wide), vm(hw, wide),
        vm(hw, wide), vm(2, 2, kr, wide),
        vm(wide, hw), vm(3, kr, hw), vm(kr, hw), vm(kr, hw), vm(kr, hw), vm(kr, hw), vm(2, kr, hw),
        vm(pairs, wide, hw), vm(pairs, 3, kr, hw), vm(pairs, kr, hw), vm(pairs, kr, hw),
        vm(pairs, kr, hw), vm(pairs, kr, hw), vm(2, pairs, kr, hw),
        vm(rows_all, wide), vm(half, wide), vm(half, wide),
        f32(16, wide), f32(16, wide), f32(4, 16, kr), f32(4, 16, kr), f32(4, 16, kr), f32(1, wide),
        pltpu.SemaphoreType.DMA((216,)), pltpu.SemaphoreType.DMA((216,)),
        pltpu.SemaphoreType.DMA((64,)),
    ]
    hbm = pl.BlockSpec(memory_space=pl.ANY)
    vmem = pl.BlockSpec(memory_space=pltpu.VMEM)
    tokens = jax.ShapeDtypeStruct((seqs, shard, wide), BF16)
    small = jax.ShapeDtypeStruct((16, kr), F32)
    grads = (w_down, w_up, w_proj, w_qkv)
    results = pl.pallas_call(
        layer_kernel,
        out_shape=(tokens, tokens) + tuple(jax.ShapeDtypeStruct(w.shape, BF16) for w in grads) + (small,),
        in_specs=[hbm] + [vmem] * 9 + [hbm] * 4 + [vmem, hbm],
        out_specs=(hbm,) * 6 + (vmem,),
        scratch_shapes=scratch,
        compiler_params=pltpu.CompilerParams(
            collective_id=0, has_side_effects=True, vmem_limit_bytes=62 << 20
        ),
    )(
        inputs.reshape(tokens.shape), segments, ln1_scale, ln1_bias, b_query, b_value, b_proj,
        ln2_scale, ln2_bias, b_down, w_qkv, w_proj, w_up, w_down, b_up, cotangent.reshape(tokens.shape),
    )
    part = jax.ShapeDtypeStruct((kr,), F32)

    def full(w):
        return jax.ShapeDtypeStruct(w.shape, F32)

    out, d_input, *rest = pl.pallas_call(
        widen_kernel,
        out_shape=(
            tokens, tokens, part, part, full(w_qkv), part, part, full(w_proj), part, part, part,
            full(w_up), jax.ShapeDtypeStruct((wide,), F32), full(w_down), part,
        ),
        in_specs=[pl.BlockSpec(memory_space=pltpu.HBM)] * 7,
        out_specs=(hbm, hbm, vmem, vmem, hbm, vmem, vmem, hbm, vmem, vmem, vmem, hbm, vmem, hbm, vmem),
        scratch_shapes=[pltpu.VMEM(small.shape, F32), pltpu.VMEM((2,) + tokens.shape, BF16)]
        + [pltpu.VMEM(w.shape, BF16) for w in grads]
        + [pltpu.VMEM(w.shape, F32) for w in grads]
        + [pltpu.SemaphoreType.DMA((32,))],
        compiler_params=pltpu.CompilerParams(vmem_limit_bytes=62 << 20),
    )(*results)
    return (out.reshape(inputs.shape), d_input.reshape(inputs.shape), *rest)


def fits_fast(mesh, inputs, w_up):
    micro_count, seqs, length, wide = inputs.shape
    return (
        mesh.shape["fsdp"] == 4
        and mesh.shape["ctx"] == 8
        and micro_count * (seqs // 4) == 4
        and length == 512
        and wide == 768
        and w_up.shape == (wide, 4 * wide)
        and HEADS * 64 == wide
    )


def solution(mesh):
    placed = (
        P(None, "fsdp", "ctx", None),
        P(None, "fsdp", "ctx"),
        P("fsdp"),
        P("fsdp"),
        P("fsdp", None),
        P("fsdp"),
        P("fsdp"),
        P("fsdp", None),
        P("fsdp"),
        P("fsdp"),
        P("fsdp"),
        P("fsdp", None),
        P("fsdp"),
        P("fsdp", None),
        P("fsdp"),
        P(None, "fsdp", "ctx", None),
    )
    spread = functools.partial(
        jax.shard_map,
        mesh=mesh,
        in_specs=placed,
        out_specs=(
            P(None, "fsdp", "ctx", None),
            P(None, "fsdp", "ctx", None),
            P("fsdp"),
            P("fsdp"),
            P("fsdp", None),
            P("fsdp"),
            P("fsdp"),
            P("fsdp", None),
            P("fsdp"),
            P("fsdp"),
            P("fsdp"),
            P("fsdp", None),
            P("fsdp"),
            P("fsdp", None),
            P("fsdp"),
        ),
        check_vma=False,
    )

    def layer(*args):
        chosen = fast_device if fits_fast(mesh, args[0], args[11]) else per_device
        return spread(chosen)(*args)

    return layer
```

```python
import functools
import math

import jax
import jax.numpy as jnp
from jax import lax
from jax.experimental import pallas as pl
from jax.experimental.pallas import tpu as pltpu
from jax.sharding import PartitionSpec as P

HEADS = 12


NORM_EPS = 1e-06
SCORE_SCALE = 0.125
MASKED = -1e30


def layer_norm(values, scale_vec, bias_vec):
    center = values - jnp.mean(values, -1, keepdims=True)
    spread = jnp.mean(center * center, -1, keepdims=True)
    return center * lax.rsqrt(spread + NORM_EPS) * scale_vec + bias_vec


def gelu_tanh(values):
    return jax.nn.gelu(values, approximate=True)


def block_size(length_in, step_rows):
    blocked = step_rows
    while blocked * 2 <= 512 and length_in % (blocked * 2) == 0:
        blocked = blocked * 2
    return blocked


def to_heads(array, head_count):
    return array.reshape(array.shape[0], array.shape[1], head_count, -1)


def allowed_mask(seg_query, pos_query, seg_key, pos_key):
    same = seg_query[:, :, None] == seg_key[:, None, :]
    living = (seg_key[:, None, :] >= 0.0) | (pos_query[:, None] == pos_key[None, :])[None]
    return (same & living)[:, :, None, :]


def score_block(query_blk, key_blk, seg_query, pos_query, seg_key, pos_key):
    scores = (
        jnp.einsum("sqhd,skhd->sqhk", query_blk, key_blk, preferred_element_type=jnp.float32)
        * SCORE_SCALE
    )
    return (scores, allowed_mask(seg_query, pos_query, seg_key, pos_key))


def block_grads(
    query_blk,
    dout_blk,
    lse_blk,
    delta_blk,
    seg_query,
    pos_query,
    key_blk,
    value_blk,
    seg_key,
    pos_key,
):
    scores, allowed = score_block(query_blk, key_blk, seg_query, pos_query, seg_key, pos_key)
    probs = jnp.where(allowed, jnp.exp(scores - lse_blk[..., None]), 0.0)
    dprobs = jnp.einsum("sqhd,skhd->sqhk", dout_blk, value_blk, preferred_element_type=jnp.float32)
    dscores = (probs * (dprobs - delta_blk[..., None])).astype(jnp.bfloat16)
    return (dscores, probs.astype(jnp.bfloat16))


def key_side(
    query_blk,
    dout_blk,
    lse_blk,
    delta_blk,
    seg_query,
    pos_query,
    key_blk,
    value_blk,
    seg_key,
    pos_key,
):
    dscores, probs_low = block_grads(
        query_blk,
        dout_blk,
        lse_blk,
        delta_blk,
        seg_query,
        pos_query,
        key_blk,
        value_blk,
        seg_key,
        pos_key,
    )
    key_grad = (
        jnp.einsum("sqhk,sqhd->skhd", dscores, query_blk, preferred_element_type=jnp.float32)
        * SCORE_SCALE
    )
    value_grad = jnp.einsum(
        "sqhk,sqhd->skhd", probs_low, dout_blk, preferred_element_type=jnp.float32
    )
    return (key_grad, value_grad)


def contract_rows(left, right):
    return lax.dot_general(
        left, right, (((0,), (0,)), ((), ())), preferred_element_type=jnp.float32
    )


def contract_cols(left, right):
    return lax.dot_general(
        left, right, (((1,), (1,)), ((), ())), preferred_element_type=jnp.float32
    )


def per_device(
    inputs,
    segments,
    ln1_scale,
    ln1_bias,
    w_qkv,
    b_query,
    b_value,
    w_proj,
    b_proj,
    ln2_scale,
    ln2_bias,
    w_up,
    b_up,
    w_down,
    b_down,
    cotangent,
):
    micro_count, seq_dev, shard_len, model_width = inputs.shape
    head_count = HEADS
    head_width = model_width // head_count
    row_count = seq_dev * shard_len
    place = lax.axis_index("ctx")
    pos_local = place * shard_len + lax.iota(jnp.int32, shard_len)
    owned = (
        ln1_scale,
        ln1_bias,
        w_qkv,
        b_query,
        b_value,
        w_proj,
        b_proj,
        ln2_scale,
        ln2_bias,
        w_up,
        b_up,
        w_down,
        b_down,
    )
    summed_shards = None
    outputs_list = []
    input_grads = []
    for batch_num in range(micro_count):
        gathered = (
            lax.all_gather(owned[0], "fsdp", axis=0, tiled=True),
            lax.all_gather(owned[1], "fsdp", axis=0, tiled=True),
            lax.all_gather(owned[2], "fsdp", axis=0, tiled=True),
            lax.all_gather(owned[3], "fsdp", axis=0, tiled=True),
            lax.all_gather(owned[4], "fsdp", axis=0, tiled=True),
            lax.all_gather(owned[5], "fsdp", axis=0, tiled=True),
            lax.all_gather(owned[6], "fsdp", axis=0, tiled=True),
            lax.all_gather(owned[7], "fsdp", axis=0, tiled=True),
            lax.all_gather(owned[8], "fsdp", axis=0, tiled=True),
            lax.all_gather(owned[9], "fsdp", axis=0, tiled=True),
            lax.all_gather(owned[10], "fsdp", axis=0, tiled=True),
            lax.all_gather(owned[11], "fsdp", axis=0, tiled=True),
            lax.all_gather(owned[12], "fsdp", axis=0, tiled=True),
        )
        (
            gain_one,
            shift_one,
            w_qkv_all,
            bias_query,
            bias_value,
            w_proj_all,
            bias_proj,
            gain_two,
            shift_two,
            w_up_all,
            bias_up,
            w_down_all,
            bias_down,
        ) = gathered
        x_rows = inputs[batch_num].reshape(row_count, model_width).astype(jnp.float32)
        seg_local = segments[batch_num].astype(jnp.float32)
        cot_rows = cotangent[batch_num].reshape(row_count, model_width)
        normed_one, norm_one_pull = jax.vjp(
            layer_norm, x_rows, gain_one.astype(jnp.float32), shift_one.astype(jnp.float32)
        )
        hidden_one = normed_one.astype(jnp.bfloat16)
        projected = jnp.dot(hidden_one, w_qkv_all, preferred_element_type=jnp.float32)
        queries = (projected[:, :model_width] + bias_query.astype(jnp.float32)).astype(jnp.bfloat16)
        keys_loc = projected[:, model_width : 2 * model_width].astype(jnp.bfloat16)
        values_loc = (projected[:, 2 * model_width :] + bias_value.astype(jnp.float32)).astype(
            jnp.bfloat16
        )
        query_heads = queries.reshape(seq_dev, shard_len, head_count, head_width)
        shipped = (
            keys_loc.reshape(seq_dev, shard_len, model_width),
            values_loc.reshape(seq_dev, shard_len, model_width),
            seg_local.astype(jnp.bfloat16),
        )
        stat_shape = (seq_dev, shard_len, head_count)
        start_state = (
            jnp.full(stat_shape, MASKED, jnp.float32),
            jnp.zeros(stat_shape, jnp.float32),
            jnp.zeros((seq_dev, shard_len, head_count, head_width), jnp.float32),
        )
        key_part = lax.all_gather(shipped[0], "ctx", axis=1, tiled=True)
        value_part = lax.all_gather(shipped[1], "ctx", axis=1, tiled=True)
        seg_part = lax.all_gather(shipped[2], "ctx", axis=1, tiled=True)
        length_in = key_part.shape[1]
        step_len = block_size(length_in, shard_len)

        def forward_inner(turn, state):
            row_max, row_sum, weighted = state
            begin = turn * step_len
            key_blk = to_heads(lax.dynamic_slice_in_dim(key_part, begin, step_len, 1), head_count)
            value_blk = to_heads(
                lax.dynamic_slice_in_dim(value_part, begin, step_len, 1), head_count
            )
            seg_blk = lax.dynamic_slice_in_dim(seg_part, begin, step_len, 1).astype(jnp.float32)
            pos_blk = begin + lax.iota(jnp.int32, step_len)
            scores, allowed = score_block(
                query_heads, key_blk, seg_local, pos_local, seg_blk, pos_blk
            )
            scores = jnp.where(allowed, scores, MASKED)
            new_max = jnp.maximum(row_max, jnp.max(scores, -1))
            expo = jnp.where(allowed, jnp.exp(scores - new_max[..., None]), 0.0)
            factor = jnp.exp(row_max - new_max)
            row_sum = row_sum * factor + jnp.sum(expo, -1)
            weighted = weighted * factor[..., None] + jnp.einsum(
                "sqhk,skhd->sqhd",
                expo.astype(jnp.bfloat16),
                value_blk,
                preferred_element_type=jnp.float32,
            )
            return (new_max, row_sum, weighted)

        row_max, row_sum, weighted = lax.fori_loop(
            0, length_in // step_len, forward_inner, start_state
        )
        attended = weighted / row_sum[..., None]
        log_sum = row_max + jnp.log(row_sum)
        mixed = attended.reshape(row_count, model_width).astype(jnp.bfloat16)
        resid = (
            x_rows
            + jnp.dot(mixed, w_proj_all, preferred_element_type=jnp.float32)
            + bias_proj.astype(jnp.float32)
        )
        normed_two, norm_two_pull = jax.vjp(
            layer_norm, resid, gain_two.astype(jnp.float32), shift_two.astype(jnp.float32)
        )
        hidden_two = normed_two.astype(jnp.bfloat16)
        pre_act = jnp.dot(
            hidden_two, w_up_all, preferred_element_type=jnp.float32
        ) + bias_up.astype(jnp.float32)
        activ, gelu_pull = jax.vjp(gelu_tanh, pre_act)
        activ_low = activ.astype(jnp.bfloat16)
        result = (
            resid
            + jnp.dot(activ_low, w_down_all, preferred_element_type=jnp.float32)
            + bias_down.astype(jnp.float32)
        )
        outputs_list.append(result.astype(jnp.bfloat16).reshape(seq_dev, shard_len, model_width))
        d_activ = contract_cols(cot_rows, w_down_all)
        grad_down = contract_rows(activ_low, cot_rows)
        grad_bias_down = jnp.sum(cot_rows.astype(jnp.float32), 0)
        d_pre = gelu_pull(d_activ)[0].astype(jnp.bfloat16)
        grad_up = contract_rows(hidden_two, d_pre)
        grad_bias_up = jnp.sum(d_pre.astype(jnp.float32), 0)
        d_hidden_two = contract_cols(d_pre, w_up_all)
        d_resid_part, grad_gain_two, grad_shift_two = norm_two_pull(d_hidden_two)
        d_resid = cot_rows.astype(jnp.float32) + d_resid_part
        d_branch = d_resid.astype(jnp.bfloat16)
        grad_proj = contract_rows(mixed, d_branch)
        grad_bias_proj = jnp.sum(d_branch.astype(jnp.float32), 0)
        d_mixed = contract_cols(d_branch, w_proj_all).astype(jnp.bfloat16)
        dout_heads = d_mixed.reshape(seq_dev, shard_len, head_count, head_width)
        delta = jnp.sum(dout_heads.astype(jnp.float32) * attended, -1)
        zero_heads = jnp.zeros((seq_dev, shard_len, head_count, head_width), jnp.float32)
        key_all, value_all, seg_all = (
            lax.all_gather(shipped[0], "ctx", axis=1, tiled=True),
            lax.all_gather(shipped[1], "ctx", axis=1, tiled=True),
            lax.all_gather(shipped[2], "ctx", axis=1, tiled=True),
        )
        query_key_part = key_all
        query_value_part = value_all
        query_seg_part = seg_all
        query_length_in = query_key_part.shape[1]
        query_step_len = block_size(query_length_in, shard_len)

        def query_inner(turn, grad_in):
            begin = turn * query_step_len
            key_blk = to_heads(
                lax.dynamic_slice_in_dim(query_key_part, begin, query_step_len, 1), head_count
            )
            value_blk = to_heads(
                lax.dynamic_slice_in_dim(query_value_part, begin, query_step_len, 1), head_count
            )
            seg_blk = lax.dynamic_slice_in_dim(query_seg_part, begin, query_step_len, 1).astype(
                jnp.float32
            )
            pos_blk = 0 + begin + lax.iota(jnp.int32, query_step_len)
            dscores, probs_low = block_grads(
                query_heads,
                dout_heads,
                log_sum,
                delta,
                seg_local,
                pos_local,
                key_blk,
                value_blk,
                seg_blk,
                pos_blk,
            )
            return (
                grad_in
                + jnp.einsum(
                    "sqhk,skhd->sqhd", dscores, key_blk, preferred_element_type=jnp.float32
                )
                * SCORE_SCALE
            )

        query_grad = lax.fori_loop(0, query_length_in // query_step_len, query_inner, zero_heads)
        rows_in = shard_len * lax.axis_size("ctx")
        key_step_len = block_size(rows_in, shard_len)

        def one_block(turn):
            begin = turn * key_step_len
            key_blk = to_heads(
                lax.dynamic_slice_in_dim(key_all, begin, key_step_len, 1), head_count
            )
            value_blk = to_heads(
                lax.dynamic_slice_in_dim(value_all, begin, key_step_len, 1), head_count
            )
            seg_blk = lax.dynamic_slice_in_dim(seg_all, begin, key_step_len, 1).astype(jnp.float32)
            pos_blk = begin + lax.iota(jnp.int32, key_step_len)
            key_grad, value_grad = key_side(
                query_heads,
                dout_heads,
                log_sum,
                delta,
                seg_local,
                pos_local,
                key_blk,
                value_blk,
                seg_blk,
                pos_blk,
            )
            joined = jnp.stack(
                (
                    key_grad.reshape(seq_dev, key_step_len, model_width),
                    value_grad.reshape(seq_dev, key_step_len, model_width),
                ),
                2,
            )
            return joined.transpose(1, 0, 2, 3).reshape(key_step_len, seq_dev * 2 * model_width)

        blocks = lax.map(one_block, jnp.arange(rows_in // key_step_len, dtype=jnp.int32))
        own_terms = lax.psum_scatter(
            blocks.reshape(rows_in, seq_dev * 2 * model_width).astype(jnp.bfloat16),
            "ctx",
            scatter_dimension=0,
            tiled=True,
        ).astype(jnp.float32)
        own_terms = own_terms.reshape(shard_len, seq_dev, 2, model_width).transpose(1, 2, 0, 3)
        key_grad = own_terms[:, 0]
        value_grad = own_terms[:, 1]
        query_low = query_grad.reshape(row_count, model_width).astype(jnp.bfloat16)
        key_low = key_grad.reshape(row_count, model_width).astype(jnp.bfloat16)
        value_low = value_grad.reshape(row_count, model_width).astype(jnp.bfloat16)
        d_qkv = jnp.concatenate((query_low, key_low, value_low), 1)
        grad_qkv = contract_rows(hidden_one, d_qkv)
        grad_bias_query = jnp.sum(query_low.astype(jnp.float32), 0)
        grad_bias_value = jnp.sum(value_low.astype(jnp.float32), 0)
        d_hidden_one = contract_cols(d_qkv, w_qkv_all)
        d_input_part, grad_gain_one, grad_shift_one = norm_one_pull(d_hidden_one)
        input_grads.append(
            (d_resid + d_input_part).astype(jnp.bfloat16).reshape(seq_dev, shard_len, model_width)
        )
        local_grads = (
            grad_gain_one,
            grad_shift_one,
            grad_qkv,
            grad_bias_query,
            grad_bias_value,
            grad_proj,
            grad_bias_proj,
            grad_gain_two,
            grad_shift_two,
            grad_up,
            grad_bias_up,
            grad_down,
            grad_bias_down,
        )
        shard_part = (
            lax.psum_scatter(
                local_grads[0].astype(jnp.bfloat16), "fsdp", scatter_dimension=0, tiled=True
            ).astype(jnp.float32),
            lax.psum_scatter(
                local_grads[1].astype(jnp.bfloat16), "fsdp", scatter_dimension=0, tiled=True
            ).astype(jnp.float32),
            lax.psum_scatter(
                local_grads[2].astype(jnp.bfloat16), "fsdp", scatter_dimension=0, tiled=True
            ).astype(jnp.float32),
            lax.psum_scatter(
                local_grads[3].astype(jnp.bfloat16), "fsdp", scatter_dimension=0, tiled=True
            ).astype(jnp.float32),
            lax.psum_scatter(
                local_grads[4].astype(jnp.bfloat16), "fsdp", scatter_dimension=0, tiled=True
            ).astype(jnp.float32),
            lax.psum_scatter(
                local_grads[5].astype(jnp.bfloat16), "fsdp", scatter_dimension=0, tiled=True
            ).astype(jnp.float32),
            lax.psum_scatter(
                local_grads[6].astype(jnp.bfloat16), "fsdp", scatter_dimension=0, tiled=True
            ).astype(jnp.float32),
            lax.psum_scatter(
                local_grads[7].astype(jnp.bfloat16), "fsdp", scatter_dimension=0, tiled=True
            ).astype(jnp.float32),
            lax.psum_scatter(
                local_grads[8].astype(jnp.bfloat16), "fsdp", scatter_dimension=0, tiled=True
            ).astype(jnp.float32),
            lax.psum_scatter(
                local_grads[9].astype(jnp.bfloat16), "fsdp", scatter_dimension=0, tiled=True
            ).astype(jnp.float32),
            lax.psum_scatter(
                local_grads[10].astype(jnp.bfloat16), "fsdp", scatter_dimension=0, tiled=True
            ).astype(jnp.float32),
            lax.psum_scatter(
                local_grads[11].astype(jnp.bfloat16), "fsdp", scatter_dimension=0, tiled=True
            ).astype(jnp.float32),
            lax.psum_scatter(
                local_grads[12].astype(jnp.bfloat16), "fsdp", scatter_dimension=0, tiled=True
            ).astype(jnp.float32),
        )
        shard_part = (
            lax.psum(shard_part[0].astype(jnp.bfloat16), "ctx").astype(jnp.float32),
            lax.psum(shard_part[1].astype(jnp.bfloat16), "ctx").astype(jnp.float32),
            lax.psum(shard_part[2].astype(jnp.bfloat16), "ctx").astype(jnp.float32),
            lax.psum(shard_part[3].astype(jnp.bfloat16), "ctx").astype(jnp.float32),
            lax.psum(shard_part[4].astype(jnp.bfloat16), "ctx").astype(jnp.float32),
            lax.psum(shard_part[5].astype(jnp.bfloat16), "ctx").astype(jnp.float32),
            lax.psum(shard_part[6].astype(jnp.bfloat16), "ctx").astype(jnp.float32),
            lax.psum(shard_part[7].astype(jnp.bfloat16), "ctx").astype(jnp.float32),
            lax.psum(shard_part[8].astype(jnp.bfloat16), "ctx").astype(jnp.float32),
            lax.psum(shard_part[9].astype(jnp.bfloat16), "ctx").astype(jnp.float32),
            lax.psum(shard_part[10].astype(jnp.bfloat16), "ctx").astype(jnp.float32),
            lax.psum(shard_part[11].astype(jnp.bfloat16), "ctx").astype(jnp.float32),
            lax.psum(shard_part[12].astype(jnp.bfloat16), "ctx").astype(jnp.float32),
        )
        if summed_shards is None:
            summed_shards = shard_part
        else:
            summed_shards = tuple((old + new for old, new in zip(summed_shards, shard_part)))
    return (jnp.stack(outputs_list), jnp.stack(input_grads)) + tuple(summed_shards)


MESH = pl.DeviceIdType.MESH
F32 = jnp.float32
BF16 = jnp.bfloat16
GELU_A = math.sqrt(2.0 / math.pi)
GELU_B = 0.044715
LN1_S, LN1_B, B_Q, B_V, B_P, LN2_S, LN2_B, B_D, B_U, B_U1 = range(10)


def dot_nn(left, right):
    return lax.dot_general(left, right, (((1,), (0,)), ((), ())), preferred_element_type=F32)


def dot_nt(left, right):
    return lax.dot_general(left, right, (((1,), (1,)), ((), ())), preferred_element_type=F32)


def dot_tn(left, right):
    return lax.dot_general(left, right, (((0,), (0,)), ((), ())), preferred_element_type=F32)


def mult(value, factor):
    return pl.multiple_of(value, factor)


def loop_rows(total, step, body):
    def once(turn, carry):
        body(mult(turn * step, step))
        return carry

    lax.fori_loop(0, total // step, once, 0)


def norm_parts(values):
    center = values - jnp.mean(values, -1, keepdims=True)
    spread = jnp.mean(center * center, -1, keepdims=True)
    inv = lax.rsqrt(spread + NORM_EPS)
    return center * inv, inv


def norm_back(d_out, hat, inv, scale):
    d_hat = d_out * scale
    return inv * (
        d_hat - jnp.mean(d_hat, -1, keepdims=True) - hat * jnp.mean(d_hat * hat, -1, keepdims=True)
    )


def layer_kernel(
    inp, seg, v0, v1, v2, v3, v4, v5, v6, v7, wq, wp, wu, wd, bu, cot,
    out_ref, din_ref, gd_ref, gu_ref, gp_ref, gq_ref, sg_ref,
    X, SEGS, SEGR, SEG, COT, H2, PV, VEC, WQ, WP, WU, WD, H1, Q, K, V, E, MB, ATT, LI, MIX, RES,
    ACT, SLOPE, DPRE, PDH, RDH, RDI, PO, RO, ROI, OUTB, DRES, DBR, DBX, DMS, DM, DOS, DLT, DQKV,
    GD, RGD, GDS, Z1D, ZSD, Z2D, ZFD, GU, RGU, GUS, Z1U, ZSU, Z2U, GUZ, ZFU,
    GPP, RGP, GP, Z1P, ZSP, Z2P, ZFP,
    GQ, RGQ, GQF, Z1Q, ZSQ, Z2Q, ZFQ, PD1, RD1, DIN, SGP, SGS, SGT, SGB, SGZ, GBU,
    send_sem, recv_sem, local_sem,
):
    f = lax.axis_index("fsdp")
    c = lax.axis_index("ctx")
    z = c // 2
    h = c % 2
    o = 1 - h
    fx, fy, fd = fpeers = (f + 1 - 2 * (f % 2), (f + 2) % 4, 3 - f)
    px = f % 2
    py = f // 2
    qx = 1 - px
    qy = 1 - py
    zpeers = (z + 1 - 2 * (z % 2), (z + 2) % 4, 3 - z)
    sib = (f, 2 * z + o)
    seq_dev = seg.shape[1]
    shard = inp.shape[1]
    half = 4 * shard
    rows_all = 2 * half
    wide = X.shape[1]
    hw = wide // 2
    kr = wide // 4
    pairs = hw // 128
    own_rows = pl.ds(mult(h * half, half), half)
    oth_rows = pl.ds(mult(o * half, half), half)
    my_block = pl.ds(mult(h * half + z * shard, shard), shard)
    counts = [0, 0]

    def rc_make(src, dst, dev):
        i = counts[0]
        counts[0] += 1
        return pltpu.make_async_remote_copy(
            src_ref=src, dst_ref=dst, send_sem=send_sem.at[i], recv_sem=recv_sem.at[i],
            device_id=dev, device_id_type=MESH,
        )

    sent = []

    def rc(src, dst, dev):
        copy = rc_make(src, dst, dev)
        copy.start()
        sent.append(copy)
        return copy

    def lc(src, dst):
        i = counts[1]
        counts[1] += 1
        copy = pltpu.make_async_copy(src, dst, local_sem.at[i])
        copy.start()
        return copy

    def chunk_rows(j):
        return pl.ds(mult(j * rows_all + h * half, half), half)

    def chunk_other(j):
        return pl.ds(mult(j * rows_all + o * half, half), half)

    def half_rows(j, core, i):
        return pl.ds(mult(j * rows_all + core * half + i * (half // 2), half // 2), half // 2)

    def slot(s):
        return pl.ds(mult(s * hw, hw), hw)

    def cols(start):
        return pl.ds(mult(start, 128), hw)

    def krows(j):
        return pl.ds(mult(j * kr, kr), kr)

    def hrows(j, i):
        return pl.ds(mult(j * kr + i * (kr // 2), kr // 2), kr // 2)

    def block_of(zp):
        return pl.ds(mult(zp * shard, shard), shard)

    class Gather:
        def __init__(self, own, at):
            self.at = at
            self.to_x, self.to_y = {}, {}
            for first, second in ((0, 1), (1, 0)):
                self.to_x[first] = [rc(src, dst, (fx, c)) for src, dst in own(first)]
                self.to_y[second] = [rc(src, dst, (fy, c)) for src, dst in own(second)]

        def relay(self):
            for copy in self.to_x[0]:
                copy.wait_recv()
            self.far_y = rc(self.at(fx, 0), self.at(fx, 0), (fy, c))
            for copy in self.to_y[1]:
                copy.wait_recv()
            self.far_x = rc(self.at(fy, 1), self.at(fy, 1), (fx, c))

        def near(self):
            for copy in self.to_x[1] + self.to_y[0]:
                copy.wait_recv()

        def far(self):
            self.far_y.wait_recv()
            self.far_x.wait_recv()

    class Scatter:
        def __init__(self, part, got, last):
            self.part, self.got, self.last = part, got, last

        def near(self):
            self.a0 = rc(self.part(fx, 0), self.got(0, 0), (fx, c))
            self.b0 = rc(self.part(fy, 1), self.got(0, 1), (fy, c))

        def far(self):
            self.a1 = rc(self.part(fd, 0), self.got(1, 0), (fx, c))
            self.b1 = rc(self.part(fd, 1), self.got(1, 1), (fy, c))

        def relay(self):
            self.a1.wait_recv()
            mine = self.part(fy, 0)
            mine[...] = (mine[...].astype(F32) + self.got(1, 0)[...].astype(F32)).astype(BF16)
            self.a2 = rc(mine, self.last(0), (fy, c))
            self.b1.wait_recv()
            mine = self.part(fx, 1)
            mine[...] = (mine[...].astype(F32) + self.got(1, 1)[...].astype(F32)).astype(BF16)
            self.b2 = rc(mine, self.last(1), (fx, c))

        def wait(self):
            for copy in (self.a0, self.b0, self.a2, self.b2):
                copy.wait_recv()

    class ScatterX:
        def __init__(self, part, got, last):
            self.part, self.got, self.last = part, got, last

        def near(self):
            self.a0 = rc(self.part(fx), self.got(0), (fx, c))

        def far(self):
            self.a1 = rc(self.part(fd), self.got(1), (fx, c))

        def relay(self):
            self.a1.wait_recv()
            mine = self.part(fy)
            mine[...] = (mine[...].astype(F32) + self.got(1)[...].astype(F32)).astype(BF16)
            self.a2 = rc(mine, self.last, (fy, c))

        def wait(self):
            self.a0.wait_recv()
            self.a2.wait_recv()

    inner = (z + 1) // 2 == 1
    outer = jnp.logical_not(inner)
    toward = (f, 2 * zpeers[0] + h)
    across = (f, 2 * zpeers[2] + h)

    class Chain:
        def __init__(self, own, z1, zs, z2, zf):
            self.own, self.z1, self.zs, self.z2, self.zf = own, z1, zs, z2, zf
            self.c1 = rc_make(own, z1, toward)
            self.c2 = rc_make(zs, z2, across)
            self.c3 = rc_make(zf, zf, toward)

        def first(self):
            @pl.when(outer)
            def _():
                self.c1.start()

        def second(self):
            @pl.when(inner)
            def _():
                self.c1.wait_recv()
                self.zs[...] = (self.own[...].astype(F32) + self.z1[...].astype(F32)).astype(BF16)
                self.c2.start()

        def third(self):
            @pl.when(inner)
            def _():
                self.c2.wait_recv()
                self.zf[...] = (self.zs[...].astype(F32) + self.z2[...].astype(F32)).astype(BF16)
                self.c3.start()

        def fourth(self):
            @pl.when(outer)
            def _():
                self.c3.wait_recv()
                self.c1.wait_send()

            @pl.when(inner)
            def _():
                self.c2.wait_send()
                self.c3.wait_send()

            return self.zf

    barrier = pltpu.get_barrier_semaphore()
    everyone = [(fp, c) for fp in fpeers] + [(f, 2 * zp + h) for zp in zpeers] + [sib]
    for dev in everyone:
        pl.semaphore_signal(barrier, inc=1, device_id=dev, device_id_type=MESH)
    stacked = jnp.concatenate(
        [v[...].astype(F32).reshape(1, kr) for v in (v0, v1, v2, v3, v4, v5, v6, v7)], axis=0
    )
    up_own = bu[...].astype(F32).reshape(1, wide)
    up_rows = [up_own[:, i * kr : (i + 1) * kr] for i in range(4)]
    PV[f] = jnp.concatenate([stacked] + up_rows + [jnp.zeros((4, kr), F32)], axis=0)
    for s in range(4):
        row = seg[s // seq_dev, s % seq_dev : s % seq_dev + 1, :].astype(F32)
        row = jnp.concatenate([row, jnp.zeros((1, 128 - shard), F32)], axis=1)
        SEGS[s] = jnp.broadcast_to(row, (8, 128))

    SGP[...] = jnp.zeros_like(SGP)
    GBU[...] = jnp.zeros_like(GBU)
    x_own = lc(inp.at[z], X.at[my_block])
    wq_own = [lc(wq.at[:, cols(b * wide + h * hw)], WQ.at[b, krows(f)]) for b in range(3)]
    wp_own = lc(wp.at[:, cols(h * hw)], WP.at[h, krows(f)])
    pl.semaphore_wait(barrier, len(everyone))

    def wq_own_part(i):
        return [
            (wq.at[hrows(0, i), cols(b * wide + h * hw)], WQ.at[b, hrows(f, i)]) for b in range(3)
        ]

    pv_in = [rc(PV.at[f], PV.at[f], (fp, c)) for fp in fpeers]
    wq_all = Gather(wq_own_part, lambda j, i: WQ.at[:, hrows(j, i), :])
    my_slot = 4 * h + z
    s_in = [rc(SEGS.at[zp], SEGR.at[my_slot], (f, 2 * zp + h)) for zp in zpeers]
    x_in = [rc(inp.at[zp], X.at[my_block], (f, 2 * zp + h)) for zp in zpeers]
    c_in = [rc(cot.at[zp], COT.at[my_block], (f, 2 * zp + h)) for zp in zpeers]
    c_own = lc(cot.at[z], COT.at[my_block])
    wd_own = lc(wd.at[slot(h)], WD.at[slot(py)])

    def wu_strips(x_to):
        return [
            (wu.at[:, cols((2 * s + x_to) * wide + h * hw)], WU.at[krows(f), pl.ds(s * hw, hw)])
            for s in range(2)
        ]

    wu_own = [lc(src, dst) for src, dst in wu_strips(px)]
    SEGR[my_slot] = SEGS[z]
    wq_all.relay()
    wp_all = Gather(
        lambda i: [(wp.at[hrows(0, i), cols(h * hw)], WP.at[h, hrows(f, i)])],
        lambda j, i: WP.at[h, hrows(j, i)],
    )
    zq = z % 2
    pair_z = (f, 2 * zpeers[0] + h)
    wu_x = [
        rc(
            wu.at[hrows(0, zq), cols((2 * s + qx) * wide + h * hw)],
            WU.at[hrows(f, zq), pl.ds(s * hw, hw)],
            (fx, c),
        )
        for s in range(2)
    ]
    wu_y = [rc(src, dst, (fy, c)) for src, dst in wu_strips(px)]

    for copy in pv_in:
        copy.wait_recv()
    VEC[...] = jnp.concatenate([PV[j] for j in range(4)], axis=1)
    up_parts = []
    for s in range(2):
        shard_vec = PV[2 * s + px]
        for i in range(2):
            up_parts.append(jnp.where(h == 0, shard_vec[8 + i : 9 + i], shard_vec[10 + i : 11 + i]))
    bias_up = jnp.concatenate(up_parts, axis=1)

    def vector(i):
        return VEC[i : i + 1, :]

    x_own.wait()
    for copy in s_in + x_in:
        copy.wait_recv()
    my_slots = pl.ds(4 * h, 4)
    s_sib = rc(SEGR.at[my_slots], SEGR.at[my_slots], sib)
    x_sib = rc(X.at[own_rows], X.at[own_rows], sib)

    def ln1(start):
        def block(r):
            rows = pl.ds(mult(start + r, 64), 64)
            hat, _ = norm_parts(X[rows, :].astype(F32))
            H1[rows, :] = (hat * vector(LN1_S) + vector(LN1_B)).astype(BF16)

        loop_rows(half, 64, block)

    ln1(h * half)
    s_sib.wait_recv()
    for b in range(8):
        turned = jnp.transpose(jnp.broadcast_to(SEGR[b][0:1, :], (128, 128)))
        SEG[pl.ds(b * shard, shard), :] = turned[:shard, :]
    seg_row = jnp.transpose(SEG[...])[0:1, :]

    def mask(r):
        rows = pl.ds(r, 128)
        seg_col = SEG[rows, 0:1]
        place_q = r + lax.broadcasted_iota(jnp.int32, (128, rows_all), 0)
        place_k = lax.broadcasted_iota(jnp.int32, (128, rows_all), 1)
        allowed = (seg_col == seg_row) & ((seg_row >= 0.0) | (place_q == place_k))
        MB[rows, :] = jnp.where(allowed, 0.0, MASKED)

    x_sib.wait_recv()
    ln1(o * half)
    loop_rows(rows_all, 128, mask)

    for copy in wq_own:
        copy.wait()
    wp_own.wait()
    wq_all.near()
    wq_all.far()
    wp_all.relay()
    bias_half = [
        jnp.where(h == 0, vector(i)[:, :hw], vector(i)[:, hw:]) for i in (B_Q, B_V)
    ]
    for b, target in ((0, Q), (1, K), (2, V)):
        prod = dot_nn(H1[...], WQ[b])
        if b == 0:
            prod = (prod + bias_half[0]).astype(BF16) * SCORE_SCALE
        if b == 2:
            prod = prod + bias_half[1]
        prod = prod.astype(BF16)
        for p in range(pairs):
            target[p] = prod[:, p * 128 : (p + 1) * 128]
    c_own.wait()
    for copy in c_in:
        copy.wait_recv()
    c_sib = rc(COT.at[own_rows], COT.at[own_rows], sib)
    cot_in = rc(COT.at[own_rows], COT.at[chunk_rows(1)], (fx, c))

    low_half = lax.broadcasted_iota(jnp.int32, (1, 128), 1) < 64

    def pick(s, values):
        keep = low_half if s == 0 else jnp.logical_not(low_half)
        return jnp.where(keep, values, jnp.zeros_like(values))

    mix_out = []
    for p in range(pairs):

        def attend(r, p=p):
            rows = pl.ds(r, 128)
            total = None
            for s in range(2):
                scores = dot_nt(pick(s, Q[p, rows, :]), K[p]) + MB[rows, :]
                top = jnp.max(scores, -1, keepdims=True)
                expo = jnp.exp(scores - top)
                inv = 1.0 / jnp.sum(expo, -1, keepdims=True)
                low = expo.astype(BF16)
                E[2 * p + s, rows, :] = low
                LI[2 * p + s, rows, :] = inv
                part = dot_nn(low, pick(s, V[p])) * inv
                total = part if total is None else total + part
            ATT[p, rows, :] = total
            MIX[pairs * h + p, rows, :] = total.astype(BF16)

        loop_rows(rows_all, 128, attend)
        mix_out.append(rc(MIX.at[pairs * h + p], MIX.at[pairs * h + p], sib))

    for copy in wu_x:
        copy.wait_recv()
    wu_far = rc(WU.at[hrows(fx, zq)], WU.at[hrows(fx, zq)], (fy, c))
    wu_pair = [rc(WU.at[hrows(fx, zq)], WU.at[hrows(fx, zq)], pair_z)]
    wd_in = rc(wd.at[slot(h)], WD.at[slot(py)], (fy, c))

    wp_all.near()
    wp_all.far()
    wp_sib = rc(WP.at[h], WP.at[h], sib)
    for copy in mix_out:
        copy.wait_recv()
    wp_sib.wait_recv()

    def project(r):
        rows = pl.ds(mult(h * half + r, 64), 64)
        mixed = jnp.concatenate([MIX[g, rows, :] for g in range(2 * pairs)], axis=1)
        branch = jnp.concatenate([dot_nn(mixed, WP[k]) for k in range(2)], axis=1)
        resid = X[rows, :].astype(F32) + branch + vector(B_P)
        RES[pl.ds(r, 64), :] = resid
        hat, _ = norm_parts(resid)
        H2[rows, :] = (
            hat * vector(LN2_S) + vector(LN2_B)
        ).astype(BF16)

    loop_rows(half, 64, project)
    h2_in = [
        rc(H2.at[half_rows(0, h, i)], H2.at[half_rows(1, h, i)], (fx, c)) for i in range(2)
    ]
    h2_sib = rc(H2.at[own_rows], H2.at[own_rows], sib)
    wu_far.wait_recv()
    wu_pair.append(rc(WU.at[hrows(fd, zq)], WU.at[hrows(fd, zq)], pair_z))

    def up(start, count):
        def block(r):
            rows = pl.ds(mult(start + r, 128), 128)
            pre = dot_nn(H2[rows, :], WU[...]) + bias_up
            square = pre * pre
            tan = jnp.tanh(GELU_A * pre * (1.0 + GELU_B * square))
            ACT[rows, :] = (0.5 * pre * (1.0 + tan)).astype(BF16)
            SLOPE[rows, :] = 0.5 * (1.0 + tan) + (0.5 * GELU_A) * pre * (1.0 - tan * tan) * (
                1.0 + (3.0 * GELU_B) * square
            )

        loop_rows(count, 128, block)

    def back(start, count):
        def block(r):
            rows = pl.ds(mult(start + r, 128), 128)
            d_pre = (dot_nt(COT[rows, :], WD[...]) * SLOPE[rows, :]).astype(BF16)
            DPRE[rows, :] = d_pre
            GBU[...] += jnp.sum(d_pre.astype(F32), 0, keepdims=True)
            PDH[rows, :] = dot_nt(d_pre, WU[...]).astype(BF16)

        loop_rows(count, 128, block)

    def start_of(j, core, i):
        return j * rows_all + core * half + i * (half // 2)

    class Owned:
        def __init__(self, mine, got, total, copy, z1, zs, z2, zf):
            self.mine, self.got, self.copy, self.total = mine, got, copy, total
            self.chain = Chain(total, z1, zs, z2, zf)
            self.second, self.third, self.fourth = (
                self.chain.second, self.chain.third, self.chain.fourth
            )

        def first(self):
            self.copy.wait_recv()
            self.total[...] = (self.mine[...].astype(F32) + self.got[...].astype(F32)).astype(BF16)
            self.chain.first()

    quarter = hw // 4

    def owned(part_of, got, total, z1, zs, z2, zf):
        made = []
        for i in range(4):
            part = pl.ds(i * quarter, quarter)

            def rows(s, i=i):
                return pl.ds(mult(s * hw + i * quarter, quarter), quarter)

            copy = rc(part_of.at[rows(qy)], got.at[part], (fy, c))
            made.append(
                Owned(
                    part_of.at[rows(py)], got.at[part], total.at[part], copy,
                    z1.at[part], zs.at[part], z2.at[part], zf.at[part],
                )
            )
        return made

    def down(j):
        rows = pl.ds(j * rows_all, rows_all)
        PO[rows, :] = dot_nn(ACT[rows, :], WD[...]).astype(BF16)
        return rc(PO.at[chunk_other(j)], RO.at[j], sib)

    def join(buf, got, j):
        def block(r):
            rows = pl.ds(mult(j * rows_all + h * half + r, 64), 64)
            buf[rows, :] = (buf[rows, :].astype(F32) + got[j, pl.ds(r, 64), :].astype(F32)).astype(BF16)

        loop_rows(half, 64, block)

    for copy in wu_own + [wd_own]:
        copy.wait()
    for copy in wu_y + wu_pair + [c_sib, h2_sib]:
        copy.wait_recv()
    up(0, rows_all)
    cot_in.wait_recv()
    cot_fwd = rc(COT.at[chunk_rows(1)], COT.at[chunk_rows(1)], sib)

    def arrive(i):
        h2_in[i].wait_recv()
        return rc(H2.at[half_rows(1, h, i)], H2.at[half_rows(1, h, i)], sib)

    def partial(i):
        return rc(PDH.at[half_rows(1, o, i)], RDH.at[1, pl.ds(i * (half // 2), half // 2)], sib)

    def pass_on(i, copy):
        copy.wait_recv()
        for r in range(0, half // 2, 64):
            rows = pl.ds(mult(start_of(1, h, i) + r, 64), 64)
            got = RDH[1, i * (half // 2) + r : i * (half // 2) + r + 64, :]
            PDH[rows, :] = (PDH[rows, :].astype(F32) + got.astype(F32)).astype(BF16)
        return rc(PDH.at[half_rows(1, h, i)], RDI.at[pl.ds(i * (half // 2), half // 2)], (fx, c))

    h2_fwd = [arrive(0)]
    up(start_of(1, h, 0), half // 2)
    h2_fwd[0].wait_recv()
    up(start_of(1, o, 0), half // 2)
    cot_fwd.wait_recv()
    wd_in.wait_recv()
    h2_fwd.append(arrive(1))
    back(start_of(1, o, 0), half // 2)
    far_dh = [partial(0)]
    back(start_of(1, h, 0), half // 2)
    h2_fwd[1].wait_recv()
    up(start_of(1, o, 1), half // 2)
    dh_in = [pass_on(0, far_dh[0])]
    up(start_of(1, h, 1), half // 2)
    GD[slot(qy), :] = dot_tn(ACT[:, slot(qy)], COT[...]).astype(BF16)
    chain_d = owned(GD, RGD, GDS, Z1D, ZSD, Z2D, ZFD.at[h])
    back(start_of(1, o, 1), half // 2)
    far_dh.append(partial(1))
    back(start_of(1, h, 1), half // 2)
    dh_in.append(pass_on(1, far_dh[1]))

    GD[slot(py), :] = dot_tn(ACT[:, slot(py)], COT[...]).astype(BF16)
    chain_d[0].first()
    far_o = down(1)
    back(0, rows_all)
    own_dh = rc(PDH.at[oth_rows], RDH.at[0], sib)
    chain_d[1].first()
    far_o.wait_recv()
    join(PO, RO, 1)
    o_in = rc(PO.at[chunk_rows(1)], ROI, (fx, c))
    GU[slot(qy), :] = dot_tn(H2[:, slot(qy)], DPRE[...]).astype(BF16)
    chain_u = owned(GU, RGU, GUS, Z1U, ZSU, Z2U, GUZ)
    chain_z = chain_d + chain_u
    for s in range(2):
        SGP[B_U + s : B_U + s + 1, cols(h * hw)] = GBU[:, s * hw : (s + 1) * hw]
    chain_z[0].second()
    own_dh.wait_recv()


    def ln2_back(r):
        rows = pl.ds(mult(r, 64), 64)
        mine = pl.ds(mult(h * half + r, 64), 64)
        d_h2 = PDH[mine, :].astype(F32) + RDH[0, rows, :].astype(F32) + RDI[rows, :].astype(F32)
        hat, inv = norm_parts(RES[rows, :])
        SGP[LN2_S : LN2_S + 1, :] += jnp.sum(d_h2 * hat, 0, keepdims=True)
        SGP[LN2_B : LN2_B + 1, :] += jnp.sum(d_h2, 0, keepdims=True)
        cot_rows = COT[mine, :].astype(F32)
        SGP[B_D : B_D + 1, :] += jnp.sum(cot_rows, 0, keepdims=True)
        d_resid = cot_rows + norm_back(d_h2, hat, inv, vector(LN2_S))
        DRES[rows, :] = d_resid
        low = d_resid.astype(BF16)
        SGP[B_P : B_P + 1, :] += jnp.sum(low.astype(F32), 0, keepdims=True)
        for k in range(2):
            DBR[k, rows, :] = low[:, k * hw : (k + 1) * hw]
        d_mixed = dot_nt(low[:, :hw], WP[0]) + dot_nt(low[:, hw:], WP[1])
        d_mixed = d_mixed.astype(BF16)
        for g in range(2 * pairs):
            DMS[g, rows, :] = d_mixed[:, g * 128 : (g + 1) * 128]

    for i in range(2):
        dh_in[i].wait_recv()
        loop_rows(half // 2, 64, lambda r, i=i: ln2_back(i * (half // 2) + r))
    dm_sib = rc(DMS.at[pl.ds(pairs * o, pairs)], DM.at[:, own_rows, :], sib)
    dbr_sib = rc(DBR.at[o], DBX.at[own_rows], sib)
    DM[:, own_rows, :] = DMS[pl.ds(pairs * h, pairs)]
    DBX[own_rows, :] = DBR[h]
    chain_z[2].first()
    chain_z[1].second()
    GU[slot(py), :] = dot_tn(H2[:, slot(py)], DPRE[...]).astype(BF16)
    own_o = down(0)
    chain_z[3].first()
    own_o.wait_recv()
    join(PO, RO, 0)
    chain_z[0].third()
    dbr_sib.wait_recv()
    mixed_all = jnp.concatenate([MIX[g] for g in range(2 * pairs)], axis=1)
    GPP[...] = dot_tn(mixed_all, DBX[...]).astype(BF16)
    p_plane = ScatterX(lambda j: GPP.at[krows(j)], lambda w: RGP.at[w], RGP.at[2])
    p_plane.far()
    p_plane.near()
    dm_sib.wait_recv()

    def attention_back(p, steps):
        def prepare(r):
            rows = pl.ds(r, 128)
            d_out = DM[p, rows, :].astype(F32)
            for s in range(2):
                scaled = pick(s, d_out * LI[2 * p + s, rows, :]).astype(BF16)
                DOS[s, rows, :] = scaled
                DLT[s, rows, :] = jnp.sum(scaled.astype(F32) * ATT[p, rows, :], -1, keepdims=True)

        loop_rows(rows_all, 128, prepare)
        d_value = dot_tn(E[2 * p], DOS[0]) + dot_tn(E[2 * p + 1], DOS[1])
        DQKV[p, :, 256:384] = d_value.astype(BF16)
        for step in steps[0]:
            step()

        def block(r):
            rows = pl.ds(r, 128)
            d_query = None
            for s in range(2):
                d_probs = dot_nt(DOS[s, rows, :], V[p])
                d_scores = (
                    E[2 * p + s, rows, :].astype(F32) * (d_probs - DLT[s, rows, :])
                ).astype(BF16)
                E[2 * p + s, rows, :] = d_scores
                part = dot_nn(d_scores, pick(s, K[p]))
                d_query = part if d_query is None else d_query + part
            DQKV[p, rows, 0:128] = (d_query * SCORE_SCALE).astype(BF16)

        loop_rows(rows_all, 128, block)
        for step in steps[1]:
            step()
        d_key = dot_tn(E[2 * p], pick(0, Q[p])) + dot_tn(E[2 * p + 1], pick(1, Q[p]))
        DQKV[p, :, 128:256] = d_key.astype(BF16)
        GQ[p] = dot_tn(H1[...], DQKV[p]).astype(BF16)
        if p < 2:
            plane = ScatterX(
                lambda j: GQ.at[p, krows(j)], lambda w: RGQ.at[p, w], RGQ.at[p, 2]
            )
        else:
            plane = Scatter(
                lambda j, i: GQ.at[p, hrows(j, i)],
                lambda w, i: RGQ.at[p, w, hrows(0, i)],
                lambda i: RGQ.at[p, 2, hrows(0, i)],
            )
        for step in steps[2]:
            step()
        plane.far()
        plane.near()
        here = pl.ds(mult(h * hw + p * 128, 128), 128)
        for b, i in ((0, B_Q), (2, B_V)):
            SGP[i : i + 1, here] = jnp.sum(
                DQKV[p, :, b * 128 : (b + 1) * 128].astype(F32), 0, keepdims=True
            )
        return plane

    kept = {}

    def finish_out():
        o_in.wait_recv()

        def finish(r):
            rows = pl.ds(r, 64)
            mine = pl.ds(mult(h * half + r, 64), 64)
            total = PO[mine, :].astype(F32) + ROI[rows, :].astype(F32)
            OUTB[rows, :] = (RES[rows, :] + total + vector(B_D)).astype(BF16)

        loop_rows(half, 64, finish)
        kept["res_own"] = lc(OUTB.at[block_of(z)], out_ref.at[z])

    def first(i):
        return chain_z[i].first

    def second(i):
        return chain_z[i].second

    def third(i):
        return chain_z[i].third

    kept["res"] = []

    def send_out(i):
        def send():
            zp = zpeers[i]
            kept["res"].append(rc(OUTB.at[block_of(zp)], out_ref.at[z], (f, 2 * zp + h)))

        return send

    q_plane = []
    q_plane.append(
        attention_back(
            0, ([second(2), first(4)], [third(1), second(3)], [first(5), third(2)])
        )
    )
    q_plane.append(
        attention_back(
            1,
            ([second(4), first(6), finish_out, send_out(1)], [third(3), send_out(2)], [second(5), send_out(0)]),
        )
    )
    q_plane.append(
        attention_back(
            2,
            ([first(7), second(6), p_plane.relay], [third(4)], [third(5), q_plane[0].relay]),
        )
    )

    def joined(b):
        return jnp.concatenate([DQKV[p, :, b * 128 : (b + 1) * 128] for p in range(pairs)], axis=1)

    PD1[...] = (
        dot_nt(joined(0), WQ[0]) + dot_nt(joined(1), WQ[1]) + dot_nt(joined(2), WQ[2])
    ).astype(BF16)
    d1_sib = rc(PD1.at[oth_rows], RD1, sib)
    links = []

    def start_chain(mine, z1, zs, z2, zf, pieces):
        rows = kr // pieces
        made = []
        for i in range(pieces):
            part = pl.ds(i * rows, rows)
            made.append(Chain(mine.at[part], z1.at[part], zs.at[part], z2.at[part], zf.at[part]))
            made[i].first()
        links.append((made, zf))

    def own_p():
        p_plane.wait()
        GP[...] = (
            GPP[krows(f), :].astype(F32) + RGP[0].astype(F32) + RGP[2].astype(F32)
        ).astype(BF16)
        start_chain(GP, Z1P, ZSP, Z2P, ZFP.at[h], 1)

    def own_q(b, pieces):
        q_plane[b].wait()
        GQF[b] = (
            GQ[b, krows(f), :].astype(F32) + RGQ[b, 0].astype(F32) + RGQ[b, 2].astype(F32)
        ).astype(BF16)
        start_chain(GQF.at[b], Z1Q.at[b], ZSQ.at[b], Z2Q.at[b], ZFQ.at[h, b], pieces)

    def step_two(i):
        for chain in links[i][0]:
            chain.second()

    def step_three(i):
        for chain in links[i][0]:
            chain.third()

    def step_four(i):
        for chain in links[i][0]:
            chain.fourth()
        return rc(links[i][1], links[i][1], sib)

    second(7)()
    own_p()
    d1_sib.wait_recv()

    def ln1_back(r):
        rows = pl.ds(r, 64)
        mine = pl.ds(mult(h * half + r, 64), 64)
        d_h1 = PD1[mine, :].astype(F32) + RD1[rows, :].astype(F32)
        hat, inv = norm_parts(X[mine, :].astype(F32))
        SGP[LN1_S : LN1_S + 1, :] += jnp.sum(d_h1 * hat, 0, keepdims=True)
        SGP[LN1_B : LN1_B + 1, :] += jnp.sum(d_h1, 0, keepdims=True)
        DIN[rows, :] = (DRES[rows, :] + norm_back(d_h1, hat, inv, vector(LN1_S))).astype(BF16)

    loop_rows(half, 64, ln1_back)
    din_in = [rc(DIN.at[block_of(zp)], din_ref.at[z], (f, 2 * zp + h)) for zp in zpeers]
    din_own = lc(DIN.at[block_of(z)], din_ref.at[z])
    sg_sib = rc(SGP, SGS, sib)
    third(6)()
    q_plane[1].relay()
    own_q(0, 1)
    step_two(0)
    sg_sib.wait_recv()
    small = SGP[...] + SGS[...]
    for j in range(4):
        units = small[B_U + j // 2 : B_U + j // 2 + 1]
        units = jnp.where(px == j % 2, units, jnp.zeros_like(units))
        SGT[j] = jnp.concatenate(
            [small[:8, j * kr : (j + 1) * kr]]
            + [units[:, i * kr : (i + 1) * kr] for i in range(4)]
            + [jnp.zeros((4, kr), F32)],
            axis=0,
        )
    SGB[f] = SGT[f]
    sgf_in = [rc(SGT.at[fp], SGB.at[f], (fp, c)) for fp in fpeers]
    q_plane[2].relay()
    third(7)()
    own_q(1, 1)
    step_two(1)
    step_three(0)
    for chain in chain_d:
        chain.fourth()
    d_sib = rc(ZFD.at[h], ZFD.at[h], sib)
    for copy in sgf_in:
        copy.wait_recv()
    SGZ[z] = SGB[0] + SGB[1] + SGB[2] + SGB[3]
    sgz_in = [rc(SGZ.at[z], SGZ.at[z], (f, 2 * zp + h)) for zp in zpeers]
    for chain in chain_u:
        chain.fourth()
    gu_out = rc(GUZ.at[krows(qx)], ZFU.at[h, px], (fx, c))
    ZFU[h, px] = GUZ[krows(px), :]
    own_q(2, 2)
    step_two(2)
    step_three(1)
    p_sib = step_four(0)
    d_sib.wait_recv()
    outs = [lc(ZFD.at[k], gd_ref.at[pl.ds(k * hw, hw)]) for k in range(2)]
    step_two(3)
    step_three(2)
    q_sib = [step_four(1)]
    for copy in sgz_in:
        copy.wait_recv()
    sg_ref[...] = SGZ[0] + SGZ[1] + SGZ[2] + SGZ[3]
    p_sib.wait_recv()
    outs += [lc(ZFP.at[k], gp_ref.at[:, pl.ds(k * hw, hw)]) for k in range(2)]
    gu_out.wait_recv()
    u_sib = rc(ZFU.at[h], ZFU.at[h], sib)
    step_three(3)
    q_sib.append(step_four(2))
    u_sib.wait_recv()
    outs += [
        lc(
            ZFU.at[k, x_of, :, pl.ds(s * hw, hw)],
            gu_ref.at[:, pl.ds((2 * s + x_of) * wide + k * hw, hw)],
        )
        for k in range(2)
        for s in range(2)
        for x_of in range(2)
    ]
    q_sib.append(step_four(3))
    for p in range(3):
        q_sib[p].wait_recv()
        outs += [
            lc(
                ZFQ.at[k, p, :, pl.ds(b * 128, 128)],
                gq_ref.at[:, pl.ds(b * wide + k * hw + p * 128, 128)],
            )
            for k in range(2)
            for b in range(3)
        ]
    for copy in kept["res"] + din_in:
        copy.wait_recv()
    for copy in outs + [kept["res_own"], din_own]:
        copy.wait()
    for copy in sent:
        copy.wait_send()


def widen_kernel(
    out_in, din_in, gd_in, gu_in, gp_in, gq_in, sg_hbm,
    out_ref, din_ref, s0, s1, gq_ref, s2, s3, gp_ref, s4, s5, s6, gu_ref, b_up_ref, gd_ref, s7,
    sg_in, LT, LD, LU, LP, LQ, FD, FU, FP, FQ, sems,
):
    counts = [0]

    def lc(src, dst):
        copy = pltpu.make_async_copy(src, dst, sems.at[counts[0]])
        counts[0] += 1
        copy.start()
        return copy

    def halves(ref):
        rows = ref.shape[0] // 4
        return [pl.ds(i * rows, rows) for i in range(4)]

    small = lc(sg_hbm, sg_in)
    work = []
    for src, low, wide, dst in (
        (gd_in, LD, FD, gd_ref), (gu_in, LU, FU, gu_ref), (gq_in, LQ, FQ, gq_ref), (gp_in, LP, FP, gp_ref)
    ):
        for part in halves(src):
            work.append((lc(src.at[part], low.at[part]), low.at[part], wide.at[part], dst.at[part]))
    tokens = [lc(out_in, LT.at[0]), lc(din_in, LT.at[1])]
    passed = []
    kr = s0.shape[0]
    small.wait()
    for i, ref in enumerate((s0, s1, s2, s3, s4, s5, s6, s7)):
        ref[...] = sg_in[i : i + 1, :].reshape(kr)
    b_up_ref[...] = jnp.concatenate([sg_in[i : i + 1, :] for i in range(8, 12)], axis=1).reshape(4 * kr)
    for copy, src, dst in zip(tokens, (LT.at[0], LT.at[1]), (out_ref, din_ref)):
        copy.wait()
        passed.append(lc(src, dst))
    for copy, low, wide, dst in work:
        copy.wait()
        wide[...] = low[...].astype(F32)
        passed.append(lc(wide, dst))
    for copy in passed:
        copy.wait()


def fast_device(
    inputs, segments, ln1_scale, ln1_bias, w_qkv, b_query, b_value, w_proj, b_proj,
    ln2_scale, ln2_bias, w_up, b_up, w_down, b_down, cotangent,
):
    micro_count, seq_dev, shard, wide = inputs.shape
    seqs = micro_count * seq_dev
    rows_all = 8 * shard
    half = rows_all // 2
    hw = wide // 2
    kr = wide // 4
    pairs = hw // 128
    heads = 2 * pairs

    def vm(*shape, dtype=BF16):
        return pltpu.VMEM(shape, dtype)

    f32 = functools.partial(vm, dtype=F32)
    pair_rows = 2 * rows_all
    scratch = [
        vm(rows_all, wide), f32(4, 8, 128), f32(8, 8, 128), f32(rows_all, 128),
        vm(pair_rows, wide), vm(pair_rows, wide), f32(4, 16, kr), f32(16, wide),
        vm(3, wide, hw), vm(2, wide, hw), vm(wide, wide), vm(wide, wide),
        vm(rows_all, wide), vm(pairs, rows_all, 128), vm(pairs, rows_all, 128),
        vm(pairs, rows_all, 128), vm(heads, rows_all, rows_all), f32(rows_all, rows_all),
        f32(pairs, rows_all, 128), f32(heads, rows_all, 1), vm(2 * pairs, rows_all, 128),
        f32(half, wide),
        vm(pair_rows, wide), f32(pair_rows, wide), vm(pair_rows, wide),
        vm(pair_rows, wide), vm(2, half, wide), vm(half, wide),
        vm(pair_rows, wide), vm(2, half, wide), vm(half, wide), vm(half, wide),
        f32(half, wide), vm(2, half, hw), vm(rows_all, hw), vm(2 * pairs, half, 128),
        vm(pairs, rows_all, 128), vm(2, rows_all, 128), f32(2, rows_all, 1),
        vm(pairs, rows_all, hw),
        vm(wide, wide), vm(hw, wide), vm(hw, wide), vm(hw, wide), vm(hw, wide), vm(hw, wide),
        vm(2, hw, wide),
        vm(wide, wide), vm(hw, wide), vm(hw, wide), vm(hw, wide), vm(hw, wide), vm(hw, wide),
        vm(hw, wide), vm(2, 2, kr, wide),
        vm(wide, hw), vm(3, kr, hw), vm(kr, hw), vm(kr, hw), vm(kr, hw), vm(kr, hw), vm(2, kr, hw),
        vm(pairs, wide, hw), vm(pairs, 3, kr, hw), vm(pairs, kr, hw), vm(pairs, kr, hw),
        vm(pairs, kr, hw), vm(pairs, kr, hw), vm(2, pairs, kr, hw),
        vm(rows_all, wide), vm(half, wide), vm(half, wide),
        f32(16, wide), f32(16, wide), f32(4, 16, kr), f32(4, 16, kr), f32(4, 16, kr), f32(1, wide),
        pltpu.SemaphoreType.DMA((216,)), pltpu.SemaphoreType.DMA((216,)),
        pltpu.SemaphoreType.DMA((64,)),
    ]
    hbm = pl.BlockSpec(memory_space=pl.ANY)
    vmem = pl.BlockSpec(memory_space=pltpu.VMEM)
    tokens = jax.ShapeDtypeStruct((seqs, shard, wide), BF16)
    small = jax.ShapeDtypeStruct((16, kr), F32)
    grads = (w_down, w_up, w_proj, w_qkv)
    results = pl.pallas_call(
        layer_kernel,
        out_shape=(tokens, tokens) + tuple(jax.ShapeDtypeStruct(w.shape, BF16) for w in grads) + (small,),
        in_specs=[hbm] + [vmem] * 9 + [hbm] * 4 + [vmem, hbm],
        out_specs=(hbm,) * 6 + (vmem,),
        scratch_shapes=scratch,
        compiler_params=pltpu.CompilerParams(
            collective_id=0, has_side_effects=True, vmem_limit_bytes=62 << 20
        ),
    )(
        inputs.reshape(tokens.shape), segments, ln1_scale, ln1_bias, b_query, b_value, b_proj,
        ln2_scale, ln2_bias, b_down, w_qkv, w_proj, w_up, w_down, b_up, cotangent.reshape(tokens.shape),
    )
    part = jax.ShapeDtypeStruct((kr,), F32)

    def full(w):
        return jax.ShapeDtypeStruct(w.shape, F32)

    out, d_input, *rest = pl.pallas_call(
        widen_kernel,
        out_shape=(
            tokens, tokens, part, part, full(w_qkv), part, part, full(w_proj), part, part, part,
            full(w_up), jax.ShapeDtypeStruct((wide,), F32), full(w_down), part,
        ),
        in_specs=[pl.BlockSpec(memory_space=pltpu.HBM)] * 7,
        out_specs=(hbm, hbm, vmem, vmem, hbm, vmem, vmem, hbm, vmem, vmem, vmem, hbm, vmem, hbm, vmem),
        scratch_shapes=[pltpu.VMEM(small.shape, F32), pltpu.VMEM((2,) + tokens.shape, BF16)]
        + [pltpu.VMEM(w.shape, BF16) for w in grads]
        + [pltpu.VMEM(w.shape, F32) for w in grads]
        + [pltpu.SemaphoreType.DMA((48,))],
        compiler_params=pltpu.CompilerParams(vmem_limit_bytes=62 << 20),
    )(*results)
    return (out.reshape(inputs.shape), d_input.reshape(inputs.shape), *rest)


def fits_fast(mesh, inputs, w_up):
    micro_count, seqs, length, wide = inputs.shape
    return (
        mesh.shape["fsdp"] == 4
        and mesh.shape["ctx"] == 8
        and micro_count * (seqs // 4) == 4
        and length == 512
        and wide == 768
        and w_up.shape == (wide, 4 * wide)
        and HEADS * 64 == wide
    )


def solution(mesh):
    placed = (
        P(None, "fsdp", "ctx", None),
        P(None, "fsdp", "ctx"),
        P("fsdp"),
        P("fsdp"),
        P("fsdp", None),
        P("fsdp"),
        P("fsdp"),
        P("fsdp", None),
        P("fsdp"),
        P("fsdp"),
        P("fsdp"),
        P("fsdp", None),
        P("fsdp"),
        P("fsdp", None),
        P("fsdp"),
        P(None, "fsdp", "ctx", None),
    )
    spread = functools.partial(
        jax.shard_map,
        mesh=mesh,
        in_specs=placed,
        out_specs=(
            P(None, "fsdp", "ctx", None),
            P(None, "fsdp", "ctx", None),
            P("fsdp"),
            P("fsdp"),
            P("fsdp", None),
            P("fsdp"),
            P("fsdp"),
            P("fsdp", None),
            P("fsdp"),
            P("fsdp"),
            P("fsdp"),
            P("fsdp", None),
            P("fsdp"),
            P("fsdp", None),
            P("fsdp"),
        ),
        check_vma=False,
    )

    def layer(*args):
        chosen = fast_device if fits_fast(mesh, args[0], args[11]) else per_device
        return spread(chosen)(*args)

    return layer
```
